32 devices in a mesh: pol: 4 (over y, x), slab: 8 (over z, core).
Axes of the slice: x: 2, y: 2, z: 4, core: 2. Of those that a mesh axis runs over, the one named last changes fastest.
Arguments:
- correlations: bfloat16 [2, 4, 512, 256], P(None, 'pol', 'slab'), may hold values from -6 to 6
- tracks: float32 [3, 512, 256], P(None, 'slab'), may hold values from -1 to 1
- vis_counts: int32 [512], P('slab'), may hold values from 1 to 256
- offsets: int32 [2, 512], replicated, may hold values from 0 to 4064, as said below
- held_counts: int32 [8], replicated, may hold values from 1 to 64, as said below
- pixel_weight: float32 [32, 32], replicated, may hold values from 0.25 to 1
Outputs:
- sky_image: float32 [2, 4, 4096, 4096], P(None, 'pol', 'slab')
The draws below stay inside these ranges and needn't reach their ends.
Inputs may be any that keep to these rules, and one draw needn't show every extreme that they name: A holder's live slots are its first held_counts ones; one holder holds 64. offsets[0, b] // 512 == b // 64: a subgrid starts in the row slab of its holder.
All inputs are finite; a program needn't handle non-finite values.
Results may differ from the reference program's by a relative error of at most 0.0039.
Values may be sent and summed in bfloat16 or wider, within the bound.
No kernel may reach another device: no remote copies, remote signals or barrier semaphores. Data moves between devices by JAX's collectives and lax.ppermute only.
A program may use at most 128 MiB of HBM per device.

```python
import math
import jax
import jax.numpy as jnp
import numpy as np
from jax import lax

G = 4096
SUB = 32
VIS = 256
SLOTS = 64
ROWS = 512
NB = 512
N_SLAB = 8


def draw_held_counts(key, part):
    key_left, key_right, key_peak = jax.random.split(key, 3)
    left_draw = jax.random.randint(key_left, (N_SLAB,), 0, SLOTS)
    right_draw = jax.random.randint(key_right, (N_SLAB,), 0, SLOTS)
    holder_loads = 1 + left_draw * right_draw // (SLOTS - 1)
    peak_holder = jax.random.randint(key_peak, (), 0, N_SLAB)
    partner = (peak_holder + N_SLAB // 2) % N_SLAB
    holder_loads = holder_loads.at[peak_holder].set(SLOTS).at[partner].set(1)
    return holder_loads.astype(jnp.int32)


def draw_offsets(key, part):
    key_list = jax.random.split(key, 5)
    holder = jnp.arange(NB, dtype=jnp.int32) // SLOTS
    slot_in_holder = jnp.arange(NB, dtype=jnp.int32) % SLOTS
    row_draw = jax.random.randint(key_list[0], (NB,), 0, ROWS)
    row_draw = jnp.where(slot_in_holder == 0, ROWS - SUB // 2, row_draw)
    row_offset = jnp.minimum(holder * ROWS + row_draw, G - SUB)
    first_pick = jax.random.randint(key_list[1], (), 1, SLOTS)
    row_offset = row_offset.at[first_pick].set(0)
    col_offset = jax.random.randint(key_list[2], (NB,), 0, G - SUB + 1)
    low_pick = jax.random.randint(key_list[3], (), 0, NB)
    high_pick = (low_pick + 1 + jax.random.randint(key_list[4], (), 0, NB - 1)) % NB
    col_offset = col_offset.at[low_pick].set(0).at[high_pick].set(G - SUB)
    return jnp.stack([row_offset, col_offset]).astype(jnp.int32)


def draw_vis_counts(key, part):
    key_drop, key_flag, key_full = jax.random.split(key, 3)
    dropped = jax.random.randint(key_drop, (NB,), 0, VIS)
    flagged = jax.random.randint(key_flag, (NB,), 0, 2)
    counts_drawn = VIS - dropped * flagged
    full_pick = jax.random.randint(key_full, (), 0, NB)
    return counts_drawn.at[full_pick].set(VIS).astype(jnp.int32)


def shard_levels(own_key, extent, pieces, low, high):
    def one(axis_at, blocks):
        steps = jax.random.uniform(jax.random.fold_in(jax.random.fold_in(own_key, 6), axis_at), (blocks,), jnp.float32, low / len(pieces), high / len(pieces))
        return jnp.repeat(jnp.exp(steps), extent[axis_at] // blocks).reshape((-1,) + (1,) * (len(extent) - axis_at - 1))

    loudness = one(*pieces[0])
    for cut in pieces[1:]:
        loudness = loudness * one(*cut)
    return loudness


def noise(rng, extent, spread, reach, pieces=(), kind=jnp.bfloat16):
    factor_of = shard_levels(rng, extent, pieces, -0.22, 0.18) if pieces else 1.0
    drawn = jax.random.normal(rng, extent, jnp.float32) * spread * factor_of
    return jnp.minimum(jnp.maximum(drawn, -reach), reach).astype(kind)


def setup_inputs(seed: int = 0) -> dict:
    streams_of = jax.random.split(jax.random.key(seed), 7)
    correlations = noise(streams_of[0], (2, 4, NB, VIS), 1.0, 6.0, ((1, 4), (2, 8)))
    tracks = jnp.clip(jax.random.uniform(streams_of[1], (3, NB, VIS), jnp.float32, -1.0, 1.0) * shard_levels(streams_of[1], (3, NB, VIS), ((1, 8),), -0.4, 0.0), -1.0, 1.0)
    vis_counts = draw_vis_counts(jax.random.fold_in(streams_of[6], 71), 0)
    offsets = draw_offsets(jax.random.fold_in(streams_of[6], 71), 0)
    held_counts = draw_held_counts(jax.random.fold_in(streams_of[6], 71), 0)
    pixel_weight = jnp.clip(jnp.exp(jax.random.uniform(streams_of[5], (SUB, SUB), jnp.float32, math.log(0.25), math.log(1.0))), 0.25, 1.0)
    return {"correlations": correlations, "tracks": tracks, "vis_counts": vis_counts, "offsets": offsets, "held_counts": held_counts, "pixel_weight": pixel_weight}


TWO_PI = 2.0 * math.pi
FIELD_VIEW = 0.6
DEPTH_SCALE = 40.0
TRACK_SCALE = 0.375
COEF_REAL = np.array([[0.5, 0.0, 0.0, 0.5], [0.5, 0.0, 0.0, -0.5], [0.0, 0.5, 0.5, 0.0], [0.0, 0.0, 0.0, 0.0]], np.float32)
COEF_IMAG = np.array([[0.0, 0.0, 0.0, 0.0], [0.0, 0.0, 0.0, 0.0], [0.0, 0.0, 0.0, 0.0], [0.0, -0.5, 0.5, 0.0]], np.float32)

def pixel_tables():
    cells = jnp.arange(SUB * SUB, dtype=jnp.int32)
    row_pos = (cells // SUB - SUB // 2).astype(jnp.float32) / SUB
    col_pos = (cells % SUB - SUB // 2).astype(jnp.float32) / SUB
    depth = jnp.sqrt(1.0 - (FIELD_VIEW * col_pos) ** 2 - (FIELD_VIEW * row_pos) ** 2) - 1.0
    return (col_pos, row_pos, depth)

def phasor_table(track_set, tables):
    col_pos, row_pos, depth = tables
    u_cells = track_set[0] * (TRACK_SCALE * SUB)
    v_cells = track_set[1] * (TRACK_SCALE * SUB)
    w_cells = track_set[2] * DEPTH_SCALE
    phase = TWO_PI * (u_cells[:, None] * col_pos[None, :] + v_cells[:, None] * row_pos[None, :] + w_cells[:, None] * depth[None, :])
    return jnp.concatenate([jnp.cos(phase), jnp.sin(phase)], axis=1).astype(jnp.bfloat16)

def subgrid_tables():
    positions = jnp.arange(SUB, dtype=jnp.int32) - SUB // 2
    turn_count = positions[:, None] * positions[None, :] % SUB
    angles = -TWO_PI * turn_count.astype(jnp.float32) / SUB
    return (jnp.cos(angles), jnp.sin(angles))

def complex_einsum(pattern, left_pair, right_pair):
    highest = lax.Precision.HIGHEST
    left_re, left_im = left_pair
    right_re, right_im = right_pair
    real_part = jnp.einsum(pattern, left_re, right_re, precision=highest) - jnp.einsum(pattern, left_im, right_im, precision=highest)
    imag_part = jnp.einsum(pattern, left_re, right_im, precision=highest) + jnp.einsum(pattern, left_im, right_re, precision=highest)
    return (real_part, imag_part)

def subgrid_transform(sub_re, sub_im, dft_pair):
    half_re, half_im = complex_einsum('...ij,cj->...ic', (sub_re, sub_im), dft_pair)
    return complex_einsum('ai,...ic->...ac', dft_pair, (half_re, half_im))

def reference(correlations, tracks, vis_counts, offsets, held_counts, pixel_weight):
    highest = lax.Precision.HIGHEST
    tables = pixel_tables()
    dft_pair = subgrid_tables()
    pixel_area = SUB * SUB
    coef_re = jnp.asarray(COEF_REAL, dtype=jnp.float32)
    coef_im = jnp.asarray(COEF_IMAG, dtype=jnp.float32)
    corr_float = correlations.astype(jnp.float32)
    stokes_re = jnp.einsum('kp,pnv->knv', coef_re, corr_float[0], precision=highest) - jnp.einsum('kp,pnv->knv', coef_im, corr_float[1], precision=highest)
    stokes_im = jnp.einsum('kp,pnv->knv', coef_re, corr_float[1], precision=highest) + jnp.einsum('kp,pnv->knv', coef_im, corr_float[0], precision=highest)
    visible = (jnp.arange(VIS, dtype=jnp.int32)[None, :] < vis_counts[:, None]).astype(jnp.bfloat16)
    stokes_vis = jnp.stack([stokes_re, stokes_im], axis=1).astype(jnp.bfloat16) * visible[None, None]
    live_slot = (jnp.arange(NB, dtype=jnp.int32) % SLOTS < jnp.repeat(held_counts, SLOTS)).astype(jnp.float32)
    weight_flat = pixel_weight.reshape(pixel_area)
    bundle_items = (jnp.transpose(stokes_vis, (2, 0, 1, 3)), jnp.transpose(tracks, (1, 0, 2)), jnp.transpose(offsets).astype(jnp.int32), live_slot)
    zero_index = jnp.zeros((), jnp.int32)

    def add_bundle(grid_sum, bundle_item):
        vis_block, track_set, corner_index, live_flag = bundle_item
        phasor = phasor_table(track_set, tables)
        product = jnp.dot(vis_block.reshape(8, VIS), phasor, preferred_element_type=jnp.float32).reshape(4, 2, 2 * pixel_area)
        sub_re = product[:, 0, :pixel_area] - product[:, 1, pixel_area:]
        sub_im = product[:, 0, pixel_area:] + product[:, 1, :pixel_area]
        sub_re = (sub_re * weight_flat).reshape(4, SUB, SUB)
        sub_im = (sub_im * weight_flat).reshape(4, SUB, SUB)
        uv_re, uv_im = subgrid_transform(sub_re, sub_im, dft_pair)
        uv_block = jnp.stack([uv_re, uv_im]) * live_flag
        corner = (zero_index, zero_index, corner_index[0].astype(jnp.int32), corner_index[1].astype(jnp.int32))
        current = lax.dynamic_slice(grid_sum, corner, (2, 4, SUB, SUB))
        return (lax.dynamic_update_slice(grid_sum, current + uv_block, corner), None)
    grid_sum, _ = lax.scan(add_bundle, jnp.zeros((2, 4, G, G), jnp.float32), bundle_items)
    norm_scale = 1.0 / (SUB * SUB * math.sqrt(VIS * NB / 8.0))
    real_parts = []
    imag_parts = []
    for stokes in range(4):
        uv_plane = lax.complex(grid_sum[0, stokes], grid_sum[1, stokes])
        sky_plane = jnp.fft.ifft2(uv_plane) * (G * G * norm_scale)
        real_parts.append(jnp.real(sky_plane).T)
        imag_parts.append(jnp.imag(sky_plane).T)
    return jnp.stack([jnp.stack(real_parts), jnp.stack(imag_parts)])
```

```python
import functools
import math

import jax
import jax.numpy as jnp
import numpy as np
from jax import lax
from jax.experimental import pallas as pl
from jax.experimental.pallas import tpu as pltpu
from jax.sharding import PartitionSpec as P

G = 4096
SUB = 32
VIS = 256
SLOTS = 64


TWO_PI = 2.0 * math.pi
FIELD_VIEW = 0.6
DEPTH_SCALE = 40.0
TRACK_SCALE = 0.375
COEF_REAL = np.array(
    [[0.5, 0.0, 0.0, 0.5], [0.5, 0.0, 0.0, -0.5], [0.0, 0.5, 0.5, 0.0], [0.0, 0.0, 0.0, 0.0]],
    np.float32,
)
COEF_IMAG = np.array(
    [[0.0, 0.0, 0.0, 0.0], [0.0, 0.0, 0.0, 0.0], [0.0, 0.0, 0.0, 0.0], [0.0, -0.5, 0.5, 0.0]],
    np.float32,
)


def partner_2(value, axis, distance):
    return lax.ppermute(value, axis, [(i, i ^ 1 << distance) for i in range(lax.axis_size(axis))])


def passed_along(value, axis, by):
    peers = lax.axis_size(axis)
    pairs = [(i, i + by) for i in range(peers) if 0 <= i + by < peers]
    return lax.ppermute(value, axis, pairs)


def pixel_tables():
    cells = jnp.arange(SUB * SUB, dtype=jnp.int32)
    row_pos = (cells // SUB - SUB // 2).astype(jnp.float32) / SUB
    col_pos = (cells % SUB - SUB // 2).astype(jnp.float32) / SUB
    depth = jnp.sqrt(1.0 - (FIELD_VIEW * col_pos) ** 2 - (FIELD_VIEW * row_pos) ** 2) - 1.0
    return (col_pos, row_pos, depth)


def phasor_table(track_set, tables):
    col_pos, row_pos, depth = tables
    u_cells = track_set[0] * (TRACK_SCALE * SUB)
    v_cells = track_set[1] * (TRACK_SCALE * SUB)
    w_cells = track_set[2] * DEPTH_SCALE
    phase = TWO_PI * (
        u_cells[:, None] * col_pos[None, :]
        + v_cells[:, None] * row_pos[None, :]
        + w_cells[:, None] * depth[None, :]
    )
    return jnp.concatenate([jnp.cos(phase), jnp.sin(phase)], axis=1).astype(jnp.bfloat16)


def subgrid_tables():
    positions = jnp.arange(SUB, dtype=jnp.int32) - SUB // 2
    turn_count = positions[:, None] * positions[None, :] % SUB
    angles = -TWO_PI * turn_count.astype(jnp.float32) / SUB
    return (jnp.cos(angles), jnp.sin(angles))


def dft_table(length):
    positions = jnp.arange(length, dtype=jnp.int32)
    turn_count = positions[:, None] * positions[None, :] % length
    angles = TWO_PI * turn_count.astype(jnp.float32) / length
    return (jnp.cos(angles), jnp.sin(angles))


def twiddle_table(first_len, second_len, length):
    first_pos = jnp.arange(first_len, dtype=jnp.int32)
    second_pos = jnp.arange(second_len, dtype=jnp.int32)
    turn_count = first_pos[:, None] * second_pos[None, :] % length
    angles = TWO_PI * turn_count.astype(jnp.float32) / length
    return (jnp.cos(angles), jnp.sin(angles))


def complex_einsum(pattern, left_pair, right_pair):
    highest = lax.Precision.HIGHEST
    left_re, left_im = left_pair
    right_re, right_im = right_pair
    real_part = jnp.einsum(pattern, left_re, right_re, precision=highest) - jnp.einsum(
        pattern, left_im, right_im, precision=highest
    )
    imag_part = jnp.einsum(pattern, left_re, right_im, precision=highest) + jnp.einsum(
        pattern, left_im, right_re, precision=highest
    )
    return (real_part, imag_part)


def complex_multiply(data_pair, table_pair):
    data_re, data_im = data_pair
    table_re, table_im = table_pair
    return (data_re * table_re - data_im * table_im, data_re * table_im + data_im * table_re)


def subgrid_transform(sub_re, sub_im, dft_pair):
    half_re, half_im = complex_einsum("...ij,cj->...ic", (sub_re, sub_im), dft_pair)
    return complex_einsum("ai,...ic->...ac", dft_pair, (half_re, half_im))


def place_blocks(window, blocks, row_starts, col_starts):
    block_count = blocks.shape[1]
    zero_index = jnp.zeros((), jnp.int32)

    def add_one(slot_index, current_window):
        block = lax.dynamic_index_in_dim(blocks, slot_index, 1, keepdims=False)
        corner = (zero_index, row_starts[slot_index], col_starts[slot_index])
        current = lax.dynamic_slice(current_window, corner, (2, SUB, SUB))
        return lax.dynamic_update_slice(current_window, current + block, corner)

    return lax.fori_loop(0, block_count, add_one, window)


def on_device(correlations, tracks, vis_counts, offsets, held_counts, pixel_weight):
    highest = lax.Precision.HIGHEST
    slab_count = lax.axis_size("slab")
    slab_index = lax.axis_index("slab")
    stokes_index = lax.axis_index("pol")
    pixel_area = SUB * SUB
    rows_local = G // slab_count
    tables = pixel_tables()
    dft_pair = subgrid_tables()
    gathered = lax.all_gather(correlations, "pol", axis=1, tiled=True)
    corr_float = gathered.astype(jnp.float32)
    select = (jnp.arange(4, dtype=jnp.int32) == stokes_index).astype(jnp.float32)
    coef_re = jnp.sum(select[:, None] * jnp.asarray(COEF_REAL), axis=0)
    coef_im = jnp.sum(select[:, None] * jnp.asarray(COEF_IMAG), axis=0)
    stokes_re = jnp.einsum("p,pnv->nv", coef_re, corr_float[0], precision=highest) - jnp.einsum(
        "p,pnv->nv", coef_im, corr_float[1], precision=highest
    )
    stokes_im = jnp.einsum("p,pnv->nv", coef_re, corr_float[1], precision=highest) + jnp.einsum(
        "p,pnv->nv", coef_im, corr_float[0], precision=highest
    )
    visible = (jnp.arange(VIS, dtype=jnp.int32)[None, :] < vis_counts[:, None]).astype(jnp.bfloat16)
    stokes_vis = jnp.stack([stokes_re, stokes_im]).astype(jnp.bfloat16) * visible[None]
    holder_ids = jnp.arange(slab_count, dtype=jnp.int32)
    own_held = jnp.sum(jnp.where(holder_ids == slab_index, held_counts, 0))

    def grid_range(vis_set, track_set, first_slot, stop_slot, capacity):

        def one_slot(slot_index, subgrid_set):
            phasor = phasor_table(
                lax.dynamic_index_in_dim(track_set, slot_index, 1, keepdims=False), tables
            )
            vis_slot = lax.dynamic_index_in_dim(vis_set, slot_index, 1, keepdims=False)
            product = jnp.dot(vis_slot, phasor, preferred_element_type=jnp.float32)
            sub_re = product[0, :pixel_area] - product[1, pixel_area:]
            sub_im = product[0, pixel_area:] + product[1, :pixel_area]
            update = jnp.stack([sub_re, sub_im])[:, None, :]
            return lax.dynamic_update_slice_in_dim(subgrid_set, update, slot_index, 1)

        zero_set = jnp.zeros((2, capacity, pixel_area), jnp.float32)
        return lax.fori_loop(first_slot, stop_slot, one_slot, zero_set)

    half_slots = SLOTS // 2
    swap_bit = slab_count.bit_length() - 2
    partner = jnp.bitwise_xor(slab_index, slab_count // 2)
    partner_held = jnp.sum(jnp.where(holder_ids == partner, held_counts, 0))
    pair_total = own_held + partner_held
    own_give = jnp.maximum(own_held - (pair_total + 1) // 2, 0)
    partner_give = jnp.maximum(partner_held - (pair_total + 1) // 2, 0)
    own_start = jnp.minimum(own_held - own_give, SLOTS - half_slots)
    partner_start = jnp.minimum(partner_held - partner_give, SLOTS - half_slots)
    send_vis = lax.dynamic_slice_in_dim(stokes_vis, own_start, half_slots, 1).astype(jnp.float32)
    send_track = lax.dynamic_slice_in_dim(tracks, own_start, half_slots, 1)
    got_vis, got_track = partner_2((send_vis, send_track), "slab", swap_bit)
    first_slot = partner_held - partner_give - partner_start
    helped = grid_range(
        got_vis.astype(jnp.bfloat16), got_track, first_slot, first_slot + partner_give, half_slots
    )
    returned_set = partner_2(helped, "slab", swap_bit)
    own_part = grid_range(stokes_vis, tracks, 0, own_held - own_give, SLOTS)
    subgrids = own_part + lax.dynamic_update_slice_in_dim(
        jnp.zeros_like(own_part), returned_set, own_start, 1
    )
    weight_flat = pixel_weight.reshape(pixel_area)
    sub_re = (subgrids[0] * weight_flat).reshape(SLOTS, SUB, SUB)
    sub_im = (subgrids[1] * weight_flat).reshape(SLOTS, SUB, SUB)
    uv_re, uv_im = subgrid_transform(sub_re, sub_im, dft_pair)
    uv_blocks = jnp.stack([uv_re, uv_im])
    own_offsets = lax.dynamic_slice_in_dim(offsets, slab_index * SLOTS, SLOTS, 1)
    own_rows = own_offsets[0] - slab_index * rows_local
    own_cols = own_offsets[1]
    window = jnp.zeros((2, rows_local + SUB, G), jnp.float32)
    window = place_blocks(window, uv_blocks, own_rows, own_cols)
    lower_rows = passed_along(window[:, rows_local:], "slab", 1)
    slab_grid = window[:, :rows_local].at[:, :SUB].add(lower_rows)
    small_side = G // 128
    large_side = 128
    table_small = dft_table(small_side)
    table_large = dft_table(large_side)
    twiddle = twiddle_table(small_side, large_side, G)
    plane_re = slab_grid[0].reshape(rows_local, small_side, large_side)
    plane_im = slab_grid[1].reshape(rows_local, small_side, large_side)
    step_re, step_im = complex_einsum("rkc,kx->rxc", (plane_re, plane_im), table_small)
    step_re, step_im = complex_multiply((step_re, step_im), twiddle)
    step_re, step_im = complex_einsum("rxc,cb->bxr", (step_re, step_im), table_large)
    moved_block = lax.all_to_all(
        jnp.stack([step_re, step_im]), "slab", split_axis=1, concat_axis=3, tiled=True
    )
    line_re = moved_block[0].reshape(rows_local, large_side, small_side)
    line_im = moved_block[1].reshape(rows_local, large_side, small_side)
    line_re, line_im = complex_einsum("xab,ay->xby", (line_re, line_im), table_large)
    line_re, line_im = complex_multiply((line_re, line_im), twiddle)
    line_re, line_im = complex_einsum("xby,bz->xzy", (line_re, line_im), table_small)
    norm_scale = 1.0 / (SUB * SUB * math.sqrt(VIS * SLOTS * slab_count / 8.0))
    sky_re = line_re.reshape(rows_local, G) * norm_scale
    sky_im = line_im.reshape(rows_local, G) * norm_scale
    return jnp.stack([sky_re, sky_im])[:, None]


LANES = 128
GROUP = 8


def turn_polynomials():
    z = np.cos(np.linspace(0.0, np.pi, 4001)) * 0.125 + 0.125
    r = np.sqrt(z)
    sine = np.where(r > 0, np.sin(np.pi * r) / np.where(r > 0, r, 1.0), np.pi)
    fits = []
    for values in (sine, np.cos(np.pi * r)):
        fit = np.polynomial.chebyshev.Chebyshev.fit(z, values, 5, domain=[0.0, 0.25])
        fits.append([float(v) for v in fit.convert(kind=np.polynomial.Polynomial).coef])
    return fits


SINE_COEF, COSINE_COEF = turn_polynomials()


def cos_sin_turns(turns):
    rest = turns - jnp.floor(turns + 0.5)
    square = rest * rest
    sine = SINE_COEF[-1]
    cosine = COSINE_COEF[-1]
    for coef in SINE_COEF[-2::-1]:
        sine = sine * square + coef
    for coef in COSINE_COEF[-2::-1]:
        cosine = cosine * square + coef
    sine = sine * rest
    double = sine + sine
    return 1.0 - double * sine, double * cosine


def times(left, right):
    return (left[0] * right[0] - left[1] * right[1], left[0] * right[1] + left[1] * right[0])


def plus(left, right):
    return (left[0] + right[0], left[1] + right[1])


def minus(left, right):
    return (left[0] - right[0], left[1] - right[1])


def quarter(value, sign):
    if sign > 0:
        return (-value[1], value[0])
    return (value[1], -value[0])


def dft_4(values, sign):
    a, b, c, d = values
    even_sum, even_diff = plus(a, c), minus(a, c)
    odd_sum, odd_diff = plus(b, d), quarter(minus(b, d), sign)
    return [plus(even_sum, odd_sum), plus(even_diff, odd_diff), minus(even_sum, odd_sum), minus(even_diff, odd_diff)]


ROOT_HALF = math.sqrt(0.5)


def dft_8(values, sign):
    even = dft_4(values[0::2], sign)
    odd = dft_4(values[1::2], sign)
    a, b = odd[1]
    odd[1] = ((a - b) * ROOT_HALF, (a + b) * ROOT_HALF) if sign > 0 else ((a + b) * ROOT_HALF, (b - a) * ROOT_HALF)
    odd[2] = quarter(odd[2], sign)
    a, b = odd[3]
    odd[3] = ((-a - b) * ROOT_HALF, (a - b) * ROOT_HALF) if sign > 0 else ((b - a) * ROOT_HALF, (-a - b) * ROOT_HALF)
    return [plus(e, o) for e, o in zip(even, odd)] + [minus(e, o) for e, o in zip(even, odd)]


def pixel_rows():
    row, col = np.divmod(np.arange(SUB * SUB), SUB)
    l = ((col - SUB // 2) / SUB).astype(np.float32)
    m = ((row - SUB // 2) / SUB).astype(np.float32)
    view = np.float32(FIELD_VIEW)
    n = (np.sqrt(np.float32(1.0) - (view * l) ** 2 - (view * m) ** 2) - np.float32(1.0)).astype(np.float32)
    return np.stack([l, m, n, row.astype(np.float32)] + [np.zeros_like(l)] * 4).astype(np.float32)


def row_twiddles():
    angle = -2.0 * np.pi * np.arange(8)[:, None] * (np.arange(LANES)[None, :] // SUB) / SUB
    return np.concatenate([np.cos(angle), np.sin(angle)], axis=0).astype(np.float32)


def subgrid_kernel(
    count_ref, pol_ref, source_ref, start_ref, slots_ref, table_ref, twiddle_ref, weight_ref, *refs
):
    out_refs, more_ref, held_ref = refs[:4], refs[4], refs[5]
    held_ref[...] = jnp.zeros_like(held_ref)
    pol = pol_ref[0]

    def one_slot(index, carry):
        values = slots_ref[source_ref[index]]
        row_start = start_ref[index].astype(jnp.float32)

        def corr(c, p):
            return values[4 * c + p : 4 * c + p + 1]

        stokes = [
            0.5 * corr(0, 0) + 0.5 * corr(0, 3),
            0.5 * corr(0, 0) - 0.5 * corr(0, 3),
            0.5 * corr(0, 1) + 0.5 * corr(0, 2),
            0.5 * corr(1, 1) - 0.5 * corr(1, 2),
            0.5 * corr(1, 0) + 0.5 * corr(1, 3),
            0.5 * corr(1, 0) - 0.5 * corr(1, 3),
            0.5 * corr(1, 1) + 0.5 * corr(1, 2),
            0.5 * corr(0, 2) - 0.5 * corr(0, 1),
        ]
        rows = []
        for part in (stokes[:4], stokes[4:]):
            for k in range(4):
                row = part[k]
                for other in range(1, 4):
                    row = jnp.where(pol == other, part[k ^ other], row)
                rows.append(row)
        vis = jnp.concatenate(rows, axis=0).astype(jnp.bfloat16)
        track = jnp.transpose(values[8:16])
        shape = (VIS, LANES)
        u = jnp.broadcast_to(track[:, 0:1] * (TRACK_SCALE * SUB), shape)
        v = jnp.broadcast_to(track[:, 1:2] * (TRACK_SCALE * SUB), shape)
        w = jnp.broadcast_to(track[:, 2:3] * DEPTH_SCALE, shape)
        placed = []
        for tile in range(SUB * SUB // LANES):
            lanes = pl.ds(tile * LANES, LANES)
            turns = u * table_ref[0:1, lanes] + v * table_ref[1:2, lanes] + w * table_ref[2:3, lanes]
            cosine, sine = cos_sin_turns(turns)
            phasor = jnp.concatenate([cosine.astype(jnp.bfloat16), sine.astype(jnp.bfloat16)], axis=1)
            product = jnp.dot(vis, phasor, preferred_element_type=jnp.float32)
            real = product[:4, :LANES] - product[4:, LANES:]
            imag = product[:4, LANES:] + product[4:, :LANES]
            weight = weight_ref[0:1, lanes]
            pixel_row = table_ref[3:4, lanes]
            turn = (row_start * (pixel_row - SUB // 2) + pixel_row * (SUB // 2)) * (1.0 / SUB)
            turn_re, turn_im = cos_sin_turns(turn)
            turn_re, turn_im = turn_re * weight, turn_im * weight
            placed.append(times((real, imag), (turn_re, turn_im)))
        for rho, value in enumerate(dft_8(placed, -1)):
            if rho:
                value = times(value, (twiddle_ref[rho : rho + 1], twiddle_ref[8 + rho : 9 + rho]))
            held_ref[index, :, pl.ds(2 * rho * LANES, LANES)] = value[0]
            held_ref[index, :, pl.ds((2 * rho + 1) * LANES, LANES)] = value[1]
        return carry

    lax.fori_loop(0, count_ref[0], one_slot, 0)
    for k in range(4):
        out_refs[k][...] = held_ref[:GROUP, k, :].astype(jnp.bfloat16)
        more_ref[k] = held_ref[GROUP:, k, :].astype(jnp.bfloat16)


def subgrids_of(count, pol, source, start, slots, weight_row):
    capacity = source.shape[0]
    smem = pl.BlockSpec(memory_space=pltpu.SMEM)
    vmem = pl.BlockSpec(memory_space=pltpu.VMEM)
    return pl.pallas_call(
        subgrid_kernel,
        out_shape=[jax.ShapeDtypeStruct((GROUP, 2 * SUB * SUB), jnp.bfloat16)] * 4
        + [jax.ShapeDtypeStruct((4, capacity - GROUP, 2 * SUB * SUB), jnp.bfloat16)],
        in_specs=[smem] * 4 + [vmem] * 4,
        out_specs=[vmem] * 5,
        scratch_shapes=[pltpu.VMEM((capacity, 4, 2 * SUB * SUB), jnp.float32)],
        name="subgrids",
    )(count, pol, source, start, slots, jnp.asarray(pixel_rows()), jnp.asarray(row_twiddles()), weight_row)


def image_kernel(pol_step, x_block, slabs, groups_ref, base_ref, row_ref, col_ref, mix_ref, twist_ref, *refs):
    first_refs, more_ref, sky_ref = refs[:slabs], refs[slabs], refs[slabs + 1]
    bundle_ref, phase_ref, col_phase_ref, half_ref, moved_ref, sum_ref, stage_ref, out_ref = refs[slabs + 2 : -3]
    later_ref, sem_ref, later_sem_ref = refs[-3:]
    x_blocks = sky_ref.shape[1] // x_block
    groups = groups_ref[0]
    lane_index = lax.broadcasted_iota(jnp.int32, (LANES, LANES), 1)
    eighth = SUB // 4
    out_rows = out_ref.shape[2]
    out_steps = x_block // out_rows
    group_chunks = 4 // pol_step
    depth = 2 * LANES

    def load_phases(group, part):
        chunk = group * group_chunks + part
        rows = jnp.transpose(jnp.broadcast_to(row_ref[pl.ds(chunk, 1), :].astype(jnp.float32), (LANES, LANES)))
        rows = rows.astype(jnp.int32)
        high = lax.shift_right_logical(rows, 5)
        low = jnp.bitwise_and(rows, SUB - 1)
        here = cos_sin_turns(jnp.bitwise_and(high * lane_index, LANES - 1).astype(jnp.float32) * (1.0 / LANES))
        later = cos_sin_turns(jnp.bitwise_and((high + 1) * lane_index, LANES - 1).astype(jnp.float32) * (1.0 / LANES))
        re_rows = pl.ds(part * depth, LANES)
        im_rows = pl.ds(part * depth + LANES, LANES)

        def one_phase(residue, inner):
            carried = low > residue
            re = jnp.where(carried, later[0], here[0]).astype(jnp.bfloat16)
            im = jnp.where(carried, later[1], here[1])
            phase_ref[residue, re_rows, :LANES] = re
            phase_ref[residue, re_rows, LANES:] = im.astype(jnp.bfloat16)
            phase_ref[residue, im_rows, :LANES] = (-im).astype(jnp.bfloat16)
            phase_ref[residue, im_rows, LANES:] = re
            return inner

        lax.fori_loop(0, SUB, one_phase, 0)

    def move_rows(group, part, block):
        chunk = group * group_chunks + part
        cols = col_ref[pl.ds(chunk, 1), :]
        x_index = lax.broadcasted_iota(jnp.int32, (x_block, LANES), 0) + (base_ref[0] + block * x_block)
        turns = jnp.bitwise_and(x_index * cols, G - 1).astype(jnp.float32) * (1.0 / G)
        turn_re, turn_im = cos_sin_turns(turns)
        col_phase_ref[0] = turn_re
        col_phase_ref[1] = turn_im
        for pair in range(eighth // 2):
            wide = jnp.concatenate(
                [
                    bundle_ref[part, :, pl.ds(4 * pair * LANES, depth)],
                    bundle_ref[part, :, pl.ds((4 * pair + 2) * LANES, depth)],
                ],
                axis=0,
            )
            for side in range(2):
                half_ref[pair, side] = lax.dot_general(
                    mix_ref[block, side], wide, (((1,), (1,)), ((), ())), preferred_element_type=jnp.float32
                )

        def one_tile(tile, inner):
            rows_at = pl.ds(pl.multiple_of(tile * 16, 16), 16)
            turn = (col_phase_ref[0, rows_at], col_phase_ref[1, rows_at])
            for low in range(eighth):
                at = pl.ds(low % 2 * LANES, LANES)
                for high in range(4):
                    tile_rows = pl.ds(pl.multiple_of(high * x_block + tile * 16, 16), 16)
                    value = (half_ref[low // 2, 0, tile_rows, at], half_ref[low // 2, 1, tile_rows, at])
                    re, im = times(value, turn)
                    moved_ref[low + 8 * high, rows_at, pl.ds(part * depth, LANES)] = re.astype(jnp.bfloat16)
                    moved_ref[low + 8 * high, rows_at, pl.ds(part * depth + LANES, LANES)] = im.astype(jnp.bfloat16)
            return inner

        lax.fori_loop(0, x_block // 16, one_tile, 0)

    def load_group(group):
        @pl.when(group > 0)
        def _():
            copy = pltpu.make_async_copy(more_ref, later_ref, later_sem_ref)
            copy.start()
            copy.wait()

        for part in range(group_chunks):
            polarized = pl.ds(part * pol_step, pol_step)
            span = pol_step * GROUP
            for peer in range(slabs):
                rows_at = pl.ds(peer * span, span)

                @pl.when(group == 0)
                def _(part=part, polarized=polarized, peer=peer, rows_at=rows_at):
                    bundle_ref[part, rows_at] = first_refs[peer][polarized].reshape(span, -1)

                @pl.when(group > 0)
                def _(part=part, polarized=polarized, peer=peer, rows_at=rows_at):
                    bundle_ref[part, rows_at] = later_ref[peer, polarized].reshape(span, -1)

            load_phases(group, part)

    def copy_out(block, step):
        x_at = pl.ds(pl.multiple_of(block * x_block + step * out_rows, 8), out_rows)
        return pltpu.make_async_copy(out_ref.at[step], sky_ref.at[:, x_at], sem_ref.at[step])

    def one_block(block, carry):
        def one_group(group, inner):
            @pl.when((block == 0) | (groups > 1))
            def _():
                load_group(group)

            for part in range(group_chunks):
                move_rows(group, part, block)

            @pl.when(group == 0)
            def _():
                def one_residue(residue, innermost):
                    sum_ref[residue] = jnp.dot(
                        moved_ref[residue], phase_ref[residue], preferred_element_type=jnp.float32
                    )
                    return innermost

                lax.fori_loop(0, SUB, one_residue, 0, unroll=4)

            @pl.when(group > 0)
            def _():
                def one_residue(residue, innermost):
                    sum_ref[residue] += jnp.dot(
                        moved_ref[residue], phase_ref[residue], preferred_element_type=jnp.float32
                    )
                    return innermost

                lax.fori_loop(0, SUB, one_residue, 0)

            return inner

        lax.fori_loop(0, groups, one_group, 0)

        def one_step(step, inner):
            @pl.when(block > 0)
            def _():
                copy_out(block - 1, step).wait()

            def one_tile(tile, innermost):
                rows_at = pl.ds(pl.multiple_of(step * out_rows + tile * 8, 8), 8)
                for second in range(4):
                    parts = []
                    for first in range(8):
                        residue = 4 * first + second
                        value = (sum_ref[residue, rows_at, :LANES], sum_ref[residue, rows_at, LANES:])
                        twist = (twist_ref[2 * residue : 2 * residue + 1], twist_ref[2 * residue + 1 : 2 * residue + 2])
                        parts.append(times(value, twist))
                    for first, value in enumerate(dft_8(parts, 1)):
                        if first * second:
                            angle = TWO_PI * first * second / SUB
                            value = times(value, (math.cos(angle), math.sin(angle)))
                        stage_ref[second, first, 0] = value[0]
                        stage_ref[second, first, 1] = value[1]
                to_rows = pl.ds(pl.multiple_of(tile * 8, 8), 8)
                for first in range(8):
                    parts = [(stage_ref[second, first, 0], stage_ref[second, first, 1]) for second in range(4)]
                    for second, value in enumerate(dft_4(parts, 1)):
                        lanes = pl.ds((first + 8 * second) * LANES, LANES)
                        out_ref[step, 0, to_rows, lanes] = value[0]
                        out_ref[step, 1, to_rows, lanes] = value[1]
                return innermost

            lax.fori_loop(0, out_rows // 8, one_tile, 0)
            copy_out(block, step).start()
            return inner

        lax.fori_loop(0, out_steps, one_step, 0)
        return carry

    lax.fori_loop(0, x_blocks, one_block, 0)
    for step in range(out_steps):
        copy_out(x_blocks - 1, step).wait()


def twist_table(scale):
    residue = np.arange(SUB)[:, None]
    lane = np.arange(LANES)[None, :]
    angle = 2.0 * np.pi * (residue * lane % G) / G
    sign = np.where(residue % 2 == 0, scale, -scale)
    return np.stack([sign * np.cos(angle), sign * np.sin(angle)], axis=1).reshape(2 * SUB, LANES).astype(np.float32)


def mix_table(x_base, x_count, x_block):
    highest = lax.Precision.HIGHEST
    x_index = x_base + jnp.arange(x_count, dtype=jnp.int32)
    cell = jnp.arange(SUB, dtype=jnp.int32)
    line_re, line_im = cos_sin_turns((x_index[:, None] * cell[None, :] % G).astype(jnp.float32) * (1.0 / G))
    cells, pixels = np.arange(SUB)[:, None], np.arange(LANES)[None, :] % SUB
    angle = -2.0 * np.pi * ((cells - SUB // 2) * (pixels - SUB // 2) % SUB) / SUB
    sub_re, sub_im = jnp.asarray(np.cos(angle), jnp.float32), jnp.asarray(np.sin(angle), jnp.float32)
    core_re = jnp.dot(line_re, sub_re, precision=highest) - jnp.dot(line_im, sub_im, precision=highest)
    core_im = jnp.dot(line_re, sub_im, precision=highest) + jnp.dot(line_im, sub_re, precision=highest)
    blocks = x_count // x_block
    core_re = core_re.reshape(blocks, 1, x_block, LANES)
    core_im = core_im.reshape(blocks, 1, x_block, LANES)
    turn = (np.arange(4)[:, None] * (np.arange(LANES)[None, :] // SUB)) % 4
    turn_re = jnp.asarray(np.array([1.0, 0.0, -1.0, 0.0], np.float32)[turn][None, :, None, :])
    turn_im = jnp.asarray(np.array([0.0, -1.0, 0.0, 1.0], np.float32)[turn][None, :, None, :])
    re = (core_re * turn_re - core_im * turn_im).astype(jnp.bfloat16)
    im = (core_re * turn_im + core_im * turn_re).astype(jnp.bfloat16)
    table = jnp.stack([jnp.concatenate([re, -im], axis=3), jnp.concatenate([im, re], axis=3)], axis=1)
    return table.reshape(blocks, 2, 4 * x_block, 2 * LANES)


def image_of(groups, x_base, first, more, rows, cols, mix, x_count, x_block, scale, pol_step):
    out_rows = min(x_block, 64)
    parts = 4 // pol_step
    slabs = len(first)
    smem = pl.BlockSpec(memory_space=pltpu.SMEM)
    vmem = pl.BlockSpec(memory_space=pltpu.VMEM)
    hbm = pl.BlockSpec(memory_space=pl.ANY)
    return pl.pallas_call(
        functools.partial(image_kernel, pol_step, x_block, slabs),
        out_shape=jax.ShapeDtypeStruct((2, x_count, G), jnp.float32),
        in_specs=[smem, smem] + [vmem] * (4 + slabs) + [hbm],
        out_specs=hbm,
        scratch_shapes=[
            pltpu.VMEM((parts, LANES, 2 * SUB * SUB), jnp.bfloat16),
            pltpu.VMEM((SUB, parts * 2 * LANES, 2 * LANES), jnp.bfloat16),
            pltpu.VMEM((2, x_block, LANES), jnp.float32),
            pltpu.VMEM((4, 2, 4 * x_block, 2 * LANES), jnp.float32),
            pltpu.VMEM((SUB, x_block, parts * 2 * LANES), jnp.bfloat16),
            pltpu.VMEM((SUB, x_block, 2 * LANES), jnp.float32),
            pltpu.VMEM((4, 8, 2, 8, LANES), jnp.float32),
            pltpu.VMEM((x_block // out_rows, 2, out_rows, G), jnp.float32),
            pltpu.VMEM(more.shape, more.dtype),
            pltpu.SemaphoreType.DMA((x_block // out_rows,)),
            pltpu.SemaphoreType.DMA,
        ],
        compiler_params=pltpu.CompilerParams(vmem_limit_bytes=60 * 1024 * 1024),
        name="image",
    )(groups, x_base, rows, cols, mix, jnp.asarray(twist_table(scale)), *first, more)


def exchanged(value, axis, distance):
    peers = lax.axis_size(axis)
    return lax.ppermute(value, axis, [(i, i ^ distance) for i in range(peers)])


def gathered(pieces):
    slabs = lax.axis_size("slab")
    value = jnp.stack([pieces[0]] + [exchanged(piece, "pol", k) for k, piece in enumerate(pieces) if k])
    values = []
    for k in range(0, slabs, 2):
        moved = exchanged(value, "slab", k) if k else value
        values += [moved, exchanged(moved, "slab", 1)]
    return values


def in_image_domain(correlations, tracks, vis_counts, offsets, held_counts, pixel_weight):
    pols, slabs = lax.axis_size("pol"), lax.axis_size("slab")
    pol, slab = lax.axis_index("pol"), lax.axis_index("slab")
    devices = pols * slabs
    waves = SLOTS // devices
    capacity = SLOTS * slabs // devices
    x_count = G // slabs
    own_device = pol * slabs + slab
    held = held_counts.astype(jnp.int32)
    holders = jnp.arange(slabs, dtype=jnp.int32)
    before = jnp.sum(jnp.where(holders[None, :] < holders[:, None], held[None, :], 0), axis=1)
    total = jnp.sum(held)
    own_before = jnp.sum(jnp.where(holders == slab, before, 0))

    slot = jnp.arange(SLOTS, dtype=jnp.int32)
    order = jnp.where(slot[None, :] < held[:, None], before[:, None] + slot[None, :], -1).reshape(-1)
    device_at, seat_at = order % devices, order // devices
    pol_step = LANES // (GROUP * slabs)
    lane_order = (device_at % slabs) ^ slab
    pol_order = (device_at // slabs) ^ pol
    place = (seat_at // GROUP) * (pols // pol_step) + pol_order // pol_step
    place = place * LANES + lane_order * (pol_step * GROUP) + pol_order % pol_step * GROUP + seat_at % GROUP
    place = jnp.where(order >= 0, place, -1)
    chunk_count = capacity // GROUP * (pols // pol_step)
    spots = jnp.arange(chunk_count * LANES, dtype=jnp.int32)
    chosen = spots[:, None] == place[None, :]
    rows = jnp.sum(jnp.where(chosen, offsets[0][None, :], 0), axis=1).reshape(chunk_count, LANES)
    cols = jnp.sum(jnp.where(chosen, offsets[1][None, :], 0), axis=1).reshape(chunk_count, LANES)
    seats = jnp.arange(capacity, dtype=jnp.int32)
    mine = (seats[:, None] * devices + own_device) == order[None, :]
    wave_at = jnp.broadcast_to(holders[:, None] * waves + slot[None, :] // devices, (slabs, SLOTS)).reshape(-1)
    source = jnp.sum(jnp.where(mine, wave_at[None, :], 0), axis=1)
    start = jnp.sum(jnp.where(mine, jnp.bitwise_and(offsets[0], SUB - 1)[None, :], 0), axis=1)
    count = jnp.maximum((total - own_device + devices - 1) // devices, 0).reshape(1)

    visible = jnp.arange(VIS, dtype=jnp.int32)[None, :] < vis_counts[:, None]
    corr = jnp.where(visible[None], correlations[:, 0].astype(jnp.float32), 0.0)
    shift = (devices - own_before % devices) % devices

    def sent(value):
        lead = value.shape[0]
        value = value.reshape(lead, waves, devices, VIS)
        value = lax.dynamic_slice_in_dim(jnp.concatenate([value, value], axis=2), shift, devices, 2)
        return jnp.transpose(value, (2, 1, 0, 3)).reshape(devices, waves * lead * VIS)

    track_piece = waves * 3 * VIS // pols
    track_part = lax.dynamic_slice_in_dim(sent(tracks), pol * track_piece, track_piece, 1)
    packed = jnp.concatenate([sent(corr), track_part], axis=1)
    got = lax.all_to_all(packed, ("pol", "slab"), 0, 0, tiled=True).reshape(pols, slabs, -1)
    corr_size = waves * 2 * VIS
    got_corr = jnp.transpose(got[:, :, :corr_size].reshape(pols, slabs, waves, 2, VIS), (1, 2, 3, 0, 4))
    got_track = jnp.transpose(got[:, :, corr_size:], (1, 0, 2)).reshape(slabs, waves, 3, VIS)
    slots = jnp.concatenate(
        [
            got_corr.reshape(slabs, waves, 2 * pols, VIS),
            got_track,
            jnp.zeros((slabs, waves, 16 - 2 * pols - 3, VIS), jnp.float32),
        ],
        axis=2,
    ).reshape(slabs * waves, 16, VIS)
    weight_row = pixel_weight.reshape(1, SUB * SUB)
    *subgrids, extra = subgrids_of(count, pol.reshape(1), source, start, slots, weight_row)
    first = gathered(subgrids)
    many = total > devices * GROUP
    more = lax.cond(
        many,
        lambda: jnp.stack(gathered([extra[k] for k in range(pols)])),
        lambda: jnp.zeros((slabs,) + extra.shape, extra.dtype),
    )
    groups = jnp.where(many, capacity // GROUP, 1).reshape(1)
    norm_scale = 1.0 / (SUB * SUB * math.sqrt(VIS * SLOTS * slabs / 8.0))
    x_base = (slab * x_count).reshape(1)
    x_block = min(x_count, 256)
    mix_base, _ = lax.optimization_barrier((x_base, subgrids[0]))
    mix = mix_table(mix_base[0], x_count, x_block)
    sky = image_of(groups, x_base, first, more, rows, cols, mix, x_count, x_block, norm_scale, pol_step)
    return sky[:, None]


def fits_image_domain(mesh):
    pols, slabs = mesh.shape["pol"], mesh.shape["slab"]
    devices = pols * slabs
    whole = slabs & (slabs - 1) == 0 and slabs * GROUP <= LANES and SLOTS * slabs == 2 * GROUP * devices
    return whole and pols == 4 and SLOTS % devices == 0 and pols % (LANES // (GROUP * slabs)) == 0


def solution(mesh):
    in_specs = (P(None, "pol", "slab", None), P(None, "slab", None), P("slab"), P(), P(), P())
    out_specs = P(None, "pol", "slab", None)
    body = in_image_domain if fits_image_domain(mesh) else on_device
    return jax.shard_map(body, mesh=mesh, in_specs=in_specs, out_specs=out_specs, check_vma=False)
```

```python
import functools
import math

import jax
import jax.numpy as jnp
import numpy as np
from jax import lax
from jax.experimental import pallas as pl
from jax.experimental.pallas import tpu as pltpu
from jax.sharding import PartitionSpec as P

G = 4096
SUB = 32
VIS = 256
SLOTS = 64


TWO_PI = 2.0 * math.pi
FIELD_VIEW = 0.6
DEPTH_SCALE = 40.0
TRACK_SCALE = 0.375
COEF_REAL = np.array(
    [[0.5, 0.0, 0.0, 0.5], [0.5, 0.0, 0.0, -0.5], [0.0, 0.5, 0.5, 0.0], [0.0, 0.0, 0.0, 0.0]],
    np.float32,
)
COEF_IMAG = np.array(
    [[0.0, 0.0, 0.0, 0.0], [0.0, 0.0, 0.0, 0.0], [0.0, 0.0, 0.0, 0.0], [0.0, -0.5, 0.5, 0.0]],
    np.float32,
)


def partner_2(value, axis, distance):
    return lax.ppermute(value, axis, [(i, i ^ 1 << distance) for i in range(lax.axis_size(axis))])


def passed_along(value, axis, by):
    peers = lax.axis_size(axis)
    pairs = [(i, i + by) for i in range(peers) if 0 <= i + by < peers]
    return lax.ppermute(value, axis, pairs)


def pixel_tables():
    cells = jnp.arange(SUB * SUB, dtype=jnp.int32)
    row_pos = (cells // SUB - SUB // 2).astype(jnp.float32) / SUB
    col_pos = (cells % SUB - SUB // 2).astype(jnp.float32) / SUB
    depth = jnp.sqrt(1.0 - (FIELD_VIEW * col_pos) ** 2 - (FIELD_VIEW * row_pos) ** 2) - 1.0
    return (col_pos, row_pos, depth)


def phasor_table(track_set, tables):
    col_pos, row_pos, depth = tables
    u_cells = track_set[0] * (TRACK_SCALE * SUB)
    v_cells = track_set[1] * (TRACK_SCALE * SUB)
    w_cells = track_set[2] * DEPTH_SCALE
    phase = TWO_PI * (
        u_cells[:, None] * col_pos[None, :]
        + v_cells[:, None] * row_pos[None, :]
        + w_cells[:, None] * depth[None, :]
    )
    return jnp.concatenate([jnp.cos(phase), jnp.sin(phase)], axis=1).astype(jnp.bfloat16)


def subgrid_tables():
    positions = jnp.arange(SUB, dtype=jnp.int32) - SUB // 2
    turn_count = positions[:, None] * positions[None, :] % SUB
    angles = -TWO_PI * turn_count.astype(jnp.float32) / SUB
    return (jnp.cos(angles), jnp.sin(angles))


def dft_table(length):
    positions = jnp.arange(length, dtype=jnp.int32)
    turn_count = positions[:, None] * positions[None, :] % length
    angles = TWO_PI * turn_count.astype(jnp.float32) / length
    return (jnp.cos(angles), jnp.sin(angles))


def twiddle_table(first_len, second_len, length):
    first_pos = jnp.arange(first_len, dtype=jnp.int32)
    second_pos = jnp.arange(second_len, dtype=jnp.int32)
    turn_count = first_pos[:, None] * second_pos[None, :] % length
    angles = TWO_PI * turn_count.astype(jnp.float32) / length
    return (jnp.cos(angles), jnp.sin(angles))


def complex_einsum(pattern, left_pair, right_pair):
    highest = lax.Precision.HIGHEST
    left_re, left_im = left_pair
    right_re, right_im = right_pair
    real_part = jnp.einsum(pattern, left_re, right_re, precision=highest) - jnp.einsum(
        pattern, left_im, right_im, precision=highest
    )
    imag_part = jnp.einsum(pattern, left_re, right_im, precision=highest) + jnp.einsum(
        pattern, left_im, right_re, precision=highest
    )
    return (real_part, imag_part)


def complex_multiply(data_pair, table_pair):
    data_re, data_im = data_pair
    table_re, table_im = table_pair
    return (data_re * table_re - data_im * table_im, data_re * table_im + data_im * table_re)


def subgrid_transform(sub_re, sub_im, dft_pair):
    half_re, half_im = complex_einsum("...ij,cj->...ic", (sub_re, sub_im), dft_pair)
    return complex_einsum("ai,...ic->...ac", dft_pair, (half_re, half_im))


def place_blocks(window, blocks, row_starts, col_starts):
    block_count = blocks.shape[1]
    zero_index = jnp.zeros((), jnp.int32)

    def add_one(slot_index, current_window):
        block = lax.dynamic_index_in_dim(blocks, slot_index, 1, keepdims=False)
        corner = (zero_index, row_starts[slot_index], col_starts[slot_index])
        current = lax.dynamic_slice(current_window, corner, (2, SUB, SUB))
        return lax.dynamic_update_slice(current_window, current + block, corner)

    return lax.fori_loop(0, block_count, add_one, window)


def on_device(correlations, tracks, vis_counts, offsets, held_counts, pixel_weight):
    highest = lax.Precision.HIGHEST
    slab_count = lax.axis_size("slab")
    slab_index = lax.axis_index("slab")
    stokes_index = lax.axis_index("pol")
    pixel_area = SUB * SUB
    rows_local = G // slab_count
    tables = pixel_tables()
    dft_pair = subgrid_tables()
    gathered = lax.all_gather(correlations, "pol", axis=1, tiled=True)
    corr_float = gathered.astype(jnp.float32)
    select = (jnp.arange(4, dtype=jnp.int32) == stokes_index).astype(jnp.float32)
    coef_re = jnp.sum(select[:, None] * jnp.asarray(COEF_REAL), axis=0)
    coef_im = jnp.sum(select[:, None] * jnp.asarray(COEF_IMAG), axis=0)
    stokes_re = jnp.einsum("p,pnv->nv", coef_re, corr_float[0], precision=highest) - jnp.einsum(
        "p,pnv->nv", coef_im, corr_float[1], precision=highest
    )
    stokes_im = jnp.einsum("p,pnv->nv", coef_re, corr_float[1], precision=highest) + jnp.einsum(
        "p,pnv->nv", coef_im, corr_float[0], precision=highest
    )
    visible = (jnp.arange(VIS, dtype=jnp.int32)[None, :] < vis_counts[:, None]).astype(jnp.bfloat16)
    stokes_vis = jnp.stack([stokes_re, stokes_im]).astype(jnp.bfloat16) * visible[None]
    holder_ids = jnp.arange(slab_count, dtype=jnp.int32)
    own_held = jnp.sum(jnp.where(holder_ids == slab_index, held_counts, 0))

    def grid_range(vis_set, track_set, first_slot, stop_slot, capacity):

        def one_slot(slot_index, subgrid_set):
            phasor = phasor_table(
                lax.dynamic_index_in_dim(track_set, slot_index, 1, keepdims=False), tables
            )
            vis_slot = lax.dynamic_index_in_dim(vis_set, slot_index, 1, keepdims=False)
            product = jnp.dot(vis_slot, phasor, preferred_element_type=jnp.float32)
            sub_re = product[0, :pixel_area] - product[1, pixel_area:]
            sub_im = product[0, pixel_area:] + product[1, :pixel_area]
            update = jnp.stack([sub_re, sub_im])[:, None, :]
            return lax.dynamic_update_slice_in_dim(subgrid_set, update, slot_index, 1)

        zero_set = jnp.zeros((2, capacity, pixel_area), jnp.float32)
        return lax.fori_loop(first_slot, stop_slot, one_slot, zero_set)

    half_slots = SLOTS // 2
    swap_bit = slab_count.bit_length() - 2
    partner = jnp.bitwise_xor(slab_index, slab_count // 2)
    partner_held = jnp.sum(jnp.where(holder_ids == partner, held_counts, 0))
    pair_total = own_held + partner_held
    own_give = jnp.maximum(own_held - (pair_total + 1) // 2, 0)
    partner_give = jnp.maximum(partner_held - (pair_total + 1) // 2, 0)
    own_start = jnp.minimum(own_held - own_give, SLOTS - half_slots)
    partner_start = jnp.minimum(partner_held - partner_give, SLOTS - half_slots)
    send_vis = lax.dynamic_slice_in_dim(stokes_vis, own_start, half_slots, 1).astype(jnp.float32)
    send_track = lax.dynamic_slice_in_dim(tracks, own_start, half_slots, 1)
    got_vis, got_track = partner_2((send_vis, send_track), "slab", swap_bit)
    first_slot = partner_held - partner_give - partner_start
    helped = grid_range(
        got_vis.astype(jnp.bfloat16), got_track, first_slot, first_slot + partner_give, half_slots
    )
    returned_set = partner_2(helped, "slab", swap_bit)
    own_part = grid_range(stokes_vis, tracks, 0, own_held - own_give, SLOTS)
    subgrids = own_part + lax.dynamic_update_slice_in_dim(
        jnp.zeros_like(own_part), returned_set, own_start, 1
    )
    weight_flat = pixel_weight.reshape(pixel_area)
    sub_re = (subgrids[0] * weight_flat).reshape(SLOTS, SUB, SUB)
    sub_im = (subgrids[1] * weight_flat).reshape(SLOTS, SUB, SUB)
    uv_re, uv_im = subgrid_transform(sub_re, sub_im, dft_pair)
    uv_blocks = jnp.stack([uv_re, uv_im])
    own_offsets = lax.dynamic_slice_in_dim(offsets, slab_index * SLOTS, SLOTS, 1)
    own_rows = own_offsets[0] - slab_index * rows_local
    own_cols = own_offsets[1]
    window = jnp.zeros((2, rows_local + SUB, G), jnp.float32)
    window = place_blocks(window, uv_blocks, own_rows, own_cols)
    lower_rows = passed_along(window[:, rows_local:], "slab", 1)
    slab_grid = window[:, :rows_local].at[:, :SUB].add(lower_rows)
    small_side = G // 128
    large_side = 128
    table_small = dft_table(small_side)
    table_large = dft_table(large_side)
    twiddle = twiddle_table(small_side, large_side, G)
    plane_re = slab_grid[0].reshape(rows_local, small_side, large_side)
    plane_im = slab_grid[1].reshape(rows_local, small_side, large_side)
    step_re, step_im = complex_einsum("rkc,kx->rxc", (plane_re, plane_im), table_small)
    step_re, step_im = complex_multiply((step_re, step_im), twiddle)
    step_re, step_im = complex_einsum("rxc,cb->bxr", (step_re, step_im), table_large)
    moved_block = lax.all_to_all(
        jnp.stack([step_re, step_im]), "slab", split_axis=1, concat_axis=3, tiled=True
    )
    line_re = moved_block[0].reshape(rows_local, large_side, small_side)
    line_im = moved_block[1].reshape(rows_local, large_side, small_side)
    line_re, line_im = complex_einsum("xab,ay->xby", (line_re, line_im), table_large)
    line_re, line_im = complex_multiply((line_re, line_im), twiddle)
    line_re, line_im = complex_einsum("xby,bz->xzy", (line_re, line_im), table_small)
    norm_scale = 1.0 / (SUB * SUB * math.sqrt(VIS * SLOTS * slab_count / 8.0))
    sky_re = line_re.reshape(rows_local, G) * norm_scale
    sky_im = line_im.reshape(rows_local, G) * norm_scale
    return jnp.stack([sky_re, sky_im])[:, None]


LANES = 128
GROUP = 8


def turn_polynomials():
    z = np.cos(np.linspace(0.0, np.pi, 4001)) * 0.125 + 0.125
    r = np.sqrt(z)
    sine = np.where(r > 0, np.sin(np.pi * r) / np.where(r > 0, r, 1.0), np.pi)
    fits = []
    for values in (sine, np.cos(np.pi * r)):
        fit = np.polynomial.chebyshev.Chebyshev.fit(z, values, 4, domain=[0.0, 0.25])
        fits.append([float(v) for v in fit.convert(kind=np.polynomial.Polynomial).coef])
    return fits


SINE_COEF, COSINE_COEF = turn_polynomials()


def cos_sin_turns(turns):
    rest = turns - jnp.floor(turns + 0.5)
    square = rest * rest
    sine = SINE_COEF[-1]
    cosine = COSINE_COEF[-1]
    for coef in SINE_COEF[-2::-1]:
        sine = sine * square + coef
    for coef in COSINE_COEF[-2::-1]:
        cosine = cosine * square + coef
    sine = sine * rest
    double = sine + sine
    return 1.0 - double * sine, double * cosine


def times(left, right):
    return (left[0] * right[0] - left[1] * right[1], left[0] * right[1] + left[1] * right[0])


def plus(left, right):
    return (left[0] + right[0], left[1] + right[1])


def minus(left, right):
    return (left[0] - right[0], left[1] - right[1])


def quarter(value, sign):
    if sign > 0:
        return (-value[1], value[0])
    return (value[1], -value[0])


def dft_4(values, sign):
    a, b, c, d = values
    even_sum, even_diff = plus(a, c), minus(a, c)
    odd_sum, odd_diff = plus(b, d), quarter(minus(b, d), sign)
    return [plus(even_sum, odd_sum), plus(even_diff, odd_diff), minus(even_sum, odd_sum), minus(even_diff, odd_diff)]


ROOT_HALF = math.sqrt(0.5)


def dft_8(values, sign):
    even = dft_4(values[0::2], sign)
    odd = dft_4(values[1::2], sign)
    a, b = odd[1]
    odd[1] = ((a - b) * ROOT_HALF, (a + b) * ROOT_HALF) if sign > 0 else ((a + b) * ROOT_HALF, (b - a) * ROOT_HALF)
    odd[2] = quarter(odd[2], sign)
    a, b = odd[3]
    odd[3] = ((-a - b) * ROOT_HALF, (a - b) * ROOT_HALF) if sign > 0 else ((b - a) * ROOT_HALF, (-a - b) * ROOT_HALF)
    return [plus(e, o) for e, o in zip(even, odd)] + [minus(e, o) for e, o in zip(even, odd)]


def pixel_rows():
    row, col = np.divmod(np.arange(SUB * SUB), SUB)
    l = ((col - SUB // 2) / SUB).astype(np.float32)
    m = ((row - SUB // 2) / SUB).astype(np.float32)
    view = np.float32(FIELD_VIEW)
    n = (np.sqrt(np.float32(1.0) - (view * l) ** 2 - (view * m) ** 2) - np.float32(1.0)).astype(np.float32)
    return np.stack([l, m, n, row.astype(np.float32)] + [np.zeros_like(l)] * 4).astype(np.float32)


HALVES = VIS // LANES
WAVES = 2
TRACK_ROWS = WAVES * 3 * HALVES


def pack_kernel(held_ref, place_ref, counts_ref, corr_ref, track_ref, out_ref):
    devices = out_ref.shape[0]
    slab, pol = place_ref[0], place_ref[1]

    def count_before(holder, total):
        return total + jnp.where(holder < slab, held_ref[holder], 0)

    shift = jnp.bitwise_and(lax.fori_loop(0, held_ref.shape[0], count_before, 0), devices - 1)
    counts = jnp.transpose(jnp.broadcast_to(counts_ref[...].astype(jnp.float32), (LANES, counts_ref.shape[1])))
    lane = lax.broadcasted_iota(jnp.int32, (devices, LANES), 1).astype(jnp.float32)
    rows = []
    for wave in range(WAVES):
        at = pl.ds(wave * devices, devices)
        for c in range(2):
            for half in range(HALVES):
                value = corr_ref[c, at, pl.ds(half * LANES, LANES)].astype(jnp.float32)
                limit = counts[wave * devices : (wave + 1) * devices] - float(half * LANES)
                rows.append(jnp.where(lane < limit, value, 0.0))
    piece = TRACK_ROWS // 4
    for row in range(piece):
        value = None
        for sender in range(4):
            wave, axis, half = np.unravel_index(sender * piece + row, (WAVES, 3, HALVES))
            part = track_ref[int(axis), pl.ds(int(wave) * devices, devices), pl.ds(int(half) * LANES, LANES)]
            value = part if value is None else jnp.where(pol == sender, part, value)
        rows.append(value)
    for row, value in enumerate(rows):
        out_ref[:, row, :] = pltpu.roll(value, shift, 0)
    for row in range(len(rows), out_ref.shape[1]):
        out_ref[:, row, :] = jnp.zeros((devices, LANES), jnp.float32)


def packed(held, place, counts, corr, tracks, devices):
    smem = pl.BlockSpec(memory_space=pltpu.SMEM)
    vmem = pl.BlockSpec(memory_space=pltpu.VMEM)
    return pl.pallas_call(
        pack_kernel,
        out_shape=jax.ShapeDtypeStruct((devices, 16, LANES), jnp.float32),
        in_specs=[smem, smem, vmem, vmem, vmem],
        out_specs=vmem,
        name="packed",
    )(held, place, counts, corr, tracks)


def row_twiddles():
    angle = -2.0 * np.pi * np.arange(8)[:, None] * (np.arange(LANES)[None, :] // SUB) / SUB
    return np.concatenate([np.cos(angle), np.sin(angle)], axis=0).astype(np.float32)


def subgrid_kernel(held_counts_ref, place_ref, offsets_ref, slots_ref, table_ref, twiddle_ref, weight_ref, *refs):
    piece_refs, more_ref, held_ref = refs[:4], refs[4], refs[5]
    held_ref[...] = jnp.zeros_like(held_ref)
    slab, pol = place_ref[0], place_ref[1]
    slabs = slots_ref.shape[0] // 4
    devices = slots_ref.shape[0]
    own = pol * slabs + slab
    total = lax.fori_loop(0, slabs, lambda holder, value: value + held_counts_ref[holder], 0)
    count = lax.shift_right_logical(total - own + (devices - 1), devices.bit_length() - 1)

    def locate(index):
        wanted = index * devices + own

        def look(holder, found):
            before, at_holder, at_slot = found
            after = before + held_counts_ref[holder]
            inside = (wanted >= before) & (wanted < after)
            return after, jnp.where(inside, holder, at_holder), jnp.where(inside, wanted - before, at_slot)

        _, at_holder, at_slot = lax.fori_loop(0, slabs, look, (0, 0, 0))
        return at_holder, at_slot

    def one_slot(index, carry):
        holder, slot = locate(index)
        early = slot < devices
        row_start = jnp.bitwise_and(offsets_ref[0, holder * SLOTS + slot], SUB - 1).astype(jnp.float32)
        tiles = [slots_ref[p * slabs + holder] for p in range(4)]
        xx, xy, yx, yy = [0.5 * jnp.where(early, tile[0:4], tile[4:8]) for tile in tiles]
        turned = xy - yx
        parameters = [xx + yy, xx - yy, xy + yx, jnp.concatenate([turned[2:4], -turned[0:2]], axis=0)]
        chosen = []
        for k in range(4):
            value = parameters[k]
            for other in range(1, 4):
                value = jnp.where(pol == other, parameters[k ^ other], value)
            chosen.append(value)
        halves = [
            jnp.concatenate([chosen[k][2 * c + half : 2 * c + half + 1] for c in range(2) for k in range(4)], axis=0)
            for half in range(2)
        ]
        vis = jnp.concatenate(halves, axis=1).astype(jnp.bfloat16)

        def track_half(axis, half):
            found = []
            for wave in range(WAVES):
                sender, row = divmod((wave * 3 + axis) * HALVES + half, TRACK_ROWS // 4)
                found.append(tiles[sender][8 + row : 9 + row])
            return jnp.where(early, found[0], found[1])

        track = jnp.concatenate(
            [jnp.concatenate([track_half(axis, half) for half in range(2)], axis=1) for axis in (0, 1, 2, 2, 2, 2, 2, 2)], axis=0
        )
        track = jnp.transpose(track)
        shape = (VIS, LANES)
        u = jnp.broadcast_to(track[:, 0:1] * (TRACK_SCALE * SUB), shape)
        v = jnp.broadcast_to(track[:, 1:2] * (TRACK_SCALE * SUB), shape)
        w = jnp.broadcast_to(track[:, 2:3] * DEPTH_SCALE, shape)
        placed = []
        for tile in range(SUB * SUB // LANES):
            lanes = pl.ds(tile * LANES, LANES)
            turns = u * table_ref[0:1, lanes] + v * table_ref[1:2, lanes] + w * table_ref[2:3, lanes]
            cosine, sine = cos_sin_turns(turns)
            phasor = jnp.concatenate([cosine.astype(jnp.bfloat16), sine.astype(jnp.bfloat16)], axis=1)
            product = jnp.dot(vis, phasor, preferred_element_type=jnp.float32)
            real = product[:4, :LANES] - product[4:, LANES:]
            imag = product[:4, LANES:] + product[4:, :LANES]
            weight = weight_ref[0:1, lanes]
            pixel_row = table_ref[3:4, lanes]
            turn = (row_start * (pixel_row - SUB // 2) + pixel_row * (SUB // 2)) * (1.0 / SUB)
            turn_re, turn_im = cos_sin_turns(turn)
            turn_re, turn_im = turn_re * weight, turn_im * weight
            placed.append(times((real, imag), (turn_re, turn_im)))
        for rho, value in enumerate(dft_8(placed, -1)):
            if rho:
                value = times(value, (twiddle_ref[rho : rho + 1], twiddle_ref[8 + rho : 9 + rho]))
            held_ref[index, :, pl.ds(2 * rho * LANES, LANES)] = value[0]
            held_ref[index, :, pl.ds((2 * rho + 1) * LANES, LANES)] = value[1]
        return carry

    lax.fori_loop(0, count, one_slot, 0)
    for k in range(4):
        piece_refs[k][...] = held_ref[:GROUP, k, :].astype(jnp.bfloat16)
        more_ref[k] = held_ref[GROUP:, k, :].astype(jnp.bfloat16)


def subgrids_of(held, place, offsets, slots, weight_row, capacity):
    smem = pl.BlockSpec(memory_space=pltpu.SMEM)
    vmem = pl.BlockSpec(memory_space=pltpu.VMEM)
    return pl.pallas_call(
        subgrid_kernel,
        out_shape=[jax.ShapeDtypeStruct((GROUP, 2 * SUB * SUB), jnp.bfloat16)] * 4
        + [jax.ShapeDtypeStruct((4, capacity - GROUP, 2 * SUB * SUB), jnp.bfloat16)],
        in_specs=[smem] * 3 + [vmem] * 4,
        out_specs=[vmem] * 5,
        scratch_shapes=[pltpu.VMEM((capacity, 4, 2 * SUB * SUB), jnp.float32)],
        name="subgrids",
    )(held, place, offsets, slots, jnp.asarray(pixel_rows()), jnp.asarray(row_twiddles()), weight_row)


def image_kernel(pol_step, x_block, slabs, groups_ref, base_ref, row_ref, col_ref, mix_ref, twist_ref, *refs):
    first_refs, more_ref, sky_ref = refs[:slabs], refs[slabs], refs[slabs + 1]
    bundle_ref, phase_ref, col_phase_ref, *half_refs, moved_ref, sum_ref, stage_ref, out_ref = refs[slabs + 2 : -3]
    later_ref, sem_ref, later_sem_ref = refs[-3:]
    x_blocks = sky_ref.shape[1] // x_block
    groups = groups_ref[0]
    lane_index = lax.broadcasted_iota(jnp.int32, (LANES, LANES), 1)
    eighth = SUB // 4
    out_rows = out_ref.shape[2]
    out_steps = x_block // out_rows
    group_chunks = 4 // pol_step
    depth = 2 * LANES

    def load_phases(group, part):
        chunk = group * group_chunks + part
        rows = jnp.transpose(jnp.broadcast_to(row_ref[pl.ds(chunk, 1), :].astype(jnp.float32), (LANES, LANES)))
        rows = rows.astype(jnp.int32)
        high = lax.shift_right_logical(rows, 5)
        low = jnp.bitwise_and(rows, SUB - 1)
        here = cos_sin_turns(jnp.bitwise_and(high * lane_index, LANES - 1).astype(jnp.float32) * (1.0 / LANES))
        later = cos_sin_turns(jnp.bitwise_and((high + 1) * lane_index, LANES - 1).astype(jnp.float32) * (1.0 / LANES))
        re_rows = pl.ds(part * depth, LANES)
        im_rows = pl.ds(part * depth + LANES, LANES)

        def one_phase(residue, inner):
            carried = low > residue
            re = jnp.where(carried, later[0], here[0]).astype(jnp.bfloat16)
            im = jnp.where(carried, later[1], here[1])
            phase_ref[residue, re_rows, :LANES] = re
            phase_ref[residue, re_rows, LANES:] = im.astype(jnp.bfloat16)
            phase_ref[residue, im_rows, :LANES] = (-im).astype(jnp.bfloat16)
            phase_ref[residue, im_rows, LANES:] = re
            return inner

        lax.fori_loop(0, SUB, one_phase, 0)

    def move_rows(group, part, block):
        chunk = group * group_chunks + part
        cols = col_ref[pl.ds(chunk, 1), :]
        x_index = lax.broadcasted_iota(jnp.int32, (x_block, LANES), 0) + (base_ref[0] + block * x_block)
        turns = jnp.bitwise_and(x_index * cols, G - 1).astype(jnp.float32) * (1.0 / G)
        turn_re, turn_im = cos_sin_turns(turns)
        col_phase_ref[0] = turn_re
        col_phase_ref[1] = turn_im
        re_lanes = pl.ds(pl.multiple_of(part * depth, LANES), LANES)
        im_lanes = pl.ds(pl.multiple_of(part * depth + LANES, LANES), LANES)

        def mix_pair(pair, half_ref):
            wide = jnp.concatenate(
                [
                    bundle_ref[part, :, pl.ds(4 * pair * LANES, depth)],
                    bundle_ref[part, :, pl.ds((4 * pair + 2) * LANES, depth)],
                ],
                axis=0,
            )
            for side in range(2):
                half_ref[side] = lax.dot_general(
                    mix_ref[block, side], wide, (((1,), (1,)), ((), ())), preferred_element_type=jnp.float32
                )

        def turn_pair(pair, half_ref):
            for tile in range(x_block // 16):
                rows_at = pl.ds(tile * 16, 16)
                turn = (col_phase_ref[0, rows_at], col_phase_ref[1, rows_at])
                for low in range(2):
                    at = pl.ds(low * LANES, LANES)
                    for high in range(4):
                        tile_rows = pl.ds(high * x_block + tile * 16, 16)
                        re, im = times((half_ref[0, tile_rows, at], half_ref[1, tile_rows, at]), turn)
                        residue = 2 * pair + low + 8 * high
                        moved_ref[residue, rows_at, re_lanes] = re.astype(jnp.bfloat16)
                        moved_ref[residue, rows_at, im_lanes] = im.astype(jnp.bfloat16)

        halves = half_refs
        mix_pair(0, halves[0])
        for pair in range(1, eighth // 2):
            mix_pair(pair, halves[pair % 2])
            turn_pair(pair - 1, halves[(pair - 1) % 2])
        turn_pair(eighth // 2 - 1, halves[(eighth // 2 - 1) % 2])

    def load_group(group):
        @pl.when(group > 0)
        def _():
            copy = pltpu.make_async_copy(more_ref, later_ref, later_sem_ref)
            copy.start()
            copy.wait()

        for part in range(group_chunks):
            polarized = pl.ds(part * pol_step, pol_step)
            span = pol_step * GROUP
            for peer in range(slabs):
                rows_at = pl.ds(peer * span, span)

                @pl.when(group == 0)
                def _(part=part, polarized=polarized, peer=peer, rows_at=rows_at):
                    bundle_ref[part, rows_at] = first_refs[peer][polarized].reshape(span, -1)

                @pl.when(group > 0)
                def _(part=part, polarized=polarized, peer=peer, rows_at=rows_at):
                    bundle_ref[part, rows_at] = later_ref[peer, polarized].reshape(span, -1)

            load_phases(group, part)

    def copy_out(block, step):
        x_at = pl.ds(pl.multiple_of(block * x_block + step * out_rows, 8), out_rows)
        return pltpu.make_async_copy(out_ref.at[step], sky_ref.at[:, x_at], sem_ref.at[step])

    def one_block(block, carry):
        def one_group(group, inner):
            @pl.when((block == 0) | (groups > 1))
            def _():
                load_group(group)

            def one_part(part, innermost):
                move_rows(group, part, block)
                return innermost

            lax.fori_loop(0, group_chunks, one_part, 0)

            @pl.when(group == 0)
            def _():
                def one_residue(residue, innermost):
                    sum_ref[residue] = jnp.dot(
                        moved_ref[residue], phase_ref[residue], preferred_element_type=jnp.float32
                    )
                    return innermost

                lax.fori_loop(0, SUB, one_residue, 0, unroll=4)

            @pl.when(group > 0)
            def _():
                def one_residue(residue, innermost):
                    sum_ref[residue] += jnp.dot(
                        moved_ref[residue], phase_ref[residue], preferred_element_type=jnp.float32
                    )
                    return innermost

                lax.fori_loop(0, SUB, one_residue, 0)

            return inner

        lax.fori_loop(0, groups, one_group, 0)

        def one_step(step, inner):
            @pl.when(block > 0)
            def _():
                copy_out(block - 1, step).wait()

            def one_tile(tile, innermost):
                rows_at = pl.ds(pl.multiple_of(step * out_rows + tile * 8, 8), 8)
                for second in range(4):
                    parts = []
                    for first in range(8):
                        residue = 4 * first + second
                        value = (sum_ref[residue, rows_at, :LANES], sum_ref[residue, rows_at, LANES:])
                        twist = (twist_ref[2 * residue : 2 * residue + 1], twist_ref[2 * residue + 1 : 2 * residue + 2])
                        parts.append(times(value, twist))
                    for first, value in enumerate(dft_8(parts, 1)):
                        if first * second:
                            angle = TWO_PI * first * second / SUB
                            value = times(value, (math.cos(angle), math.sin(angle)))
                        stage_ref[second, first, 0] = value[0]
                        stage_ref[second, first, 1] = value[1]
                to_rows = pl.ds(pl.multiple_of(tile * 8, 8), 8)
                for first in range(8):
                    parts = [(stage_ref[second, first, 0], stage_ref[second, first, 1]) for second in range(4)]
                    for second, value in enumerate(dft_4(parts, 1)):
                        lanes = pl.ds((first + 8 * second) * LANES, LANES)
                        out_ref[step, 0, to_rows, lanes] = value[0]
                        out_ref[step, 1, to_rows, lanes] = value[1]
                return innermost

            lax.fori_loop(0, out_rows // 8, one_tile, 0)
            copy_out(block, step).start()
            return inner

        lax.fori_loop(0, out_steps, one_step, 0)
        return carry

    lax.fori_loop(0, x_blocks, one_block, 0)
    for step in range(out_steps):
        copy_out(x_blocks - 1, step).wait()


def twist_table(scale):
    residue = np.arange(SUB)[:, None]
    lane = np.arange(LANES)[None, :]
    angle = 2.0 * np.pi * (residue * lane % G) / G
    sign = np.where(residue % 2 == 0, scale, -scale)
    return np.stack([sign * np.cos(angle), sign * np.sin(angle)], axis=1).reshape(2 * SUB, LANES).astype(np.float32)


def mix_kernel(base_ref, sub_ref, turn_ref, mix_ref):
    x_block = mix_ref.shape[2] // 4
    highest = lax.Precision.HIGHEST
    cell = lax.broadcasted_iota(jnp.int32, (x_block, LANES), 1)

    def one_block(block, carry):
        x_index = lax.broadcasted_iota(jnp.int32, (x_block, LANES), 0) + (base_ref[0] + block * x_block)
        line_re, line_im = cos_sin_turns(jnp.bitwise_and(x_index * cell, G - 1).astype(jnp.float32) * (1.0 / G))
        by_re = jnp.dot(line_re, sub_ref[...], precision=highest, preferred_element_type=jnp.float32)
        by_im = jnp.dot(line_im, sub_ref[...], precision=highest, preferred_element_type=jnp.float32)
        core = (by_re[:, :LANES] - by_im[:, LANES:], by_re[:, LANES:] + by_im[:, :LANES])
        for rho in range(4):
            re, im = times(core, (turn_ref[rho : rho + 1], turn_ref[4 + rho : 5 + rho]))
            rows_at = pl.ds(rho * x_block, x_block)
            mix_ref[block, 0, rows_at, :LANES] = re.astype(jnp.bfloat16)
            mix_ref[block, 0, rows_at, LANES:] = (-im).astype(jnp.bfloat16)
            mix_ref[block, 1, rows_at, :LANES] = im.astype(jnp.bfloat16)
            mix_ref[block, 1, rows_at, LANES:] = re.astype(jnp.bfloat16)
        return carry

    lax.fori_loop(0, mix_ref.shape[0], one_block, 0)


def mix_table(x_base, x_count, x_block):
    cells, pixels = np.arange(LANES)[:, None], np.arange(LANES)[None, :] % SUB
    angle = -2.0 * np.pi * ((cells - SUB // 2) * (pixels - SUB // 2) % SUB) / SUB
    used = cells < SUB
    sub = np.concatenate([np.where(used, np.cos(angle), 0.0), np.where(used, np.sin(angle), 0.0)], axis=1)
    turn = (np.arange(4)[:, None] * (np.arange(LANES)[None, :] // SUB)) % 4
    turns = np.concatenate([np.array([1.0, 0.0, -1.0, 0.0])[turn], np.array([0.0, -1.0, 0.0, 1.0])[turn]])
    smem = pl.BlockSpec(memory_space=pltpu.SMEM)
    vmem = pl.BlockSpec(memory_space=pltpu.VMEM)
    return pl.pallas_call(
        mix_kernel,
        out_shape=jax.ShapeDtypeStruct((x_count // x_block, 2, 4 * x_block, 2 * LANES), jnp.bfloat16),
        in_specs=[smem, vmem, vmem],
        out_specs=vmem,
        cost_estimate=pl.CostEstimate(flops=1 << 30, bytes_accessed=1 << 22, transcendentals=0),
        name="mix",
    )(x_base, jnp.asarray(sub, jnp.float32), jnp.asarray(turns, jnp.float32))


def image_of(groups, x_base, first, more, rows, cols, mix, x_count, x_block, scale, pol_step):
    out_rows = min(x_block, 64)
    parts = 4 // pol_step
    slabs = len(first)
    smem = pl.BlockSpec(memory_space=pltpu.SMEM)
    vmem = pl.BlockSpec(memory_space=pltpu.VMEM)
    hbm = pl.BlockSpec(memory_space=pl.ANY)
    return pl.pallas_call(
        functools.partial(image_kernel, pol_step, x_block, slabs),
        out_shape=jax.ShapeDtypeStruct((2, x_count, G), jnp.float32),
        in_specs=[smem, smem] + [vmem] * (4 + slabs) + [hbm],
        out_specs=hbm,
        scratch_shapes=[
            pltpu.VMEM((parts, LANES, 2 * SUB * SUB), jnp.bfloat16),
            pltpu.VMEM((SUB, parts * 2 * LANES, 2 * LANES), jnp.bfloat16),
            pltpu.VMEM((2, x_block, LANES), jnp.float32),
            pltpu.VMEM((2, 4 * x_block, 2 * LANES), jnp.float32),
            pltpu.VMEM((2, 4 * x_block, 2 * LANES), jnp.float32),
            pltpu.VMEM((SUB, x_block, parts * 2 * LANES), jnp.bfloat16),
            pltpu.VMEM((SUB, x_block, 2 * LANES), jnp.float32),
            pltpu.VMEM((4, 8, 2, 8, LANES), jnp.float32),
            pltpu.VMEM((x_block // out_rows, 2, out_rows, G), jnp.float32),
            pltpu.VMEM(more.shape, more.dtype),
            pltpu.SemaphoreType.DMA((x_block // out_rows,)),
            pltpu.SemaphoreType.DMA,
        ],
        compiler_params=pltpu.CompilerParams(vmem_limit_bytes=60 * 1024 * 1024),
        name="image",
    )(groups, x_base, rows, cols, mix, jnp.asarray(twist_table(scale)), *first, more)


def exchanged(value, axis, distance):
    peers = lax.axis_size(axis)
    return lax.ppermute(value, axis, [(i, i ^ distance) for i in range(peers)])


def gathered(pieces, beside=None):
    slabs = lax.axis_size("slab")
    value = jnp.stack([pieces[0]] + [exchanged(piece, "pol", k) for k, piece in enumerate(pieces) if k])
    planes = [value] + [exchanged(value, "slab", k) for k in range(2, slabs, 2)]
    made = None
    if beside is not None:
        made = beside(value)
        planes[-1], made = lax.optimization_barrier((planes[-1], made))
    values = []
    for plane in planes:
        values += [plane, exchanged(plane, "slab", 1)]
    return values, made


def in_image_domain(correlations, tracks, vis_counts, offsets, held_counts, pixel_weight):
    pols, slabs = lax.axis_size("pol"), lax.axis_size("slab")
    pol, slab = lax.axis_index("pol"), lax.axis_index("slab")
    devices = pols * slabs
    capacity = SLOTS * slabs // devices
    x_count = G // slabs
    held = held_counts.astype(jnp.int32)
    holders = jnp.arange(slabs, dtype=jnp.int32)
    where_at = jnp.stack([slab, pol]).astype(jnp.int32)
    sent = packed(held, where_at, vis_counts.reshape(1, SLOTS), correlations[:, 0], tracks, devices)
    slots = lax.all_to_all(sent, ("pol", "slab"), 0, 0, tiled=True)
    held, _ = lax.optimization_barrier((held, sent))
    before = jnp.sum(jnp.where(holders[None, :] < holders[:, None], held[None, :], 0), axis=1)
    total = jnp.sum(held)

    slot = jnp.arange(SLOTS, dtype=jnp.int32)
    order = jnp.where(slot[None, :] < held[:, None], before[:, None] + slot[None, :], -1).reshape(-1)
    device_at, seat_at = order % devices, order // devices
    pol_step = LANES // (GROUP * slabs)
    lane_order = (device_at % slabs) ^ slab
    pol_order = (device_at // slabs) ^ pol
    place = (seat_at // GROUP) * (pols // pol_step) + pol_order // pol_step
    place = place * LANES + lane_order * (pol_step * GROUP) + pol_order % pol_step * GROUP + seat_at % GROUP
    place = jnp.where(order >= 0, place, -1)
    chunk_count = capacity // GROUP * (pols // pol_step)
    spots = jnp.arange(chunk_count * LANES, dtype=jnp.int32)
    chosen = spots[:, None] == place[None, :]
    rows = jnp.sum(jnp.where(chosen, offsets[0][None, :], 0), axis=1).reshape(chunk_count, LANES)
    cols = jnp.sum(jnp.where(chosen, offsets[1][None, :], 0), axis=1).reshape(chunk_count, LANES)
    slots, rows, cols = lax.optimization_barrier((slots, rows, cols))
    weight_row = pixel_weight.reshape(1, SUB * SUB)
    *pieces, extra = subgrids_of(held, where_at, offsets.astype(jnp.int32), slots, weight_row, capacity)
    norm_scale = 1.0 / (SUB * SUB * math.sqrt(VIS * SLOTS * slabs / 8.0))
    x_base = (slab * x_count).reshape(1)
    x_block = min(x_count, 256)

    def mixed(after):
        base, _ = lax.optimization_barrier((x_base, after))
        return mix_table(base, x_count, x_block)

    first, mix = gathered(pieces, mixed)
    many = total > devices * GROUP
    more = lax.cond(
        many,
        lambda: jnp.stack(gathered([extra[k] for k in range(pols)])[0]),
        lambda: jnp.zeros((slabs,) + extra.shape, extra.dtype),
    )
    groups = jnp.where(many, capacity // GROUP, 1).reshape(1)
    sky = image_of(groups, x_base, first, more, rows, cols, mix, x_count, x_block, norm_scale, pol_step)
    return sky[:, None]


def fits_image_domain(mesh):
    pols, slabs = mesh.shape["pol"], mesh.shape["slab"]
    devices = pols * slabs
    whole = slabs & (slabs - 1) == 0 and slabs * GROUP <= LANES and SLOTS * slabs == 2 * GROUP * devices
    return whole and pols == 4 and SLOTS == WAVES * devices and pols % (LANES // (GROUP * slabs)) == 0


def solution(mesh):
    in_specs = (P(None, "pol", "slab", None), P(None, "slab", None), P("slab"), P(), P(), P())
    out_specs = P(None, "pol", "slab", None)
    body = in_image_domain if fits_image_domain(mesh) else on_device
    return jax.shard_map(body, mesh=mesh, in_specs=in_specs, out_specs=out_specs, check_vma=False)
```

```python
import functools
import math

import jax
import jax.numpy as jnp
import numpy as np
from jax import lax
from jax.experimental import pallas as pl
from jax.experimental.pallas import tpu as pltpu
from jax.sharding import PartitionSpec as P

G = 4096
SUB = 32
VIS = 256
SLOTS = 64


TWO_PI = 2.0 * math.pi
FIELD_VIEW = 0.6
DEPTH_SCALE = 40.0
TRACK_SCALE = 0.375
COEF_REAL = np.array(
    [[0.5, 0.0, 0.0, 0.5], [0.5, 0.0, 0.0, -0.5], [0.0, 0.5, 0.5, 0.0], [0.0, 0.0, 0.0, 0.0]],
    np.float32,
)
COEF_IMAG = np.array(
    [[0.0, 0.0, 0.0, 0.0], [0.0, 0.0, 0.0, 0.0], [0.0, 0.0, 0.0, 0.0], [0.0, -0.5, 0.5, 0.0]],
    np.float32,
)


def partner_2(value, axis, distance):
    return lax.ppermute(value, axis, [(i, i ^ 1 << distance) for i in range(lax.axis_size(axis))])


def passed_along(value, axis, by):
    peers = lax.axis_size(axis)
    pairs = [(i, i + by) for i in range(peers) if 0 <= i + by < peers]
    return lax.ppermute(value, axis, pairs)


def pixel_tables():
    cells = jnp.arange(SUB * SUB, dtype=jnp.int32)
    row_pos = (cells // SUB - SUB // 2).astype(jnp.float32) / SUB
    col_pos = (cells % SUB - SUB // 2).astype(jnp.float32) / SUB
    depth = jnp.sqrt(1.0 - (FIELD_VIEW * col_pos) ** 2 - (FIELD_VIEW * row_pos) ** 2) - 1.0
    return (col_pos, row_pos, depth)


def phasor_table(track_set, tables):
    col_pos, row_pos, depth = tables
    u_cells = track_set[0] * (TRACK_SCALE * SUB)
    v_cells = track_set[1] * (TRACK_SCALE * SUB)
    w_cells = track_set[2] * DEPTH_SCALE
    phase = TWO_PI * (
        u_cells[:, None] * col_pos[None, :]
        + v_cells[:, None] * row_pos[None, :]
        + w_cells[:, None] * depth[None, :]
    )
    return jnp.concatenate([jnp.cos(phase), jnp.sin(phase)], axis=1).astype(jnp.bfloat16)


def subgrid_tables():
    positions = jnp.arange(SUB, dtype=jnp.int32) - SUB // 2
    turn_count = positions[:, None] * positions[None, :] % SUB
    angles = -TWO_PI * turn_count.astype(jnp.float32) / SUB
    return (jnp.cos(angles), jnp.sin(angles))


def dft_table(length):
    positions = jnp.arange(length, dtype=jnp.int32)
    turn_count = positions[:, None] * positions[None, :] % length
    angles = TWO_PI * turn_count.astype(jnp.float32) / length
    return (jnp.cos(angles), jnp.sin(angles))


def twiddle_table(first_len, second_len, length):
    first_pos = jnp.arange(first_len, dtype=jnp.int32)
    second_pos = jnp.arange(second_len, dtype=jnp.int32)
    turn_count = first_pos[:, None] * second_pos[None, :] % length
    angles = TWO_PI * turn_count.astype(jnp.float32) / length
    return (jnp.cos(angles), jnp.sin(angles))


def complex_einsum(pattern, left_pair, right_pair):
    highest = lax.Precision.HIGHEST
    left_re, left_im = left_pair
    right_re, right_im = right_pair
    real_part = jnp.einsum(pattern, left_re, right_re, precision=highest) - jnp.einsum(
        pattern, left_im, right_im, precision=highest
    )
    imag_part = jnp.einsum(pattern, left_re, right_im, precision=highest) + jnp.einsum(
        pattern, left_im, right_re, precision=highest
    )
    return (real_part, imag_part)


def complex_multiply(data_pair, table_pair):
    data_re, data_im = data_pair
    table_re, table_im = table_pair
    return (data_re * table_re - data_im * table_im, data_re * table_im + data_im * table_re)


def subgrid_transform(sub_re, sub_im, dft_pair):
    half_re, half_im = complex_einsum("...ij,cj->...ic", (sub_re, sub_im), dft_pair)
    return complex_einsum("ai,...ic->...ac", dft_pair, (half_re, half_im))


def place_blocks(window, blocks, row_starts, col_starts):
    block_count = blocks.shape[1]
    zero_index = jnp.zeros((), jnp.int32)

    def add_one(slot_index, current_window):
        block = lax.dynamic_index_in_dim(blocks, slot_index, 1, keepdims=False)
        corner = (zero_index, row_starts[slot_index], col_starts[slot_index])
        current = lax.dynamic_slice(current_window, corner, (2, SUB, SUB))
        return lax.dynamic_update_slice(current_window, current + block, corner)

    return lax.fori_loop(0, block_count, add_one, window)


def on_device(correlations, tracks, vis_counts, offsets, held_counts, pixel_weight):
    highest = lax.Precision.HIGHEST
    slab_count = lax.axis_size("slab")
    slab_index = lax.axis_index("slab")
    stokes_index = lax.axis_index("pol")
    pixel_area = SUB * SUB
    rows_local = G // slab_count
    tables = pixel_tables()
    dft_pair = subgrid_tables()
    gathered = lax.all_gather(correlations, "pol", axis=1, tiled=True)
    corr_float = gathered.astype(jnp.float32)
    select = (jnp.arange(4, dtype=jnp.int32) == stokes_index).astype(jnp.float32)
    coef_re = jnp.sum(select[:, None] * jnp.asarray(COEF_REAL), axis=0)
    coef_im = jnp.sum(select[:, None] * jnp.asarray(COEF_IMAG), axis=0)
    stokes_re = jnp.einsum("p,pnv->nv", coef_re, corr_float[0], precision=highest) - jnp.einsum(
        "p,pnv->nv", coef_im, corr_float[1], precision=highest
    )
    stokes_im = jnp.einsum("p,pnv->nv", coef_re, corr_float[1], precision=highest) + jnp.einsum(
        "p,pnv->nv", coef_im, corr_float[0], precision=highest
    )
    visible = (jnp.arange(VIS, dtype=jnp.int32)[None, :] < vis_counts[:, None]).astype(jnp.bfloat16)
    stokes_vis = jnp.stack([stokes_re, stokes_im]).astype(jnp.bfloat16) * visible[None]
    holder_ids = jnp.arange(slab_count, dtype=jnp.int32)
    own_held = jnp.sum(jnp.where(holder_ids == slab_index, held_counts, 0))

    def grid_range(vis_set, track_set, first_slot, stop_slot, capacity):

        def one_slot(slot_index, subgrid_set):
            phasor = phasor_table(
                lax.dynamic_index_in_dim(track_set, slot_index, 1, keepdims=False), tables
            )
            vis_slot = lax.dynamic_index_in_dim(vis_set, slot_index, 1, keepdims=False)
            product = jnp.dot(vis_slot, phasor, preferred_element_type=jnp.float32)
            sub_re = product[0, :pixel_area] - product[1, pixel_area:]
            sub_im = product[0, pixel_area:] + product[1, :pixel_area]
            update = jnp.stack([sub_re, sub_im])[:, None, :]
            return lax.dynamic_update_slice_in_dim(subgrid_set, update, slot_index, 1)

        zero_set = jnp.zeros((2, capacity, pixel_area), jnp.float32)
        return lax.fori_loop(first_slot, stop_slot, one_slot, zero_set)

    half_slots = SLOTS // 2
    swap_bit = slab_count.bit_length() - 2
    partner = jnp.bitwise_xor(slab_index, slab_count // 2)
    partner_held = jnp.sum(jnp.where(holder_ids == partner, held_counts, 0))
    pair_total = own_held + partner_held
    own_give = jnp.maximum(own_held - (pair_total + 1) // 2, 0)
    partner_give = jnp.maximum(partner_held - (pair_total + 1) // 2, 0)
    own_start = jnp.minimum(own_held - own_give, SLOTS - half_slots)
    partner_start = jnp.minimum(partner_held - partner_give, SLOTS - half_slots)
    send_vis = lax.dynamic_slice_in_dim(stokes_vis, own_start, half_slots, 1).astype(jnp.float32)
    send_track = lax.dynamic_slice_in_dim(tracks, own_start, half_slots, 1)
    got_vis, got_track = partner_2((send_vis, send_track), "slab", swap_bit)
    first_slot = partner_held - partner_give - partner_start
    helped = grid_range(
        got_vis.astype(jnp.bfloat16), got_track, first_slot, first_slot + partner_give, half_slots
    )
    returned_set = partner_2(helped, "slab", swap_bit)
    own_part = grid_range(stokes_vis, tracks, 0, own_held - own_give, SLOTS)
    subgrids = own_part + lax.dynamic_update_slice_in_dim(
        jnp.zeros_like(own_part), returned_set, own_start, 1
    )
    weight_flat = pixel_weight.reshape(pixel_area)
    sub_re = (subgrids[0] * weight_flat).reshape(SLOTS, SUB, SUB)
    sub_im = (subgrids[1] * weight_flat).reshape(SLOTS, SUB, SUB)
    uv_re, uv_im = subgrid_transform(sub_re, sub_im, dft_pair)
    uv_blocks = jnp.stack([uv_re, uv_im])
    own_offsets = lax.dynamic_slice_in_dim(offsets, slab_index * SLOTS, SLOTS, 1)
    own_rows = own_offsets[0] - slab_index * rows_local
    own_cols = own_offsets[1]
    window = jnp.zeros((2, rows_local + SUB, G), jnp.float32)
    window = place_blocks(window, uv_blocks, own_rows, own_cols)
    lower_rows = passed_along(window[:, rows_local:], "slab", 1)
    slab_grid = window[:, :rows_local].at[:, :SUB].add(lower_rows)
    small_side = G // 128
    large_side = 128
    table_small = dft_table(small_side)
    table_large = dft_table(large_side)
    twiddle = twiddle_table(small_side, large_side, G)
    plane_re = slab_grid[0].reshape(rows_local, small_side, large_side)
    plane_im = slab_grid[1].reshape(rows_local, small_side, large_side)
    step_re, step_im = complex_einsum("rkc,kx->rxc", (plane_re, plane_im), table_small)
    step_re, step_im = complex_multiply((step_re, step_im), twiddle)
    step_re, step_im = complex_einsum("rxc,cb->bxr", (step_re, step_im), table_large)
    moved_block = lax.all_to_all(
        jnp.stack([step_re, step_im]), "slab", split_axis=1, concat_axis=3, tiled=True
    )
    line_re = moved_block[0].reshape(rows_local, large_side, small_side)
    line_im = moved_block[1].reshape(rows_local, large_side, small_side)
    line_re, line_im = complex_einsum("xab,ay->xby", (line_re, line_im), table_large)
    line_re, line_im = complex_multiply((line_re, line_im), twiddle)
    line_re, line_im = complex_einsum("xby,bz->xzy", (line_re, line_im), table_small)
    norm_scale = 1.0 / (SUB * SUB * math.sqrt(VIS * SLOTS * slab_count / 8.0))
    sky_re = line_re.reshape(rows_local, G) * norm_scale
    sky_im = line_im.reshape(rows_local, G) * norm_scale
    return jnp.stack([sky_re, sky_im])[:, None]


LANES = 128
GROUP = 8


def turn_polynomials():
    z = np.cos(np.linspace(0.0, np.pi, 4001)) * 0.125 + 0.125
    r = np.sqrt(z)
    sine = np.where(r > 0, np.sin(np.pi * r) / np.where(r > 0, r, 1.0), np.pi)
    fits = []
    for values in (sine, np.cos(np.pi * r)):
        fit = np.polynomial.chebyshev.Chebyshev.fit(z, values, 4, domain=[0.0, 0.25])
        fits.append([float(v) for v in fit.convert(kind=np.polynomial.Polynomial).coef])
    return fits


SINE_COEF, COSINE_COEF = turn_polynomials()


def cos_sin_turns(turns):
    rest = turns - jnp.floor(turns + 0.5)
    square = rest * rest
    sine = SINE_COEF[-1]
    cosine = COSINE_COEF[-1]
    for coef in SINE_COEF[-2::-1]:
        sine = sine * square + coef
    for coef in COSINE_COEF[-2::-1]:
        cosine = cosine * square + coef
    sine = sine * rest
    double = sine + sine
    return 1.0 - double * sine, double * cosine


def times(left, right):
    return (left[0] * right[0] - left[1] * right[1], left[0] * right[1] + left[1] * right[0])


def plus(left, right):
    return (left[0] + right[0], left[1] + right[1])


def minus(left, right):
    return (left[0] - right[0], left[1] - right[1])


def quarter(value, sign):
    if sign > 0:
        return (-value[1], value[0])
    return (value[1], -value[0])


def dft_4(values, sign):
    a, b, c, d = values
    even_sum, even_diff = plus(a, c), minus(a, c)
    odd_sum, odd_diff = plus(b, d), quarter(minus(b, d), sign)
    return [plus(even_sum, odd_sum), plus(even_diff, odd_diff), minus(even_sum, odd_sum), minus(even_diff, odd_diff)]


ROOT_HALF = math.sqrt(0.5)


def dft_8(values, sign):
    even = dft_4(values[0::2], sign)
    odd = dft_4(values[1::2], sign)
    a, b = odd[1]
    odd[1] = ((a - b) * ROOT_HALF, (a + b) * ROOT_HALF) if sign > 0 else ((a + b) * ROOT_HALF, (b - a) * ROOT_HALF)
    odd[2] = quarter(odd[2], sign)
    a, b = odd[3]
    odd[3] = ((-a - b) * ROOT_HALF, (a - b) * ROOT_HALF) if sign > 0 else ((b - a) * ROOT_HALF, (-a - b) * ROOT_HALF)
    return [plus(e, o) for e, o in zip(even, odd)] + [minus(e, o) for e, o in zip(even, odd)]


def pixel_rows():
    row, col = np.divmod(np.arange(SUB * SUB), SUB)
    l = ((col - SUB // 2) / SUB).astype(np.float32)
    m = ((row - SUB // 2) / SUB).astype(np.float32)
    view = np.float32(FIELD_VIEW)
    n = (np.sqrt(np.float32(1.0) - (view * l) ** 2 - (view * m) ** 2) - np.float32(1.0)).astype(np.float32)
    return np.stack([l, m, n, row.astype(np.float32)] + [np.zeros_like(l)] * 4).astype(np.float32)


HALVES = VIS // LANES
WAVES = 2
TRACK_ROWS = WAVES * 3 * HALVES


def pack_kernel(held_ref, place_ref, counts_ref, corr_ref, track_ref, out_ref):
    devices = out_ref.shape[0]
    slab, pol = place_ref[0], place_ref[1]

    def count_before(holder, total):
        return total + jnp.where(holder < slab, held_ref[holder], 0)

    shift = jnp.bitwise_and(lax.fori_loop(0, held_ref.shape[0], count_before, 0), devices - 1)
    counts = jnp.transpose(jnp.broadcast_to(counts_ref[...].astype(jnp.float32), (LANES, counts_ref.shape[1])))
    lane = lax.broadcasted_iota(jnp.int32, (devices, LANES), 1).astype(jnp.float32)
    rows = []
    for wave in range(WAVES):
        at = pl.ds(wave * devices, devices)
        for c in range(2):
            for half in range(HALVES):
                value = corr_ref[c, at, pl.ds(half * LANES, LANES)].astype(jnp.float32)
                limit = counts[wave * devices : (wave + 1) * devices] - float(half * LANES)
                rows.append(jnp.where(lane < limit, value, 0.0))
    piece = TRACK_ROWS // 4
    for row in range(piece):
        value = None
        for sender in range(4):
            wave, axis, half = np.unravel_index(sender * piece + row, (WAVES, 3, HALVES))
            part = track_ref[int(axis), pl.ds(int(wave) * devices, devices), pl.ds(int(half) * LANES, LANES)]
            value = part if value is None else jnp.where(pol == sender, part, value)
        rows.append(value)
    for row, value in enumerate(rows):
        out_ref[:, row, :] = pltpu.roll(value, shift, 0)
    for row in range(len(rows), out_ref.shape[1]):
        out_ref[:, row, :] = jnp.zeros((devices, LANES), jnp.float32)


def packed(held, place, counts, corr, tracks, devices):
    smem = pl.BlockSpec(memory_space=pltpu.SMEM)
    vmem = pl.BlockSpec(memory_space=pltpu.VMEM)
    return pl.pallas_call(
        pack_kernel,
        out_shape=jax.ShapeDtypeStruct((devices, 16, LANES), jnp.float32),
        in_specs=[smem, smem, vmem, vmem, vmem],
        out_specs=vmem,
        name="packed",
    )(held, place, counts, corr, tracks)


def row_twiddles():
    angle = -2.0 * np.pi * np.arange(8)[:, None] * (np.arange(LANES)[None, :] // SUB) / SUB
    return np.concatenate([np.cos(angle), np.sin(angle)], axis=0).astype(np.float32)


def subgrid_kernel(held_counts_ref, place_ref, offsets_ref, slots_ref, table_ref, twiddle_ref, weight_ref, *refs):
    piece_refs, more_ref, held_ref = refs[:4], refs[4], refs[5]
    held_ref[...] = jnp.zeros_like(held_ref)
    slab, pol = place_ref[0], place_ref[1]
    slabs = slots_ref.shape[0] // 4
    devices = slots_ref.shape[0]
    own = pol * slabs + slab
    total = lax.fori_loop(0, slabs, lambda holder, value: value + held_counts_ref[holder], 0)
    count = lax.shift_right_logical(total - own + (devices - 1), devices.bit_length() - 1)

    def locate(index):
        wanted = index * devices + own

        def look(holder, found):
            before, at_holder, at_slot = found
            after = before + held_counts_ref[holder]
            inside = (wanted >= before) & (wanted < after)
            return after, jnp.where(inside, holder, at_holder), jnp.where(inside, wanted - before, at_slot)

        _, at_holder, at_slot = lax.fori_loop(0, slabs, look, (0, 0, 0))
        return at_holder, at_slot

    def one_slot(index, carry):
        holder, slot = locate(index)
        early = slot < devices
        row_start = jnp.bitwise_and(offsets_ref[0, holder * SLOTS + slot], SUB - 1).astype(jnp.float32)
        tiles = [slots_ref[p * slabs + holder] for p in range(4)]
        xx, xy, yx, yy = [0.5 * jnp.where(early, tile[0:4], tile[4:8]) for tile in tiles]
        turned = xy - yx
        parameters = [xx + yy, xx - yy, xy + yx, jnp.concatenate([turned[2:4], -turned[0:2]], axis=0)]
        chosen = []
        for k in range(4):
            value = parameters[k]
            for other in range(1, 4):
                value = jnp.where(pol == other, parameters[k ^ other], value)
            chosen.append(value)
        halves = [
            jnp.concatenate([chosen[k][2 * c + half : 2 * c + half + 1] for c in range(2) for k in range(4)], axis=0)
            for half in range(2)
        ]
        vis = jnp.concatenate(halves, axis=1).astype(jnp.bfloat16)

        def track_half(axis, half):
            found = []
            for wave in range(WAVES):
                sender, row = divmod((wave * 3 + axis) * HALVES + half, TRACK_ROWS // 4)
                found.append(tiles[sender][8 + row : 9 + row])
            return jnp.where(early, found[0], found[1])

        track = jnp.concatenate(
            [jnp.concatenate([track_half(axis, half) for half in range(2)], axis=1) for axis in (0, 1, 2, 2, 2, 2, 2, 2)], axis=0
        )
        track = jnp.transpose(track)
        shape = (VIS, LANES)
        u = jnp.broadcast_to(track[:, 0:1] * (TRACK_SCALE * SUB), shape)
        v = jnp.broadcast_to(track[:, 1:2] * (TRACK_SCALE * SUB), shape)
        w = jnp.broadcast_to(track[:, 2:3] * DEPTH_SCALE, shape)
        placed = []
        for tile in range(SUB * SUB // LANES):
            lanes = pl.ds(tile * LANES, LANES)
            turns = u * table_ref[0:1, lanes] + v * table_ref[1:2, lanes] + w * table_ref[2:3, lanes]
            cosine, sine = cos_sin_turns(turns)
            phasor = jnp.concatenate([cosine.astype(jnp.bfloat16), sine.astype(jnp.bfloat16)], axis=1)
            product = jnp.dot(vis, phasor, preferred_element_type=jnp.float32)
            real = product[:4, :LANES] - product[4:, LANES:]
            imag = product[:4, LANES:] + product[4:, :LANES]
            weight = weight_ref[0:1, lanes]
            pixel_row = table_ref[3:4, lanes]
            turn = (row_start * (pixel_row - SUB // 2) + pixel_row * (SUB // 2)) * (1.0 / SUB)
            turn_re, turn_im = cos_sin_turns(turn)
            turn_re, turn_im = turn_re * weight, turn_im * weight
            placed.append(times((real, imag), (turn_re, turn_im)))
        for rho, value in enumerate(dft_8(placed, -1)):
            if rho:
                value = times(value, (twiddle_ref[rho : rho + 1], twiddle_ref[8 + rho : 9 + rho]))
            held_ref[index, :, pl.ds(2 * rho * LANES, LANES)] = value[0]
            held_ref[index, :, pl.ds((2 * rho + 1) * LANES, LANES)] = value[1]
        return carry

    lax.fori_loop(0, count, one_slot, 0)
    for k in range(4):
        piece_refs[k][...] = held_ref[:GROUP, k, :].astype(jnp.bfloat16)
        more_ref[k] = held_ref[GROUP:, k, :].astype(jnp.bfloat16)


def subgrids_of(held, place, offsets, slots, weight_row, capacity):
    smem = pl.BlockSpec(memory_space=pltpu.SMEM)
    vmem = pl.BlockSpec(memory_space=pltpu.VMEM)
    return pl.pallas_call(
        subgrid_kernel,
        out_shape=[jax.ShapeDtypeStruct((GROUP, 2 * SUB * SUB), jnp.bfloat16)] * 4
        + [jax.ShapeDtypeStruct((4, capacity - GROUP, 2 * SUB * SUB), jnp.bfloat16)],
        in_specs=[smem] * 3 + [vmem] * 4,
        out_specs=[vmem] * 5,
        scratch_shapes=[pltpu.VMEM((capacity, 4, 2 * SUB * SUB), jnp.float32)],
        name="subgrids",
    )(held, place, offsets, slots, jnp.asarray(pixel_rows()), jnp.asarray(row_twiddles()), weight_row)


def image_kernel(pol_step, x_block, slabs, groups_ref, base_ref, row_ref, col_ref, mix_ref, twist_ref, *refs):
    first_refs, more_ref, sky_ref = refs[:slabs], refs[slabs], refs[slabs + 1]
    bundle_ref, phase_ref, col_phase_ref, *half_refs, moved_ref, sum_ref, stage_ref, out_ref = refs[slabs + 2 : -3]
    later_ref, sem_ref, later_sem_ref = refs[-3:]
    x_blocks = sky_ref.shape[1] // x_block
    groups = groups_ref[0]
    lane_index = lax.broadcasted_iota(jnp.int32, (LANES, LANES), 1)
    eighth = SUB // 4
    out_rows = out_ref.shape[2]
    out_steps = x_block // out_rows
    group_chunks = 4 // pol_step
    depth = 2 * LANES

    def load_phases(group, part):
        chunk = group * group_chunks + part
        rows = jnp.transpose(jnp.broadcast_to(row_ref[pl.ds(chunk, 1), :].astype(jnp.float32), (LANES, LANES)))
        rows = rows.astype(jnp.int32)
        high = lax.shift_right_logical(rows, 5)
        low = jnp.bitwise_and(rows, SUB - 1)
        here = cos_sin_turns(jnp.bitwise_and(high * lane_index, LANES - 1).astype(jnp.float32) * (1.0 / LANES))
        later = cos_sin_turns(jnp.bitwise_and((high + 1) * lane_index, LANES - 1).astype(jnp.float32) * (1.0 / LANES))
        re_rows = pl.ds(part * depth, LANES)
        im_rows = pl.ds(part * depth + LANES, LANES)

        def one_phase(residue, inner):
            carried = low > residue
            twist = (twist_ref[pl.ds(2 * residue, 1)], twist_ref[pl.ds(2 * residue + 1, 1)])
            re, im = times((jnp.where(carried, later[0], here[0]), jnp.where(carried, later[1], here[1])), twist)
            re = re.astype(jnp.bfloat16)
            phase_ref[residue, re_rows, :LANES] = re
            phase_ref[residue, re_rows, LANES:] = im.astype(jnp.bfloat16)
            phase_ref[residue, im_rows, :LANES] = (-im).astype(jnp.bfloat16)
            phase_ref[residue, im_rows, LANES:] = re
            return inner

        lax.fori_loop(0, SUB, one_phase, 0)

    def move_rows(group, part, block):
        chunk = group * group_chunks + part
        cols = col_ref[pl.ds(chunk, 1), :]
        x_index = lax.broadcasted_iota(jnp.int32, (x_block, LANES), 0) + (base_ref[0] + block * x_block)
        turns = jnp.bitwise_and(x_index * cols, G - 1).astype(jnp.float32) * (1.0 / G)
        turn_re, turn_im = cos_sin_turns(turns)
        col_phase_ref[0] = turn_re
        col_phase_ref[1] = turn_im
        re_lanes = pl.ds(pl.multiple_of(part * depth, LANES), LANES)
        im_lanes = pl.ds(pl.multiple_of(part * depth + LANES, LANES), LANES)

        def mix_pair(pair, half_ref):
            wide = jnp.concatenate(
                [
                    bundle_ref[part, :, pl.ds(4 * pair * LANES, depth)],
                    bundle_ref[part, :, pl.ds((4 * pair + 2) * LANES, depth)],
                ],
                axis=0,
            )
            for side in range(2):
                half_ref[side] = lax.dot_general(
                    mix_ref[block, side], wide, (((1,), (1,)), ((), ())), preferred_element_type=jnp.float32
                )

        def turn_pair(pair, half_ref):
            for tile in range(x_block // 16):
                rows_at = pl.ds(tile * 16, 16)
                turn = (col_phase_ref[0, rows_at], col_phase_ref[1, rows_at])
                for low in range(2):
                    at = pl.ds(low * LANES, LANES)
                    for high in range(4):
                        tile_rows = pl.ds(high * x_block + tile * 16, 16)
                        re, im = times((half_ref[0, tile_rows, at], half_ref[1, tile_rows, at]), turn)
                        residue = 2 * pair + low + 8 * high
                        moved_ref[residue, rows_at, re_lanes] = re.astype(jnp.bfloat16)
                        moved_ref[residue, rows_at, im_lanes] = im.astype(jnp.bfloat16)

        halves = half_refs
        mix_pair(0, halves[0])
        for pair in range(1, eighth // 2):
            mix_pair(pair, halves[pair % 2])
            turn_pair(pair - 1, halves[(pair - 1) % 2])
        turn_pair(eighth // 2 - 1, halves[(eighth // 2 - 1) % 2])

    def load_group(group):
        @pl.when(group > 0)
        def _():
            copy = pltpu.make_async_copy(more_ref, later_ref, later_sem_ref)
            copy.start()
            copy.wait()

        for part in range(group_chunks):
            polarized = pl.ds(part * pol_step, pol_step)
            span = pol_step * GROUP
            for peer in range(slabs):
                rows_at = pl.ds(peer * span, span)

                @pl.when(group == 0)
                def _(part=part, polarized=polarized, peer=peer, rows_at=rows_at):
                    bundle_ref[part, rows_at] = first_refs[peer][polarized].reshape(span, -1)

                @pl.when(group > 0)
                def _(part=part, polarized=polarized, peer=peer, rows_at=rows_at):
                    bundle_ref[part, rows_at] = later_ref[peer, polarized].reshape(span, -1)

            load_phases(group, part)

    def copy_out(block, step):
        x_at = pl.ds(pl.multiple_of(block * x_block + step * out_rows, 8), out_rows)
        return pltpu.make_async_copy(out_ref.at[step], sky_ref.at[:, x_at], sem_ref.at[step])

    def one_block(block, carry):
        def one_group(group, inner):
            @pl.when((block == 0) | (groups > 1))
            def _():
                load_group(group)

            def one_part(part, innermost):
                move_rows(group, part, block)
                return innermost

            lax.fori_loop(0, group_chunks, one_part, 0)

            @pl.when(group == 0)
            def _():
                def one_residue(residue, innermost):
                    sum_ref[residue] = jnp.dot(
                        moved_ref[residue], phase_ref[residue], preferred_element_type=jnp.float32
                    )
                    return innermost

                lax.fori_loop(0, SUB, one_residue, 0, unroll=16)

            @pl.when(group > 0)
            def _():
                def one_residue(residue, innermost):
                    sum_ref[residue] += jnp.dot(
                        moved_ref[residue], phase_ref[residue], preferred_element_type=jnp.float32
                    )
                    return innermost

                lax.fori_loop(0, SUB, one_residue, 0)

            return inner

        lax.fori_loop(0, groups, one_group, 0)

        def one_step(step, inner):
            @pl.when(block > 0)
            def _():
                copy_out(block - 1, step).wait()

            def one_tile(tile, innermost):
                rows_at = pl.ds(pl.multiple_of(step * out_rows + tile * 8, 8), 8)
                for second in range(4):
                    parts = []
                    for first in range(8):
                        residue = 4 * first + second
                        parts.append((sum_ref[residue, rows_at, :LANES], sum_ref[residue, rows_at, LANES:]))
                    for first, value in enumerate(dft_8(parts, 1)):
                        if first * second:
                            angle = TWO_PI * first * second / SUB
                            value = times(value, (math.cos(angle), math.sin(angle)))
                        stage_ref[second, first, 0] = value[0]
                        stage_ref[second, first, 1] = value[1]
                to_rows = pl.ds(pl.multiple_of(tile * 8, 8), 8)
                for first in range(8):
                    parts = [(stage_ref[second, first, 0], stage_ref[second, first, 1]) for second in range(4)]
                    for second, value in enumerate(dft_4(parts, 1)):
                        lanes = pl.ds((first + 8 * second) * LANES, LANES)
                        out_ref[step, 0, to_rows, lanes] = value[0]
                        out_ref[step, 1, to_rows, lanes] = value[1]
                return innermost

            lax.fori_loop(0, out_rows // 8, one_tile, 0)
            copy_out(block, step).start()
            return inner

        lax.fori_loop(0, out_steps, one_step, 0)
        return carry

    lax.fori_loop(0, x_blocks, one_block, 0)
    for step in range(out_steps):
        copy_out(x_blocks - 1, step).wait()


def twist_table(scale):
    residue = np.arange(SUB)[:, None]
    lane = np.arange(LANES)[None, :]
    angle = 2.0 * np.pi * (residue * lane % G) / G
    sign = np.where(residue % 2 == 0, scale, -scale)
    return np.stack([sign * np.cos(angle), sign * np.sin(angle)], axis=1).reshape(2 * SUB, LANES).astype(np.float32)


def mix_kernel(base_ref, sub_ref, turn_ref, mix_ref):
    x_block = mix_ref.shape[2] // 4
    highest = lax.Precision.HIGHEST
    cell = lax.broadcasted_iota(jnp.int32, (x_block, LANES), 1)

    def one_block(block, carry):
        x_index = lax.broadcasted_iota(jnp.int32, (x_block, LANES), 0) + (base_ref[0] + block * x_block)
        line_re, line_im = cos_sin_turns(jnp.bitwise_and(x_index * cell, G - 1).astype(jnp.float32) * (1.0 / G))
        by_re = jnp.dot(line_re, sub_ref[...], precision=highest, preferred_element_type=jnp.float32)
        by_im = jnp.dot(line_im, sub_ref[...], precision=highest, preferred_element_type=jnp.float32)
        core = (by_re[:, :LANES] - by_im[:, LANES:], by_re[:, LANES:] + by_im[:, :LANES])
        for rho in range(4):
            re, im = times(core, (turn_ref[rho : rho + 1], turn_ref[4 + rho : 5 + rho]))
            rows_at = pl.ds(rho * x_block, x_block)
            mix_ref[block, 0, rows_at, :LANES] = re.astype(jnp.bfloat16)
            mix_ref[block, 0, rows_at, LANES:] = (-im).astype(jnp.bfloat16)
            mix_ref[block, 1, rows_at, :LANES] = im.astype(jnp.bfloat16)
            mix_ref[block, 1, rows_at, LANES:] = re.astype(jnp.bfloat16)
        return carry

    lax.fori_loop(0, mix_ref.shape[0], one_block, 0)


def mix_table(x_base, x_count, x_block):
    cells, pixels = np.arange(LANES)[:, None], np.arange(LANES)[None, :] % SUB
    angle = -2.0 * np.pi * ((cells - SUB // 2) * (pixels - SUB // 2) % SUB) / SUB
    used = cells < SUB
    sub = np.concatenate([np.where(used, np.cos(angle), 0.0), np.where(used, np.sin(angle), 0.0)], axis=1)
    turn = (np.arange(4)[:, None] * (np.arange(LANES)[None, :] // SUB)) % 4
    turns = np.concatenate([np.array([1.0, 0.0, -1.0, 0.0])[turn], np.array([0.0, -1.0, 0.0, 1.0])[turn]])
    smem = pl.BlockSpec(memory_space=pltpu.SMEM)
    vmem = pl.BlockSpec(memory_space=pltpu.VMEM)
    return pl.pallas_call(
        mix_kernel,
        out_shape=jax.ShapeDtypeStruct((x_count // x_block, 2, 4 * x_block, 2 * LANES), jnp.bfloat16),
        in_specs=[smem, vmem, vmem],
        out_specs=vmem,
        cost_estimate=pl.CostEstimate(flops=1 << 30, bytes_accessed=1 << 22, transcendentals=0),
        name="mix",
    )(x_base, jnp.asarray(sub, jnp.float32), jnp.asarray(turns, jnp.float32))


def image_of(groups, x_base, first, more, rows, cols, mix, x_count, x_block, scale, pol_step):
    out_rows = min(x_block, 64)
    parts = 4 // pol_step
    slabs = len(first)
    smem = pl.BlockSpec(memory_space=pltpu.SMEM)
    vmem = pl.BlockSpec(memory_space=pltpu.VMEM)
    hbm = pl.BlockSpec(memory_space=pl.ANY)
    return pl.pallas_call(
        functools.partial(image_kernel, pol_step, x_block, slabs),
        out_shape=jax.ShapeDtypeStruct((2, x_count, G), jnp.float32),
        in_specs=[smem, smem] + [vmem] * (4 + slabs) + [hbm],
        out_specs=hbm,
        scratch_shapes=[
            pltpu.VMEM((parts, LANES, 2 * SUB * SUB), jnp.bfloat16),
            pltpu.VMEM((SUB, parts * 2 * LANES, 2 * LANES), jnp.bfloat16),
            pltpu.VMEM((2, x_block, LANES), jnp.float32),
            pltpu.VMEM((2, 4 * x_block, 2 * LANES), jnp.float32),
            pltpu.VMEM((2, 4 * x_block, 2 * LANES), jnp.float32),
            pltpu.VMEM((SUB, x_block, parts * 2 * LANES), jnp.bfloat16),
            pltpu.VMEM((SUB, x_block, 2 * LANES), jnp.float32),
            pltpu.VMEM((4, 8, 2, 8, LANES), jnp.float32),
            pltpu.VMEM((x_block // out_rows, 2, out_rows, G), jnp.float32),
            pltpu.VMEM(more.shape, more.dtype),
            pltpu.SemaphoreType.DMA((x_block // out_rows,)),
            pltpu.SemaphoreType.DMA,
        ],
        compiler_params=pltpu.CompilerParams(vmem_limit_bytes=46 * 1024 * 1024),
        name="image",
    )(groups, x_base, rows, cols, mix, jnp.asarray(twist_table(scale)), *first, more)


def exchanged(value, axis, distance):
    peers = lax.axis_size(axis)
    return lax.ppermute(value, axis, [(i, i ^ distance) for i in range(peers)])


def gathered(pieces, beside=None):
    slabs = lax.axis_size("slab")
    value = jnp.stack([pieces[0]] + [exchanged(piece, "pol", k) for k, piece in enumerate(pieces) if k])
    planes = [value] + [exchanged(value, "slab", k) for k in range(2, slabs, 2)]
    made = None
    if beside is not None:
        made = beside(value)
        planes[-1], made = lax.optimization_barrier((planes[-1], made))
    values = []
    for plane in planes:
        values += [plane, exchanged(plane, "slab", 1)]
    return values, made


def in_image_domain(correlations, tracks, vis_counts, offsets, held_counts, pixel_weight):
    pols, slabs = lax.axis_size("pol"), lax.axis_size("slab")
    pol, slab = lax.axis_index("pol"), lax.axis_index("slab")
    devices = pols * slabs
    capacity = SLOTS * slabs // devices
    x_count = G // slabs
    held = held_counts.astype(jnp.int32)
    holders = jnp.arange(slabs, dtype=jnp.int32)
    where_at = jnp.stack([slab, pol]).astype(jnp.int32)
    sent = packed(held, where_at, vis_counts.reshape(1, SLOTS), correlations[:, 0], tracks, devices)
    slots = lax.all_to_all(sent, ("pol", "slab"), 0, 0, tiled=True)
    held, _ = lax.optimization_barrier((held, sent))
    before = jnp.sum(jnp.where(holders[None, :] < holders[:, None], held[None, :], 0), axis=1)
    total = jnp.sum(held)

    slot = jnp.arange(SLOTS, dtype=jnp.int32)
    order = jnp.where(slot[None, :] < held[:, None], before[:, None] + slot[None, :], -1).reshape(-1)
    device_at, seat_at = order % devices, order // devices
    pol_step = LANES // (GROUP * slabs)
    lane_order = (device_at % slabs) ^ slab
    pol_order = (device_at // slabs) ^ pol
    place = (seat_at // GROUP) * (pols // pol_step) + pol_order // pol_step
    place = place * LANES + lane_order * (pol_step * GROUP) + pol_order % pol_step * GROUP + seat_at % GROUP
    place = jnp.where(order >= 0, place, -1)
    chunk_count = capacity // GROUP * (pols // pol_step)
    spots = jnp.arange(chunk_count * LANES, dtype=jnp.int32)
    chosen = spots[:, None] == place[None, :]
    rows = jnp.sum(jnp.where(chosen, offsets[0][None, :], 0), axis=1).reshape(chunk_count, LANES)
    cols = jnp.sum(jnp.where(chosen, offsets[1][None, :], 0), axis=1).reshape(chunk_count, LANES)
    slots, rows, cols = lax.optimization_barrier((slots, rows, cols))
    weight_row = pixel_weight.reshape(1, SUB * SUB)
    *pieces, extra = subgrids_of(held, where_at, offsets.astype(jnp.int32), slots, weight_row, capacity)
    norm_scale = 1.0 / (SUB * SUB * math.sqrt(VIS * SLOTS * slabs / 8.0))
    x_base = (slab * x_count).reshape(1)
    x_block = min(x_count, 256)

    def mixed(after):
        base, _ = lax.optimization_barrier((x_base, after))
        return mix_table(base, x_count, x_block)

    first, mix = gathered(pieces, mixed)
    many = total > devices * GROUP
    more = lax.cond(
        many,
        lambda: jnp.stack(gathered([extra[k] for k in range(pols)])[0]),
        lambda: jnp.zeros((slabs,) + extra.shape, extra.dtype),
    )
    groups = jnp.where(many, capacity // GROUP, 1).reshape(1)
    sky = image_of(groups, x_base, first, more, rows, cols, mix, x_count, x_block, norm_scale, pol_step)
    return sky[:, None]


def fits_image_domain(mesh):
    pols, slabs = mesh.shape["pol"], mesh.shape["slab"]
    devices = pols * slabs
    whole = slabs & (slabs - 1) == 0 and slabs * GROUP <= LANES and SLOTS * slabs == 2 * GROUP * devices
    return whole and pols == 4 and SLOTS == WAVES * devices and pols % (LANES // (GROUP * slabs)) == 0


def solution(mesh):
    in_specs = (P(None, "pol", "slab", None), P(None, "slab", None), P("slab"), P(), P(), P())
    out_specs = P(None, "pol", "slab", None)
    body = in_image_domain if fits_image_domain(mesh) else on_device
    return jax.shard_map(body, mesh=mesh, in_specs=in_specs, out_specs=out_specs, check_vma=False)
```

```python
import functools
import math

import jax
import jax.numpy as jnp
import numpy as np
from jax import lax
from jax.experimental import pallas as pl
from jax.experimental.pallas import tpu as pltpu
from jax.sharding import PartitionSpec as P

G = 4096
SUB = 32
VIS = 256
SLOTS = 64


TWO_PI = 2.0 * math.pi
FIELD_VIEW = 0.6
DEPTH_SCALE = 40.0
TRACK_SCALE = 0.375
COEF_REAL = np.array(
    [[0.5, 0.0, 0.0, 0.5], [0.5, 0.0, 0.0, -0.5], [0.0, 0.5, 0.5, 0.0], [0.0, 0.0, 0.0, 0.0]],
    np.float32,
)
COEF_IMAG = np.array(
    [[0.0, 0.0, 0.0, 0.0], [0.0, 0.0, 0.0, 0.0], [0.0, 0.0, 0.0, 0.0], [0.0, -0.5, 0.5, 0.0]],
    np.float32,
)


def partner_2(value, axis, distance):
    return lax.ppermute(value, axis, [(i, i ^ 1 << distance) for i in range(lax.axis_size(axis))])


def passed_along(value, axis, by):
    peers = lax.axis_size(axis)
    pairs = [(i, i + by) for i in range(peers) if 0 <= i + by < peers]
    return lax.ppermute(value, axis, pairs)


def pixel_tables():
    cells = jnp.arange(SUB * SUB, dtype=jnp.int32)
    row_pos = (cells // SUB - SUB // 2).astype(jnp.float32) / SUB
    col_pos = (cells % SUB - SUB // 2).astype(jnp.float32) / SUB
    depth = jnp.sqrt(1.0 - (FIELD_VIEW * col_pos) ** 2 - (FIELD_VIEW * row_pos) ** 2) - 1.0
    return (col_pos, row_pos, depth)


def phasor_table(track_set, tables):
    col_pos, row_pos, depth = tables
    u_cells = track_set[0] * (TRACK_SCALE * SUB)
    v_cells = track_set[1] * (TRACK_SCALE * SUB)
    w_cells = track_set[2] * DEPTH_SCALE
    phase = TWO_PI * (
        u_cells[:, None] * col_pos[None, :]
        + v_cells[:, None] * row_pos[None, :]
        + w_cells[:, None] * depth[None, :]
    )
    return jnp.concatenate([jnp.cos(phase), jnp.sin(phase)], axis=1).astype(jnp.bfloat16)


def subgrid_tables():
    positions = jnp.arange(SUB, dtype=jnp.int32) - SUB // 2
    turn_count = positions[:, None] * positions[None, :] % SUB
    angles = -TWO_PI * turn_count.astype(jnp.float32) / SUB
    return (jnp.cos(angles), jnp.sin(angles))


def dft_table(length):
    positions = jnp.arange(length, dtype=jnp.int32)
    turn_count = positions[:, None] * positions[None, :] % length
    angles = TWO_PI * turn_count.astype(jnp.float32) / length
    return (jnp.cos(angles), jnp.sin(angles))


def twiddle_table(first_len, second_len, length):
    first_pos = jnp.arange(first_len, dtype=jnp.int32)
    second_pos = jnp.arange(second_len, dtype=jnp.int32)
    turn_count = first_pos[:, None] * second_pos[None, :] % length
    angles = TWO_PI * turn_count.astype(jnp.float32) / length
    return (jnp.cos(angles), jnp.sin(angles))


def complex_einsum(pattern, left_pair, right_pair):
    highest = lax.Precision.HIGHEST
    left_re, left_im = left_pair
    right_re, right_im = right_pair
    real_part = jnp.einsum(pattern, left_re, right_re, precision=highest) - jnp.einsum(
        pattern, left_im, right_im, precision=highest
    )
    imag_part = jnp.einsum(pattern, left_re, right_im, precision=highest) + jnp.einsum(
        pattern, left_im, right_re, precision=highest
    )
    return (real_part, imag_part)


def complex_multiply(data_pair, table_pair):
    data_re, data_im = data_pair
    table_re, table_im = table_pair
    return (data_re * table_re - data_im * table_im, data_re * table_im + data_im * table_re)


def subgrid_transform(sub_re, sub_im, dft_pair):
    half_re, half_im = complex_einsum("...ij,cj->...ic", (sub_re, sub_im), dft_pair)
    return complex_einsum("ai,...ic->...ac", dft_pair, (half_re, half_im))


def place_blocks(window, blocks, row_starts, col_starts):
    block_count = blocks.shape[1]
    zero_index = jnp.zeros((), jnp.int32)

    def add_one(slot_index, current_window):
        block = lax.dynamic_index_in_dim(blocks, slot_index, 1, keepdims=False)
        corner = (zero_index, row_starts[slot_index], col_starts[slot_index])
        current = lax.dynamic_slice(current_window, corner, (2, SUB, SUB))
        return lax.dynamic_update_slice(current_window, current + block, corner)

    return lax.fori_loop(0, block_count, add_one, window)


def on_device(correlations, tracks, vis_counts, offsets, held_counts, pixel_weight):
    highest = lax.Precision.HIGHEST
    slab_count = lax.axis_size("slab")
    slab_index = lax.axis_index("slab")
    stokes_index = lax.axis_index("pol")
    pixel_area = SUB * SUB
    rows_local = G // slab_count
    tables = pixel_tables()
    dft_pair = subgrid_tables()
    gathered = lax.all_gather(correlations, "pol", axis=1, tiled=True)
    corr_float = gathered.astype(jnp.float32)
    select = (jnp.arange(4, dtype=jnp.int32) == stokes_index).astype(jnp.float32)
    coef_re = jnp.sum(select[:, None] * jnp.asarray(COEF_REAL), axis=0)
    coef_im = jnp.sum(select[:, None] * jnp.asarray(COEF_IMAG), axis=0)
    stokes_re = jnp.einsum("p,pnv->nv", coef_re, corr_float[0], precision=highest) - jnp.einsum(
        "p,pnv->nv", coef_im, corr_float[1], precision=highest
    )
    stokes_im = jnp.einsum("p,pnv->nv", coef_re, corr_float[1], precision=highest) + jnp.einsum(
        "p,pnv->nv", coef_im, corr_float[0], precision=highest
    )
    visible = (jnp.arange(VIS, dtype=jnp.int32)[None, :] < vis_counts[:, None]).astype(jnp.bfloat16)
    stokes_vis = jnp.stack([stokes_re, stokes_im]).astype(jnp.bfloat16) * visible[None]
    holder_ids = jnp.arange(slab_count, dtype=jnp.int32)
    own_held = jnp.sum(jnp.where(holder_ids == slab_index, held_counts, 0))

    def grid_range(vis_set, track_set, first_slot, stop_slot, capacity):

        def one_slot(slot_index, subgrid_set):
            phasor = phasor_table(
                lax.dynamic_index_in_dim(track_set, slot_index, 1, keepdims=False), tables
            )
            vis_slot = lax.dynamic_index_in_dim(vis_set, slot_index, 1, keepdims=False)
            product = jnp.dot(vis_slot, phasor, preferred_element_type=jnp.float32)
            sub_re = product[0, :pixel_area] - product[1, pixel_area:]
            sub_im = product[0, pixel_area:] + product[1, :pixel_area]
            update = jnp.stack([sub_re, sub_im])[:, None, :]
            return lax.dynamic_update_slice_in_dim(subgrid_set, update, slot_index, 1)

        zero_set = jnp.zeros((2, capacity, pixel_area), jnp.float32)
        return lax.fori_loop(first_slot, stop_slot, one_slot, zero_set)

    half_slots = SLOTS // 2
    swap_bit = slab_count.bit_length() - 2
    partner = jnp.bitwise_xor(slab_index, slab_count // 2)
    partner_held = jnp.sum(jnp.where(holder_ids == partner, held_counts, 0))
    pair_total = own_held + partner_held
    own_give = jnp.maximum(own_held - (pair_total + 1) // 2, 0)
    partner_give = jnp.maximum(partner_held - (pair_total + 1) // 2, 0)
    own_start = jnp.minimum(own_held - own_give, SLOTS - half_slots)
    partner_start = jnp.minimum(partner_held - partner_give, SLOTS - half_slots)
    send_vis = lax.dynamic_slice_in_dim(stokes_vis, own_start, half_slots, 1).astype(jnp.float32)
    send_track = lax.dynamic_slice_in_dim(tracks, own_start, half_slots, 1)
    got_vis, got_track = partner_2((send_vis, send_track), "slab", swap_bit)
    first_slot = partner_held - partner_give - partner_start
    helped = grid_range(
        got_vis.astype(jnp.bfloat16), got_track, first_slot, first_slot + partner_give, half_slots
    )
    returned_set = partner_2(helped, "slab", swap_bit)
    own_part = grid_range(stokes_vis, tracks, 0, own_held - own_give, SLOTS)
    subgrids = own_part + lax.dynamic_update_slice_in_dim(
        jnp.zeros_like(own_part), returned_set, own_start, 1
    )
    weight_flat = pixel_weight.reshape(pixel_area)
    sub_re = (subgrids[0] * weight_flat).reshape(SLOTS, SUB, SUB)
    sub_im = (subgrids[1] * weight_flat).reshape(SLOTS, SUB, SUB)
    uv_re, uv_im = subgrid_transform(sub_re, sub_im, dft_pair)
    uv_blocks = jnp.stack([uv_re, uv_im])
    own_offsets = lax.dynamic_slice_in_dim(offsets, slab_index * SLOTS, SLOTS, 1)
    own_rows = own_offsets[0] - slab_index * rows_local
    own_cols = own_offsets[1]
    window = jnp.zeros((2, rows_local + SUB, G), jnp.float32)
    window = place_blocks(window, uv_blocks, own_rows, own_cols)
    lower_rows = passed_along(window[:, rows_local:], "slab", 1)
    slab_grid = window[:, :rows_local].at[:, :SUB].add(lower_rows)
    small_side = G // 128
    large_side = 128
    table_small = dft_table(small_side)
    table_large = dft_table(large_side)
    twiddle = twiddle_table(small_side, large_side, G)
    plane_re = slab_grid[0].reshape(rows_local, small_side, large_side)
    plane_im = slab_grid[1].reshape(rows_local, small_side, large_side)
    step_re, step_im = complex_einsum("rkc,kx->rxc", (plane_re, plane_im), table_small)
    step_re, step_im = complex_multiply((step_re, step_im), twiddle)
    step_re, step_im = complex_einsum("rxc,cb->bxr", (step_re, step_im), table_large)
    moved_block = lax.all_to_all(
        jnp.stack([step_re, step_im]), "slab", split_axis=1, concat_axis=3, tiled=True
    )
    line_re = moved_block[0].reshape(rows_local, large_side, small_side)
    line_im = moved_block[1].reshape(rows_local, large_side, small_side)
    line_re, line_im = complex_einsum("xab,ay->xby", (line_re, line_im), table_large)
    line_re, line_im = complex_multiply((line_re, line_im), twiddle)
    line_re, line_im = complex_einsum("xby,bz->xzy", (line_re, line_im), table_small)
    norm_scale = 1.0 / (SUB * SUB * math.sqrt(VIS * SLOTS * slab_count / 8.0))
    sky_re = line_re.reshape(rows_local, G) * norm_scale
    sky_im = line_im.reshape(rows_local, G) * norm_scale
    return jnp.stack([sky_re, sky_im])[:, None]


LANES = 128
GROUP = 8


def turn_polynomials():
    z = np.cos(np.linspace(0.0, np.pi, 4001)) * 0.125 + 0.125
    r = np.sqrt(z)
    sine = np.where(r > 0, np.sin(np.pi * r) / np.where(r > 0, r, 1.0), np.pi)
    fits = []
    for values in (sine, np.cos(np.pi * r)):
        fit = np.polynomial.chebyshev.Chebyshev.fit(z, values, 4, domain=[0.0, 0.25])
        fits.append([float(v) for v in fit.convert(kind=np.polynomial.Polynomial).coef])
    return fits


SINE_COEF, COSINE_COEF = turn_polynomials()


def cos_sin_turns(turns):
    rest = turns - jnp.floor(turns + 0.5)
    square = rest * rest
    sine = SINE_COEF[-1]
    cosine = COSINE_COEF[-1]
    for coef in SINE_COEF[-2::-1]:
        sine = sine * square + coef
    for coef in COSINE_COEF[-2::-1]:
        cosine = cosine * square + coef
    sine = sine * rest
    double = sine + sine
    return 1.0 - double * sine, double * cosine


def times(left, right):
    return (left[0] * right[0] - left[1] * right[1], left[0] * right[1] + left[1] * right[0])


def plus(left, right):
    return (left[0] + right[0], left[1] + right[1])


def minus(left, right):
    return (left[0] - right[0], left[1] - right[1])


def quarter(value, sign):
    if sign > 0:
        return (-value[1], value[0])
    return (value[1], -value[0])


def dft_4(values, sign):
    a, b, c, d = values
    even_sum, even_diff = plus(a, c), minus(a, c)
    odd_sum, odd_diff = plus(b, d), quarter(minus(b, d), sign)
    return [plus(even_sum, odd_sum), plus(even_diff, odd_diff), minus(even_sum, odd_sum), minus(even_diff, odd_diff)]


ROOT_HALF = math.sqrt(0.5)


def dft_8(values, sign):
    even = dft_4(values[0::2], sign)
    odd = dft_4(values[1::2], sign)
    a, b = odd[1]
    odd[1] = ((a - b) * ROOT_HALF, (a + b) * ROOT_HALF) if sign > 0 else ((a + b) * ROOT_HALF, (b - a) * ROOT_HALF)
    odd[2] = quarter(odd[2], sign)
    a, b = odd[3]
    odd[3] = ((-a - b) * ROOT_HALF, (a - b) * ROOT_HALF) if sign > 0 else ((b - a) * ROOT_HALF, (-a - b) * ROOT_HALF)
    return [plus(e, o) for e, o in zip(even, odd)] + [minus(e, o) for e, o in zip(even, odd)]


def pixel_rows():
    row, col = np.divmod(np.arange(SUB * SUB), SUB)
    l = ((col - SUB // 2) / SUB).astype(np.float32)
    m = ((row - SUB // 2) / SUB).astype(np.float32)
    view = np.float32(FIELD_VIEW)
    n = (np.sqrt(np.float32(1.0) - (view * l) ** 2 - (view * m) ** 2) - np.float32(1.0)).astype(np.float32)
    return np.stack([l, m, n, row.astype(np.float32)] + [np.zeros_like(l)] * 4).astype(np.float32)


HALVES = VIS // LANES
WAVES = 2
TRACK_ROWS = WAVES * 3 * HALVES


def pack_kernel(held_ref, place_ref, counts_ref, corr_ref, track_ref, out_ref):
    devices = out_ref.shape[0]
    slab, pol = place_ref[0], place_ref[1]

    def count_before(holder, total):
        return total + jnp.where(holder < slab, held_ref[holder], 0)

    shift = jnp.bitwise_and(lax.fori_loop(0, held_ref.shape[0], count_before, 0), devices - 1)
    counts = jnp.transpose(jnp.broadcast_to(counts_ref[...].astype(jnp.float32), (LANES, counts_ref.shape[1])))
    lane = lax.broadcasted_iota(jnp.int32, (devices, LANES), 1).astype(jnp.float32)
    rows = []
    for wave in range(WAVES):
        at = pl.ds(wave * devices, devices)
        for c in range(2):
            for half in range(HALVES):
                value = corr_ref[c, at, pl.ds(half * LANES, LANES)].astype(jnp.float32)
                limit = counts[wave * devices : (wave + 1) * devices] - float(half * LANES)
                rows.append(jnp.where(lane < limit, value, 0.0))
    piece = TRACK_ROWS // 4
    for row in range(piece):
        value = None
        for sender in range(4):
            wave, axis, half = np.unravel_index(sender * piece + row, (WAVES, 3, HALVES))
            part = track_ref[int(axis), pl.ds(int(wave) * devices, devices), pl.ds(int(half) * LANES, LANES)]
            value = part if value is None else jnp.where(pol == sender, part, value)
        rows.append(value)
    for row, value in enumerate(rows):
        out_ref[:, row, :] = pltpu.roll(value, shift, 0)
    for row in range(len(rows), out_ref.shape[1]):
        out_ref[:, row, :] = jnp.zeros((devices, LANES), jnp.float32)


def packed(held, place, counts, corr, tracks, devices):
    smem = pl.BlockSpec(memory_space=pltpu.SMEM)
    vmem = pl.BlockSpec(memory_space=pltpu.VMEM)
    return pl.pallas_call(
        pack_kernel,
        out_shape=jax.ShapeDtypeStruct((devices, 16, LANES), jnp.float32),
        in_specs=[smem, smem, vmem, vmem, vmem],
        out_specs=vmem,
        compiler_params=pltpu.CompilerParams(vmem_limit_bytes=8 * 1024 * 1024),
        name="packed",
    )(held, place, counts, corr, tracks)


def row_twiddles():
    angle = -2.0 * np.pi * np.arange(8)[:, None] * (np.arange(LANES)[None, :] // SUB) / SUB
    return np.concatenate([np.cos(angle), np.sin(angle)], axis=0).astype(np.float32)


def subgrid_kernel(held_counts_ref, place_ref, offsets_ref, slots_ref, table_ref, twiddle_ref, weight_ref, *refs):
    piece_refs, more_ref, held_ref = refs[:4], refs[4], refs[5]
    held_ref[...] = jnp.zeros_like(held_ref)
    slab, pol = place_ref[0], place_ref[1]
    slabs = slots_ref.shape[0] // 4
    devices = slots_ref.shape[0]
    own = pol * slabs + slab
    total = lax.fori_loop(0, slabs, lambda holder, value: value + held_counts_ref[holder], 0)
    count = lax.shift_right_logical(total - own + (devices - 1), devices.bit_length() - 1)

    def locate(index):
        wanted = index * devices + own

        def look(holder, found):
            before, at_holder, at_slot = found
            after = before + held_counts_ref[holder]
            inside = (wanted >= before) & (wanted < after)
            return after, jnp.where(inside, holder, at_holder), jnp.where(inside, wanted - before, at_slot)

        _, at_holder, at_slot = lax.fori_loop(0, slabs, look, (0, 0, 0))
        return at_holder, at_slot

    def one_slot(index, carry):
        holder, slot = locate(index)
        early = slot < devices
        row_start = jnp.bitwise_and(offsets_ref[0, holder * SLOTS + slot], SUB - 1).astype(jnp.float32)
        tiles = [slots_ref[p * slabs + holder] for p in range(4)]
        xx, xy, yx, yy = [0.5 * jnp.where(early, tile[0:4], tile[4:8]) for tile in tiles]
        turned = xy - yx
        parameters = [xx + yy, xx - yy, xy + yx, jnp.concatenate([turned[2:4], -turned[0:2]], axis=0)]
        chosen = []
        for k in range(4):
            value = parameters[k]
            for other in range(1, 4):
                value = jnp.where(pol == other, parameters[k ^ other], value)
            chosen.append(value)
        halves = [
            jnp.concatenate([chosen[k][2 * c + half : 2 * c + half + 1] for c in range(2) for k in range(4)], axis=0)
            for half in range(2)
        ]
        vis = jnp.concatenate(halves, axis=1).astype(jnp.bfloat16)

        def track_half(axis, half):
            found = []
            for wave in range(WAVES):
                sender, row = divmod((wave * 3 + axis) * HALVES + half, TRACK_ROWS // 4)
                found.append(tiles[sender][8 + row : 9 + row])
            return jnp.where(early, found[0], found[1])

        track = jnp.concatenate(
            [jnp.concatenate([track_half(axis, half) for half in range(2)], axis=1) for axis in (0, 1, 2, 2, 2, 2, 2, 2)], axis=0
        )
        track = jnp.transpose(track)
        shape = (VIS, LANES)
        u = jnp.broadcast_to(track[:, 0:1] * (TRACK_SCALE * SUB), shape)
        v = jnp.broadcast_to(track[:, 1:2] * (TRACK_SCALE * SUB), shape)
        w = jnp.broadcast_to(track[:, 2:3] * DEPTH_SCALE, shape)
        placed = []
        for tile in range(SUB * SUB // LANES):
            lanes = pl.ds(tile * LANES, LANES)
            turns = u * table_ref[0:1, lanes] + v * table_ref[1:2, lanes] + w * table_ref[2:3, lanes]
            cosine, sine = cos_sin_turns(turns)
            phasor = jnp.concatenate([cosine.astype(jnp.bfloat16), sine.astype(jnp.bfloat16)], axis=1)
            product = jnp.dot(vis, phasor, preferred_element_type=jnp.float32)
            real = product[:4, :LANES] - product[4:, LANES:]
            imag = product[:4, LANES:] + product[4:, :LANES]
            weight = weight_ref[0:1, lanes]
            pixel_row = table_ref[3:4, lanes]
            turn = (row_start * (pixel_row - SUB // 2) + pixel_row * (SUB // 2)) * (1.0 / SUB)
            turn_re, turn_im = cos_sin_turns(turn)
            turn_re, turn_im = turn_re * weight, turn_im * weight
            placed.append(times((real, imag), (turn_re, turn_im)))
        for rho, value in enumerate(dft_8(placed, -1)):
            if rho:
                value = times(value, (twiddle_ref[rho : rho + 1], twiddle_ref[8 + rho : 9 + rho]))
            held_ref[index, :, pl.ds(2 * rho * LANES, LANES)] = value[0]
            held_ref[index, :, pl.ds((2 * rho + 1) * LANES, LANES)] = value[1]
        return carry

    lax.fori_loop(0, count, one_slot, 0)
    for k in range(4):
        piece_refs[k][...] = held_ref[:GROUP, k, :].astype(jnp.bfloat16)
        more_ref[k] = held_ref[GROUP:, k, :].astype(jnp.bfloat16)


def subgrids_of(held, place, offsets, slots, weight_row, capacity):
    smem = pl.BlockSpec(memory_space=pltpu.SMEM)
    vmem = pl.BlockSpec(memory_space=pltpu.VMEM)
    return pl.pallas_call(
        subgrid_kernel,
        out_shape=[jax.ShapeDtypeStruct((GROUP, 2 * SUB * SUB), jnp.bfloat16)] * 4
        + [jax.ShapeDtypeStruct((4, capacity - GROUP, 2 * SUB * SUB), jnp.bfloat16)],
        in_specs=[smem] * 3 + [vmem] * 4,
        out_specs=[vmem] * 5,
        scratch_shapes=[pltpu.VMEM((capacity, 4, 2 * SUB * SUB), jnp.float32)],
        compiler_params=pltpu.CompilerParams(vmem_limit_bytes=16 * 1024 * 1024),
        name="subgrids",
    )(held, place, offsets, slots, jnp.asarray(pixel_rows()), jnp.asarray(row_twiddles()), weight_row)


def image_kernel(pol_step, x_block, slabs, groups_ref, base_ref, row_ref, col_ref, mix_ref, twist_ref, *refs):
    first_refs, more_ref, sky_ref = refs[:slabs], refs[slabs], refs[slabs + 1]
    bundle_ref, phase_ref, col_phase_ref, *half_refs, moved_ref, sum_ref, stage_ref, out_ref = refs[slabs + 2 : -3]
    later_ref, sem_ref, later_sem_ref = refs[-3:]
    x_blocks = sky_ref.shape[1] // x_block
    groups = groups_ref[0]
    lane_index = lax.broadcasted_iota(jnp.int32, (LANES, LANES), 1)
    eighth = SUB // 4
    out_rows = out_ref.shape[2]
    out_steps = x_block // out_rows
    group_chunks = 4 // pol_step
    depth = 2 * LANES

    def load_phases(group, part):
        chunk = group * group_chunks + part
        rows = jnp.transpose(jnp.broadcast_to(row_ref[pl.ds(chunk, 1), :].astype(jnp.float32), (LANES, LANES)))
        rows = rows.astype(jnp.int32)
        high = lax.shift_right_logical(rows, 5)
        low = jnp.bitwise_and(rows, SUB - 1)
        here = cos_sin_turns(jnp.bitwise_and(high * lane_index, LANES - 1).astype(jnp.float32) * (1.0 / LANES))
        later = cos_sin_turns(jnp.bitwise_and((high + 1) * lane_index, LANES - 1).astype(jnp.float32) * (1.0 / LANES))
        re_rows = pl.ds(part * depth, LANES)
        im_rows = pl.ds(part * depth + LANES, LANES)

        def one_phase(residue, inner):
            carried = low > residue
            twist = (twist_ref[pl.ds(2 * residue, 1)], twist_ref[pl.ds(2 * residue + 1, 1)])
            re, im = times((jnp.where(carried, later[0], here[0]), jnp.where(carried, later[1], here[1])), twist)
            re = re.astype(jnp.bfloat16)
            phase_ref[residue, re_rows, :LANES] = re
            phase_ref[residue, re_rows, LANES:] = im.astype(jnp.bfloat16)
            phase_ref[residue, im_rows, :LANES] = (-im).astype(jnp.bfloat16)
            phase_ref[residue, im_rows, LANES:] = re
            return inner

        lax.fori_loop(0, SUB, one_phase, 0)

    def move_rows(group, part, block):
        chunk = group * group_chunks + part
        cols = col_ref[pl.ds(chunk, 1), :]
        x_index = lax.broadcasted_iota(jnp.int32, (x_block, LANES), 0) + (base_ref[0] + block * x_block)
        turns = jnp.bitwise_and(x_index * cols, G - 1).astype(jnp.float32) * (1.0 / G)
        turn_re, turn_im = cos_sin_turns(turns)
        col_phase_ref[0] = turn_re
        col_phase_ref[1] = turn_im
        re_lanes = pl.ds(pl.multiple_of(part * depth, LANES), LANES)
        im_lanes = pl.ds(pl.multiple_of(part * depth + LANES, LANES), LANES)

        def mix_pair(pair, half_ref):
            wide = jnp.concatenate(
                [
                    bundle_ref[part, :, pl.ds(4 * pair * LANES, depth)],
                    bundle_ref[part, :, pl.ds((4 * pair + 2) * LANES, depth)],
                ],
                axis=0,
            )
            for side in range(2):
                half_ref[side] = lax.dot_general(
                    mix_ref[block, side], wide, (((1,), (1,)), ((), ())), preferred_element_type=jnp.float32
                )

        def turn_pair(pair, half_ref):
            for tile in range(x_block // 16):
                rows_at = pl.ds(tile * 16, 16)
                turn = (col_phase_ref[0, rows_at], col_phase_ref[1, rows_at])
                for low in range(2):
                    at = pl.ds(low * LANES, LANES)
                    for high in range(4):
                        tile_rows = pl.ds(high * x_block + tile * 16, 16)
                        re, im = times((half_ref[0, tile_rows, at], half_ref[1, tile_rows, at]), turn)
                        residue = 2 * pair + low + 8 * high
                        moved_ref[residue, rows_at, re_lanes] = re.astype(jnp.bfloat16)
                        moved_ref[residue, rows_at, im_lanes] = im.astype(jnp.bfloat16)

        halves = half_refs
        mix_pair(0, halves[0])
        for pair in range(1, eighth // 2):
            mix_pair(pair, halves[pair % 2])
            turn_pair(pair - 1, halves[(pair - 1) % 2])
        turn_pair(eighth // 2 - 1, halves[(eighth // 2 - 1) % 2])

    def load_group(group):
        @pl.when(group > 0)
        def _():
            copy = pltpu.make_async_copy(more_ref, later_ref, later_sem_ref)
            copy.start()
            copy.wait()

        for part in range(group_chunks):
            polarized = pl.ds(part * pol_step, pol_step)
            span = pol_step * GROUP
            for peer in range(slabs):
                rows_at = pl.ds(peer * span, span)

                @pl.when(group == 0)
                def _(part=part, polarized=polarized, peer=peer, rows_at=rows_at):
                    bundle_ref[part, rows_at] = first_refs[peer][polarized].reshape(span, -1)

                @pl.when(group > 0)
                def _(part=part, polarized=polarized, peer=peer, rows_at=rows_at):
                    bundle_ref[part, rows_at] = later_ref[peer, polarized].reshape(span, -1)

            load_phases(group, part)

    def copy_out(block, step):
        x_at = pl.ds(pl.multiple_of(block * x_block + step * out_rows, 8), out_rows)
        return pltpu.make_async_copy(out_ref.at[step], sky_ref.at[:, x_at], sem_ref.at[step])

    def one_block(block, carry):
        def one_group(group, inner):
            @pl.when((block == 0) | (groups > 1))
            def _():
                load_group(group)

            def one_part(part, innermost):
                move_rows(group, part, block)
                return innermost

            lax.fori_loop(0, group_chunks, one_part, 0)

            @pl.when(group == 0)
            def _():
                def one_residue(residue, innermost):
                    sum_ref[residue] = jnp.dot(
                        moved_ref[residue], phase_ref[residue], preferred_element_type=jnp.float32
                    )
                    return innermost

                lax.fori_loop(0, SUB, one_residue, 0, unroll=16)

            @pl.when(group > 0)
            def _():
                def one_residue(residue, innermost):
                    sum_ref[residue] += jnp.dot(
                        moved_ref[residue], phase_ref[residue], preferred_element_type=jnp.float32
                    )
                    return innermost

                lax.fori_loop(0, SUB, one_residue, 0)

            return inner

        lax.fori_loop(0, groups, one_group, 0)

        def one_step(step, inner):
            @pl.when(block > 0)
            def _():
                copy_out(block - 1, step).wait()

            def one_tile(tile, innermost):
                rows_at = pl.ds(pl.multiple_of(step * out_rows + tile * 8, 8), 8)
                for second in range(4):
                    parts = []
                    for first in range(8):
                        residue = 4 * first + second
                        parts.append((sum_ref[residue, rows_at, :LANES], sum_ref[residue, rows_at, LANES:]))
                    for first, value in enumerate(dft_8(parts, 1)):
                        if first * second:
                            angle = TWO_PI * first * second / SUB
                            value = times(value, (math.cos(angle), math.sin(angle)))
                        stage_ref[second, first, 0] = value[0]
                        stage_ref[second, first, 1] = value[1]
                to_rows = pl.ds(pl.multiple_of(tile * 8, 8), 8)
                for first in range(8):
                    parts = [(stage_ref[second, first, 0], stage_ref[second, first, 1]) for second in range(4)]
                    for second, value in enumerate(dft_4(parts, 1)):
                        lanes = pl.ds((first + 8 * second) * LANES, LANES)
                        out_ref[step, 0, to_rows, lanes] = value[0]
                        out_ref[step, 1, to_rows, lanes] = value[1]
                return innermost

            lax.fori_loop(0, out_rows // 8, one_tile, 0)
            copy_out(block, step).start()
            return inner

        lax.fori_loop(0, out_steps, one_step, 0)
        return carry

    lax.fori_loop(0, x_blocks, one_block, 0)
    for step in range(out_steps):
        copy_out(x_blocks - 1, step).wait()


def twist_table(scale):
    residue = np.arange(SUB)[:, None]
    lane = np.arange(LANES)[None, :]
    angle = 2.0 * np.pi * (residue * lane % G) / G
    sign = np.where(residue % 2 == 0, scale, -scale)
    return np.stack([sign * np.cos(angle), sign * np.sin(angle)], axis=1).reshape(2 * SUB, LANES).astype(np.float32)


def mix_kernel(base_ref, sub_ref, turn_ref, mix_ref):
    x_block = mix_ref.shape[2] // 4
    highest = lax.Precision.HIGHEST
    cell = lax.broadcasted_iota(jnp.int32, (x_block, LANES), 1)

    def one_block(block, carry):
        x_index = lax.broadcasted_iota(jnp.int32, (x_block, LANES), 0) + (base_ref[0] + block * x_block)
        line_re, line_im = cos_sin_turns(jnp.bitwise_and(x_index * cell, G - 1).astype(jnp.float32) * (1.0 / G))
        by_re = jnp.dot(line_re, sub_ref[...], precision=highest, preferred_element_type=jnp.float32)
        by_im = jnp.dot(line_im, sub_ref[...], precision=highest, preferred_element_type=jnp.float32)
        core = (by_re[:, :LANES] - by_im[:, LANES:], by_re[:, LANES:] + by_im[:, :LANES])
        for rho in range(4):
            re, im = times(core, (turn_ref[rho : rho + 1], turn_ref[4 + rho : 5 + rho]))
            rows_at = pl.ds(rho * x_block, x_block)
            mix_ref[block, 0, rows_at, :LANES] = re.astype(jnp.bfloat16)
            mix_ref[block, 0, rows_at, LANES:] = (-im).astype(jnp.bfloat16)
            mix_ref[block, 1, rows_at, :LANES] = im.astype(jnp.bfloat16)
            mix_ref[block, 1, rows_at, LANES:] = re.astype(jnp.bfloat16)
        return carry

    lax.fori_loop(0, mix_ref.shape[0], one_block, 0)


def mix_table(x_base, x_count, x_block):
    cells, pixels = np.arange(LANES)[:, None], np.arange(LANES)[None, :] % SUB
    angle = -2.0 * np.pi * ((cells - SUB // 2) * (pixels - SUB // 2) % SUB) / SUB
    used = cells < SUB
    sub = np.concatenate([np.where(used, np.cos(angle), 0.0), np.where(used, np.sin(angle), 0.0)], axis=1)
    turn = (np.arange(4)[:, None] * (np.arange(LANES)[None, :] // SUB)) % 4
    turns = np.concatenate([np.array([1.0, 0.0, -1.0, 0.0])[turn], np.array([0.0, -1.0, 0.0, 1.0])[turn]])
    smem = pl.BlockSpec(memory_space=pltpu.SMEM)
    vmem = pl.BlockSpec(memory_space=pltpu.VMEM)
    return pl.pallas_call(
        mix_kernel,
        out_shape=jax.ShapeDtypeStruct((x_count // x_block, 2, 4 * x_block, 2 * LANES), jnp.bfloat16),
        in_specs=[smem, vmem, vmem],
        out_specs=vmem,
        cost_estimate=pl.CostEstimate(flops=1 << 30, bytes_accessed=1 << 22, transcendentals=0),
        compiler_params=pltpu.CompilerParams(vmem_limit_bytes=16 * 1024 * 1024),
        name="mix",
    )(x_base, jnp.asarray(sub, jnp.float32), jnp.asarray(turns, jnp.float32))


def image_of(groups, x_base, first, more, rows, cols, mix, x_count, x_block, scale, pol_step):
    out_rows = min(x_block, 64)
    parts = 4 // pol_step
    slabs = len(first)
    smem = pl.BlockSpec(memory_space=pltpu.SMEM)
    vmem = pl.BlockSpec(memory_space=pltpu.VMEM)
    hbm = pl.BlockSpec(memory_space=pl.ANY)
    return pl.pallas_call(
        functools.partial(image_kernel, pol_step, x_block, slabs),
        out_shape=jax.ShapeDtypeStruct((2, x_count, G), jnp.float32),
        in_specs=[smem, smem] + [vmem] * (4 + slabs) + [hbm],
        out_specs=hbm,
        scratch_shapes=[
            pltpu.VMEM((parts, LANES, 2 * SUB * SUB), jnp.bfloat16),
            pltpu.VMEM((SUB, parts * 2 * LANES, 2 * LANES), jnp.bfloat16),
            pltpu.VMEM((2, x_block, LANES), jnp.float32),
            pltpu.VMEM((2, 4 * x_block, 2 * LANES), jnp.float32),
            pltpu.VMEM((2, 4 * x_block, 2 * LANES), jnp.float32),
            pltpu.VMEM((SUB, x_block, parts * 2 * LANES), jnp.bfloat16),
            pltpu.VMEM((SUB, x_block, 2 * LANES), jnp.float32),
            pltpu.VMEM((4, 8, 2, 8, LANES), jnp.float32),
            pltpu.VMEM((x_block // out_rows, 2, out_rows, G), jnp.float32),
            pltpu.VMEM(more.shape, more.dtype),
            pltpu.SemaphoreType.DMA((x_block // out_rows,)),
            pltpu.SemaphoreType.DMA,
        ],
        compiler_params=pltpu.CompilerParams(vmem_limit_bytes=46 * 1024 * 1024),
        name="image",
    )(groups, x_base, rows, cols, mix, jnp.asarray(twist_table(scale)), *first, more)


def exchanged(value, axis, distance):
    peers = lax.axis_size(axis)
    return lax.ppermute(value, axis, [(i, i ^ distance) for i in range(peers)])


def gathered(pieces, beside=None):
    slabs = lax.axis_size("slab")
    value = jnp.stack([pieces[0]] + [exchanged(piece, "pol", k) for k, piece in enumerate(pieces) if k])
    planes = [value] + [exchanged(value, "slab", k) for k in range(2, slabs, 2)]
    made = None
    if beside is not None:
        made = beside(value)
        planes[-1], made = lax.optimization_barrier((planes[-1], made))
    values = []
    for plane in planes:
        values += [plane, exchanged(plane, "slab", 1)]
    return values, made


def in_image_domain(correlations, tracks, vis_counts, offsets, held_counts, pixel_weight):
    pols, slabs = lax.axis_size("pol"), lax.axis_size("slab")
    pol, slab = lax.axis_index("pol"), lax.axis_index("slab")
    devices = pols * slabs
    capacity = SLOTS * slabs // devices
    x_count = G // slabs
    held = held_counts.astype(jnp.int32)
    holders = jnp.arange(slabs, dtype=jnp.int32)
    where_at = jnp.stack([slab, pol]).astype(jnp.int32)
    sent = packed(held, where_at, vis_counts.reshape(1, SLOTS), correlations[:, 0], tracks, devices)
    slots = lax.all_to_all(sent, ("pol", "slab"), 0, 0, tiled=True)
    held, _ = lax.optimization_barrier((held, sent))
    before = jnp.sum(jnp.where(holders[None, :] < holders[:, None], held[None, :], 0), axis=1)
    total = jnp.sum(held)

    slot = jnp.arange(SLOTS, dtype=jnp.int32)
    order = jnp.where(slot[None, :] < held[:, None], before[:, None] + slot[None, :], -1).reshape(-1)
    device_at, seat_at = order % devices, order // devices
    pol_step = LANES // (GROUP * slabs)
    lane_order = (device_at % slabs) ^ slab
    pol_order = (device_at // slabs) ^ pol
    place = (seat_at // GROUP) * (pols // pol_step) + pol_order // pol_step
    place = place * LANES + lane_order * (pol_step * GROUP) + pol_order % pol_step * GROUP + seat_at % GROUP
    place = jnp.where(order >= 0, place, -1)
    chunk_count = capacity // GROUP * (pols // pol_step)
    spots = jnp.arange(chunk_count * LANES, dtype=jnp.int32)
    chosen = spots[:, None] == place[None, :]
    rows = jnp.sum(jnp.where(chosen, offsets[0][None, :], 0), axis=1).reshape(chunk_count, LANES)
    cols = jnp.sum(jnp.where(chosen, offsets[1][None, :], 0), axis=1).reshape(chunk_count, LANES)
    slots, rows, cols = lax.optimization_barrier((slots, rows, cols))
    weight_row = pixel_weight.reshape(1, SUB * SUB)
    *pieces, extra = subgrids_of(held, where_at, offsets.astype(jnp.int32), slots, weight_row, capacity)
    norm_scale = 1.0 / (SUB * SUB * math.sqrt(VIS * SLOTS * slabs / 8.0))
    x_base = (slab * x_count).reshape(1)
    x_block = min(x_count, 256)

    many = total > devices * GROUP

    def besides(after):
        base, _ = lax.optimization_barrier((x_base, after))
        mix = mix_table(base, x_count, x_block)
        more_needed, _ = lax.optimization_barrier((many, mix))
        more = lax.cond(
            more_needed,
            lambda: jnp.stack(gathered([extra[k] for k in range(pols)])[0]),
            lambda: jnp.zeros((slabs,) + extra.shape, extra.dtype),
        )
        return mix, more

    first, (mix, more) = gathered(pieces, besides)
    groups = jnp.where(many, capacity // GROUP, 1).reshape(1)
    sky = image_of(groups, x_base, first, more, rows, cols, mix, x_count, x_block, norm_scale, pol_step)
    return sky[:, None]


def fits_image_domain(mesh):
    pols, slabs = mesh.shape["pol"], mesh.shape["slab"]
    devices = pols * slabs
    whole = slabs & (slabs - 1) == 0 and slabs * GROUP <= LANES and SLOTS * slabs == 2 * GROUP * devices
    return whole and pols == 4 and SLOTS == WAVES * devices and pols % (LANES // (GROUP * slabs)) == 0


def solution(mesh):
    in_specs = (P(None, "pol", "slab", None), P(None, "slab", None), P("slab"), P(), P(), P())
    out_specs = P(None, "pol", "slab", None)
    body = in_image_domain if fits_image_domain(mesh) else on_device
    return jax.shard_map(body, mesh=mesh, in_specs=in_specs, out_specs=out_specs, check_vma=False)
```

```python
import functools
import math

import jax
import jax.numpy as jnp
import numpy as np
from jax import lax
from jax.experimental import pallas as pl
from jax.experimental.pallas import tpu as pltpu
from jax.sharding import PartitionSpec as P

G = 4096
SUB = 32
VIS = 256
SLOTS = 64


TWO_PI = 2.0 * math.pi
FIELD_VIEW = 0.6
DEPTH_SCALE = 40.0
TRACK_SCALE = 0.375
COEF_REAL = np.array(
    [[0.5, 0.0, 0.0, 0.5], [0.5, 0.0, 0.0, -0.5], [0.0, 0.5, 0.5, 0.0], [0.0, 0.0, 0.0, 0.0]],
    np.float32,
)
COEF_IMAG = np.array(
    [[0.0, 0.0, 0.0, 0.0], [0.0, 0.0, 0.0, 0.0], [0.0, 0.0, 0.0, 0.0], [0.0, -0.5, 0.5, 0.0]],
    np.float32,
)


def partner_2(value, axis, distance):
    return lax.ppermute(value, axis, [(i, i ^ 1 << distance) for i in range(lax.axis_size(axis))])


def passed_along(value, axis, by):
    peers = lax.axis_size(axis)
    pairs = [(i, i + by) for i in range(peers) if 0 <= i + by < peers]
    return lax.ppermute(value, axis, pairs)


def pixel_tables():
    cells = jnp.arange(SUB * SUB, dtype=jnp.int32)
    row_pos = (cells // SUB - SUB // 2).astype(jnp.float32) / SUB
    col_pos = (cells % SUB - SUB // 2).astype(jnp.float32) / SUB
    depth = jnp.sqrt(1.0 - (FIELD_VIEW * col_pos) ** 2 - (FIELD_VIEW * row_pos) ** 2) - 1.0
    return (col_pos, row_pos, depth)


def phasor_table(track_set, tables):
    col_pos, row_pos, depth = tables
    u_cells = track_set[0] * (TRACK_SCALE * SUB)
    v_cells = track_set[1] * (TRACK_SCALE * SUB)
    w_cells = track_set[2] * DEPTH_SCALE
    phase = TWO_PI * (
        u_cells[:, None] * col_pos[None, :]
        + v_cells[:, None] * row_pos[None, :]
        + w_cells[:, None] * depth[None, :]
    )
    return jnp.concatenate([jnp.cos(phase), jnp.sin(phase)], axis=1).astype(jnp.bfloat16)


def subgrid_tables():
    positions = jnp.arange(SUB, dtype=jnp.int32) - SUB // 2
    turn_count = positions[:, None] * positions[None, :] % SUB
    angles = -TWO_PI * turn_count.astype(jnp.float32) / SUB
    return (jnp.cos(angles), jnp.sin(angles))


def dft_table(length):
    positions = jnp.arange(length, dtype=jnp.int32)
    turn_count = positions[:, None] * positions[None, :] % length
    angles = TWO_PI * turn_count.astype(jnp.float32) / length
    return (jnp.cos(angles), jnp.sin(angles))


def twiddle_table(first_len, second_len, length):
    first_pos = jnp.arange(first_len, dtype=jnp.int32)
    second_pos = jnp.arange(second_len, dtype=jnp.int32)
    turn_count = first_pos[:, None] * second_pos[None, :] % length
    angles = TWO_PI * turn_count.astype(jnp.float32) / length
    return (jnp.cos(angles), jnp.sin(angles))


def complex_einsum(pattern, left_pair, right_pair):
    highest = lax.Precision.HIGHEST
    left_re, left_im = left_pair
    right_re, right_im = right_pair
    real_part = jnp.einsum(pattern, left_re, right_re, precision=highest) - jnp.einsum(
        pattern, left_im, right_im, precision=highest
    )
    imag_part = jnp.einsum(pattern, left_re, right_im, precision=highest) + jnp.einsum(
        pattern, left_im, right_re, precision=highest
    )
    return (real_part, imag_part)


def complex_multiply(data_pair, table_pair):
    data_re, data_im = data_pair
    table_re, table_im = table_pair
    return (data_re * table_re - data_im * table_im, data_re * table_im + data_im * table_re)


def subgrid_transform(sub_re, sub_im, dft_pair):
    half_re, half_im = complex_einsum("...ij,cj->...ic", (sub_re, sub_im), dft_pair)
    return complex_einsum("ai,...ic->...ac", dft_pair, (half_re, half_im))


def place_blocks(window, blocks, row_starts, col_starts):
    block_count = blocks.shape[1]
    zero_index = jnp.zeros((), jnp.int32)

    def add_one(slot_index, current_window):
        block = lax.dynamic_index_in_dim(blocks, slot_index, 1, keepdims=False)
        corner = (zero_index, row_starts[slot_index], col_starts[slot_index])
        current = lax.dynamic_slice(current_window, corner, (2, SUB, SUB))
        return lax.dynamic_update_slice(current_window, current + block, corner)

    return lax.fori_loop(0, block_count, add_one, window)


def on_device(correlations, tracks, vis_counts, offsets, held_counts, pixel_weight):
    highest = lax.Precision.HIGHEST
    slab_count = lax.axis_size("slab")
    slab_index = lax.axis_index("slab")
    stokes_index = lax.axis_index("pol")
    pixel_area = SUB * SUB
    rows_local = G // slab_count
    tables = pixel_tables()
    dft_pair = subgrid_tables()
    gathered = lax.all_gather(correlations, "pol", axis=1, tiled=True)
    corr_float = gathered.astype(jnp.float32)
    select = (jnp.arange(4, dtype=jnp.int32) == stokes_index).astype(jnp.float32)
    coef_re = jnp.sum(select[:, None] * jnp.asarray(COEF_REAL), axis=0)
    coef_im = jnp.sum(select[:, None] * jnp.asarray(COEF_IMAG), axis=0)
    stokes_re = jnp.einsum("p,pnv->nv", coef_re, corr_float[0], precision=highest) - jnp.einsum(
        "p,pnv->nv", coef_im, corr_float[1], precision=highest
    )
    stokes_im = jnp.einsum("p,pnv->nv", coef_re, corr_float[1], precision=highest) + jnp.einsum(
        "p,pnv->nv", coef_im, corr_float[0], precision=highest
    )
    visible = (jnp.arange(VIS, dtype=jnp.int32)[None, :] < vis_counts[:, None]).astype(jnp.bfloat16)
    stokes_vis = jnp.stack([stokes_re, stokes_im]).astype(jnp.bfloat16) * visible[None]
    holder_ids = jnp.arange(slab_count, dtype=jnp.int32)
    own_held = jnp.sum(jnp.where(holder_ids == slab_index, held_counts, 0))

    def grid_range(vis_set, track_set, first_slot, stop_slot, capacity):

        def one_slot(slot_index, subgrid_set):
            phasor = phasor_table(
                lax.dynamic_index_in_dim(track_set, slot_index, 1, keepdims=False), tables
            )
            vis_slot = lax.dynamic_index_in_dim(vis_set, slot_index, 1, keepdims=False)
            product = jnp.dot(vis_slot, phasor, preferred_element_type=jnp.float32)
            sub_re = product[0, :pixel_area] - product[1, pixel_area:]
            sub_im = product[0, pixel_area:] + product[1, :pixel_area]
            update = jnp.stack([sub_re, sub_im])[:, None, :]
            return lax.dynamic_update_slice_in_dim(subgrid_set, update, slot_index, 1)

        zero_set = jnp.zeros((2, capacity, pixel_area), jnp.float32)
        return lax.fori_loop(first_slot, stop_slot, one_slot, zero_set)

    half_slots = SLOTS // 2
    swap_bit = slab_count.bit_length() - 2
    partner = jnp.bitwise_xor(slab_index, slab_count // 2)
    partner_held = jnp.sum(jnp.where(holder_ids == partner, held_counts, 0))
    pair_total = own_held + partner_held
    own_give = jnp.maximum(own_held - (pair_total + 1) // 2, 0)
    partner_give = jnp.maximum(partner_held - (pair_total + 1) // 2, 0)
    own_start = jnp.minimum(own_held - own_give, SLOTS - half_slots)
    partner_start = jnp.minimum(partner_held - partner_give, SLOTS - half_slots)
    send_vis = lax.dynamic_slice_in_dim(stokes_vis, own_start, half_slots, 1).astype(jnp.float32)
    send_track = lax.dynamic_slice_in_dim(tracks, own_start, half_slots, 1)
    got_vis, got_track = partner_2((send_vis, send_track), "slab", swap_bit)
    first_slot = partner_held - partner_give - partner_start
    helped = grid_range(
        got_vis.astype(jnp.bfloat16), got_track, first_slot, first_slot + partner_give, half_slots
    )
    returned_set = partner_2(helped, "slab", swap_bit)
    own_part = grid_range(stokes_vis, tracks, 0, own_held - own_give, SLOTS)
    subgrids = own_part + lax.dynamic_update_slice_in_dim(
        jnp.zeros_like(own_part), returned_set, own_start, 1
    )
    weight_flat = pixel_weight.reshape(pixel_area)
    sub_re = (subgrids[0] * weight_flat).reshape(SLOTS, SUB, SUB)
    sub_im = (subgrids[1] * weight_flat).reshape(SLOTS, SUB, SUB)
    uv_re, uv_im = subgrid_transform(sub_re, sub_im, dft_pair)
    uv_blocks = jnp.stack([uv_re, uv_im])
    own_offsets = lax.dynamic_slice_in_dim(offsets, slab_index * SLOTS, SLOTS, 1)
    own_rows = own_offsets[0] - slab_index * rows_local
    own_cols = own_offsets[1]
    window = jnp.zeros((2, rows_local + SUB, G), jnp.float32)
    window = place_blocks(window, uv_blocks, own_rows, own_cols)
    lower_rows = passed_along(window[:, rows_local:], "slab", 1)
    slab_grid = window[:, :rows_local].at[:, :SUB].add(lower_rows)
    small_side = G // 128
    large_side = 128
    table_small = dft_table(small_side)
    table_large = dft_table(large_side)
    twiddle = twiddle_table(small_side, large_side, G)
    plane_re = slab_grid[0].reshape(rows_local, small_side, large_side)
    plane_im = slab_grid[1].reshape(rows_local, small_side, large_side)
    step_re, step_im = complex_einsum("rkc,kx->rxc", (plane_re, plane_im), table_small)
    step_re, step_im = complex_multiply((step_re, step_im), twiddle)
    step_re, step_im = complex_einsum("rxc,cb->bxr", (step_re, step_im), table_large)
    moved_block = lax.all_to_all(
        jnp.stack([step_re, step_im]), "slab", split_axis=1, concat_axis=3, tiled=True
    )
    line_re = moved_block[0].reshape(rows_local, large_side, small_side)
    line_im = moved_block[1].reshape(rows_local, large_side, small_side)
    line_re, line_im = complex_einsum("xab,ay->xby", (line_re, line_im), table_large)
    line_re, line_im = complex_multiply((line_re, line_im), twiddle)
    line_re, line_im = complex_einsum("xby,bz->xzy", (line_re, line_im), table_small)
    norm_scale = 1.0 / (SUB * SUB * math.sqrt(VIS * SLOTS * slab_count / 8.0))
    sky_re = line_re.reshape(rows_local, G) * norm_scale
    sky_im = line_im.reshape(rows_local, G) * norm_scale
    return jnp.stack([sky_re, sky_im])[:, None]


LANES = 128
GROUP = 8


def turn_polynomials():
    z = np.cos(np.linspace(0.0, np.pi, 4001)) * 0.125 + 0.125
    r = np.sqrt(z)
    sine = np.where(r > 0, np.sin(np.pi * r) / np.where(r > 0, r, 1.0), np.pi)
    fits = []
    for values in (sine, np.cos(np.pi * r)):
        fit = np.polynomial.chebyshev.Chebyshev.fit(z, values, 4, domain=[0.0, 0.25])
        fits.append([float(v) for v in fit.convert(kind=np.polynomial.Polynomial).coef])
    return fits


SINE_COEF, COSINE_COEF = turn_polynomials()


def cos_sin_turns(turns):
    rest = turns - jnp.floor(turns + 0.5)
    square = rest * rest
    sine = SINE_COEF[-1]
    cosine = COSINE_COEF[-1]
    for coef in SINE_COEF[-2::-1]:
        sine = sine * square + coef
    for coef in COSINE_COEF[-2::-1]:
        cosine = cosine * square + coef
    sine = sine * rest
    double = sine + sine
    return 1.0 - double * sine, double * cosine


def times(left, right):
    return (left[0] * right[0] - left[1] * right[1], left[0] * right[1] + left[1] * right[0])


def plus(left, right):
    return (left[0] + right[0], left[1] + right[1])


def minus(left, right):
    return (left[0] - right[0], left[1] - right[1])


def quarter(value, sign):
    if sign > 0:
        return (-value[1], value[0])
    return (value[1], -value[0])


def dft_4(values, sign):
    a, b, c, d = values
    even_sum, even_diff = plus(a, c), minus(a, c)
    odd_sum, odd_diff = plus(b, d), quarter(minus(b, d), sign)
    return [plus(even_sum, odd_sum), plus(even_diff, odd_diff), minus(even_sum, odd_sum), minus(even_diff, odd_diff)]


ROOT_HALF = math.sqrt(0.5)


def dft_8(values, sign):
    even = dft_4(values[0::2], sign)
    odd = dft_4(values[1::2], sign)
    a, b = odd[1]
    odd[1] = ((a - b) * ROOT_HALF, (a + b) * ROOT_HALF) if sign > 0 else ((a + b) * ROOT_HALF, (b - a) * ROOT_HALF)
    odd[2] = quarter(odd[2], sign)
    a, b = odd[3]
    odd[3] = ((-a - b) * ROOT_HALF, (a - b) * ROOT_HALF) if sign > 0 else ((b - a) * ROOT_HALF, (-a - b) * ROOT_HALF)
    return [plus(e, o) for e, o in zip(even, odd)] + [minus(e, o) for e, o in zip(even, odd)]


def pixel_rows():
    row, col = np.divmod(np.arange(SUB * SUB), SUB)
    l = ((col - SUB // 2) / SUB).astype(np.float32)
    m = ((row - SUB // 2) / SUB).astype(np.float32)
    view = np.float32(FIELD_VIEW)
    n = (np.sqrt(np.float32(1.0) - (view * l) ** 2 - (view * m) ** 2) - np.float32(1.0)).astype(np.float32)
    return np.stack([l, m, n, row.astype(np.float32)] + [np.zeros_like(l)] * 4).astype(np.float32)


HALVES = VIS // LANES
WAVES = 2
TRACK_ROWS = WAVES * 3 * HALVES


def pack_kernel(held_ref, place_ref, counts_ref, corr_ref, track_ref, out_ref):
    devices = out_ref.shape[0]
    slab, pol = place_ref[0], place_ref[1]

    def count_before(holder, total):
        return total + jnp.where(holder < slab, held_ref[holder], 0)

    shift = jnp.bitwise_and(lax.fori_loop(0, held_ref.shape[0], count_before, 0), devices - 1)
    counts = jnp.transpose(jnp.broadcast_to(counts_ref[...].astype(jnp.float32), (LANES, counts_ref.shape[1])))
    lane = lax.broadcasted_iota(jnp.int32, (devices, LANES), 1).astype(jnp.float32)
    rows = []
    for wave in range(WAVES):
        at = pl.ds(wave * devices, devices)
        for c in range(2):
            for half in range(HALVES):
                value = corr_ref[c, at, pl.ds(half * LANES, LANES)].astype(jnp.float32)
                limit = counts[wave * devices : (wave + 1) * devices] - float(half * LANES)
                rows.append(jnp.where(lane < limit, value, 0.0))
    piece = TRACK_ROWS // 4
    for row in range(piece):
        value = None
        for sender in range(4):
            wave, axis, half = np.unravel_index(sender * piece + row, (WAVES, 3, HALVES))
            part = track_ref[int(axis), pl.ds(int(wave) * devices, devices), pl.ds(int(half) * LANES, LANES)]
            value = part if value is None else jnp.where(pol == sender, part, value)
        rows.append(value)
    for row, value in enumerate(rows):
        out_ref[:, row, :] = pltpu.roll(value, shift, 0)
    for row in range(len(rows), out_ref.shape[1]):
        out_ref[:, row, :] = jnp.zeros((devices, LANES), jnp.float32)


def packed(held, place, counts, corr, tracks, devices):
    smem = pl.BlockSpec(memory_space=pltpu.SMEM)
    vmem = pl.BlockSpec(memory_space=pltpu.VMEM)
    return pl.pallas_call(
        pack_kernel,
        out_shape=jax.ShapeDtypeStruct((devices, 16, LANES), jnp.float32),
        in_specs=[smem, smem, vmem, vmem, vmem],
        out_specs=vmem,
        name="packed",
    )(held, place, counts, corr, tracks)


def row_twiddles():
    angle = -2.0 * np.pi * np.arange(8)[:, None] * (np.arange(LANES)[None, :] // SUB) / SUB
    return np.concatenate([np.cos(angle), np.sin(angle)], axis=0).astype(np.float32)


def subgrid_kernel(held_counts_ref, place_ref, offsets_ref, slots_ref, table_ref, twiddle_ref, weight_ref, *refs):
    piece_refs, more_ref, held_ref = refs[:4], refs[4], refs[5]
    held_ref[...] = jnp.zeros_like(held_ref)
    slab, pol = place_ref[0], place_ref[1]
    slabs = slots_ref.shape[0] // 4
    devices = slots_ref.shape[0]
    own = pol * slabs + slab
    total = lax.fori_loop(0, slabs, lambda holder, value: value + held_counts_ref[holder], 0)
    count = lax.shift_right_logical(total - own + (devices - 1), devices.bit_length() - 1)

    def locate(index):
        wanted = index * devices + own

        def look(holder, found):
            before, at_holder, at_slot = found
            after = before + held_counts_ref[holder]
            inside = (wanted >= before) & (wanted < after)
            return after, jnp.where(inside, holder, at_holder), jnp.where(inside, wanted - before, at_slot)

        _, at_holder, at_slot = lax.fori_loop(0, slabs, look, (0, 0, 0))
        return at_holder, at_slot

    def one_slot(index, carry):
        holder, slot = locate(index)
        early = slot < devices
        row_start = jnp.bitwise_and(offsets_ref[0, holder * SLOTS + slot], SUB - 1).astype(jnp.float32)
        tiles = [slots_ref[p * slabs + holder] for p in range(4)]
        xx, xy, yx, yy = [0.5 * jnp.where(early, tile[0:4], tile[4:8]) for tile in tiles]
        turned = xy - yx
        parameters = [xx + yy, xx - yy, xy + yx, jnp.concatenate([turned[2:4], -turned[0:2]], axis=0)]
        chosen = []
        for k in range(4):
            value = parameters[k]
            for other in range(1, 4):
                value = jnp.where(pol == other, parameters[k ^ other], value)
            chosen.append(value)
        halves = [
            jnp.concatenate([chosen[k][2 * c + half : 2 * c + half + 1] for c in range(2) for k in range(4)], axis=0)
            for half in range(2)
        ]
        vis = jnp.concatenate(halves, axis=1).astype(jnp.bfloat16)

        def track_half(axis, half):
            found = []
            for wave in range(WAVES):
                sender, row = divmod((wave * 3 + axis) * HALVES + half, TRACK_ROWS // 4)
                found.append(tiles[sender][8 + row : 9 + row])
            return jnp.where(early, found[0], found[1])

        track = jnp.concatenate(
            [jnp.concatenate([track_half(axis, half) for half in range(2)], axis=1) for axis in (0, 1, 2, 2, 2, 2, 2, 2)], axis=0
        )
        track = jnp.transpose(track)
        shape = (VIS, LANES)
        u = jnp.broadcast_to(track[:, 0:1] * (TRACK_SCALE * SUB), shape)
        v = jnp.broadcast_to(track[:, 1:2] * (TRACK_SCALE * SUB), shape)
        w = jnp.broadcast_to(track[:, 2:3] * DEPTH_SCALE, shape)
        placed = []
        for tile in range(SUB * SUB // LANES):
            lanes = pl.ds(tile * LANES, LANES)
            turns = u * table_ref[0:1, lanes] + v * table_ref[1:2, lanes] + w * table_ref[2:3, lanes]
            cosine, sine = cos_sin_turns(turns)
            phasor = jnp.concatenate([cosine.astype(jnp.bfloat16), sine.astype(jnp.bfloat16)], axis=1)
            product = jnp.dot(vis, phasor, preferred_element_type=jnp.float32)
            real = product[:4, :LANES] - product[4:, LANES:]
            imag = product[:4, LANES:] + product[4:, :LANES]
            weight = weight_ref[0:1, lanes]
            pixel_row = table_ref[3:4, lanes]
            turn = (row_start * (pixel_row - SUB // 2) + pixel_row * (SUB // 2)) * (1.0 / SUB)
            turn_re, turn_im = cos_sin_turns(turn)
            turn_re, turn_im = turn_re * weight, turn_im * weight
            placed.append(times((real, imag), (turn_re, turn_im)))
        for rho, value in enumerate(dft_8(placed, -1)):
            if rho:
                value = times(value, (twiddle_ref[rho : rho + 1], twiddle_ref[8 + rho : 9 + rho]))
            held_ref[index, :, pl.ds(2 * rho * LANES, LANES)] = value[0]
            held_ref[index, :, pl.ds((2 * rho + 1) * LANES, LANES)] = value[1]
        return carry

    lax.fori_loop(0, count, one_slot, 0)
    for k in range(4):
        piece_refs[k][...] = held_ref[:GROUP, k, :].astype(jnp.bfloat16)
        more_ref[k] = held_ref[GROUP:, k, :].astype(jnp.bfloat16)


def subgrids_of(held, place, offsets, slots, weight_row, capacity):
    smem = pl.BlockSpec(memory_space=pltpu.SMEM)
    vmem = pl.BlockSpec(memory_space=pltpu.VMEM)
    return pl.pallas_call(
        subgrid_kernel,
        out_shape=[jax.ShapeDtypeStruct((GROUP, 2 * SUB * SUB), jnp.bfloat16)] * 4
        + [jax.ShapeDtypeStruct((4, capacity - GROUP, 2 * SUB * SUB), jnp.bfloat16)],
        in_specs=[smem] * 3 + [vmem] * 4,
        out_specs=[vmem] * 5,
        scratch_shapes=[pltpu.VMEM((capacity, 4, 2 * SUB * SUB), jnp.float32)],
        name="subgrids",
    )(held, place, offsets, slots, jnp.asarray(pixel_rows()), jnp.asarray(row_twiddles()), weight_row)


def image_kernel(pol_step, x_block, slabs, twice, groups_ref, base_ref, row_ref, col_ref, mix_ref, twist_ref, *refs):
    first_refs, more_ref = refs[:slabs], refs[slabs]
    refs = refs[slabs + twice :]
    sky_ref = refs[0]
    bundle_ref, phase_ref, col_phase_ref, *half_refs, moved_ref, sum_ref, stage_ref, out_ref = refs[1:-3]
    later_ref, sem_ref, later_sem_ref = refs[-3:]
    x_blocks = sky_ref.shape[1] // x_block
    groups = groups_ref[0] if twice else 1
    lane_index = lax.broadcasted_iota(jnp.int32, (LANES, LANES), 1)
    eighth = SUB // 4
    out_rows = out_ref.shape[2]
    out_steps = x_block // out_rows
    group_chunks = 4 // pol_step
    depth = 2 * LANES

    def load_phases(group, part):
        chunk = group * group_chunks + part
        rows = jnp.transpose(jnp.broadcast_to(row_ref[pl.ds(chunk, 1), :].astype(jnp.float32), (LANES, LANES)))
        rows = rows.astype(jnp.int32)
        high = lax.shift_right_logical(rows, 5)
        low = jnp.bitwise_and(rows, SUB - 1)
        here = cos_sin_turns(jnp.bitwise_and(high * lane_index, LANES - 1).astype(jnp.float32) * (1.0 / LANES))
        later = cos_sin_turns(jnp.bitwise_and((high + 1) * lane_index, LANES - 1).astype(jnp.float32) * (1.0 / LANES))
        re_rows = pl.ds(part * depth, LANES)
        im_rows = pl.ds(part * depth + LANES, LANES)

        def one_phase(residue, inner):
            carried = low > residue
            twist = (twist_ref[pl.ds(residue, 1)], twist_ref[pl.ds(SUB + residue, 1)])
            re, im = times((jnp.where(carried, later[0], here[0]), jnp.where(carried, later[1], here[1])), twist)
            re = re.astype(jnp.bfloat16)
            phase_ref[residue, re_rows, :LANES] = re
            phase_ref[residue, re_rows, LANES:] = im.astype(jnp.bfloat16)
            phase_ref[residue, im_rows, :LANES] = (-im).astype(jnp.bfloat16)
            phase_ref[residue, im_rows, LANES:] = re
            return inner

        lax.fori_loop(0, SUB, one_phase, 0)

    def move_rows(group, part, block):
        chunk = group * group_chunks + part
        cols = col_ref[pl.ds(chunk, 1), :]
        x_index = lax.broadcasted_iota(jnp.int32, (x_block, LANES), 0) + (base_ref[0] + block * x_block)
        turns = jnp.bitwise_and(x_index * cols, G - 1).astype(jnp.float32) * (1.0 / G)
        turn_re, turn_im = cos_sin_turns(turns)
        col_phase_ref[0] = turn_re
        col_phase_ref[1] = turn_im
        re_lanes = pl.ds(pl.multiple_of(part * depth, LANES), LANES)
        im_lanes = pl.ds(pl.multiple_of(part * depth + LANES, LANES), LANES)

        def mix_pair(pair, half_ref):
            wide = jnp.concatenate(
                [
                    bundle_ref[part, :, pl.ds(4 * pair * LANES, depth)],
                    bundle_ref[part, :, pl.ds((4 * pair + 2) * LANES, depth)],
                ],
                axis=0,
            )
            for side in range(2):
                half_ref[side] = lax.dot_general(
                    mix_ref[block, side], wide, (((1,), (1,)), ((), ())), preferred_element_type=jnp.float32
                )

        def turn_pair(pair, half_ref):
            for tile in range(x_block // 16):
                rows_at = pl.ds(tile * 16, 16)
                turn = (col_phase_ref[0, rows_at], col_phase_ref[1, rows_at])
                for low in range(2):
                    at = pl.ds(low * LANES, LANES)
                    for high in range(4):
                        tile_rows = pl.ds(high * x_block + tile * 16, 16)
                        re, im = times((half_ref[0, tile_rows, at], half_ref[1, tile_rows, at]), turn)
                        residue = 2 * pair + low + 8 * high
                        moved_ref[residue, rows_at, re_lanes] = re.astype(jnp.bfloat16)
                        moved_ref[residue, rows_at, im_lanes] = im.astype(jnp.bfloat16)

        halves = half_refs
        mix_pair(0, halves[0])
        for pair in range(1, eighth // 2):
            mix_pair(pair, halves[pair % 2])
            turn_pair(pair - 1, halves[(pair - 1) % 2])
        turn_pair(eighth // 2 - 1, halves[(eighth // 2 - 1) % 2])

    def load_group(group):
        if twice:

            @pl.when(group > 0)
            def _():
                copy = pltpu.make_async_copy(more_ref, later_ref, later_sem_ref)
                copy.start()
                copy.wait()

        for part in range(group_chunks):
            polarized = pl.ds(part * pol_step, pol_step)
            span = pol_step * GROUP
            for peer in range(slabs):
                rows_at = pl.ds(peer * span, span)

                @pl.when(group == 0)
                def _(part=part, polarized=polarized, peer=peer, rows_at=rows_at):
                    bundle_ref[part, rows_at] = first_refs[peer][polarized].reshape(span, -1)

                if twice:

                    @pl.when(group > 0)
                    def _(part=part, polarized=polarized, peer=peer, rows_at=rows_at):
                        bundle_ref[part, rows_at] = later_ref[peer, polarized].reshape(span, -1)

            load_phases(group, part)

    def copy_out(block, step):
        x_at = pl.ds(pl.multiple_of(block * x_block + step * out_rows, 8), out_rows)
        return pltpu.make_async_copy(out_ref.at[step], sky_ref.at[:, x_at], sem_ref.at[step])

    def one_block(block, carry):
        def one_group(group, inner):
            @pl.when((block == 0) | (groups > 1))
            def _():
                load_group(group)

            def one_part(part, innermost):
                move_rows(group, part, block)
                return innermost

            lax.fori_loop(0, group_chunks, one_part, 0)

            @pl.when(group == 0)
            def _():
                def one_residue(residue, innermost):
                    sum_ref[residue] = jnp.dot(
                        moved_ref[residue], phase_ref[residue], preferred_element_type=jnp.float32
                    )
                    return innermost

                lax.fori_loop(0, SUB, one_residue, 0, unroll=16)

            @pl.when(group > 0)
            def _():
                def one_residue(residue, innermost):
                    sum_ref[residue] += jnp.dot(
                        moved_ref[residue], phase_ref[residue], preferred_element_type=jnp.float32
                    )
                    return innermost

                lax.fori_loop(0, SUB, one_residue, 0)

            return inner

        lax.fori_loop(0, groups, one_group, 0)

        def one_step(step, inner):
            @pl.when(block > 0)
            def _():
                copy_out(block - 1, step).wait()

            def one_tile(tile, innermost):
                rows_at = pl.ds(pl.multiple_of(step * out_rows + tile * 8, 8), 8)
                for second in range(4):
                    parts = []
                    for first in range(8):
                        residue = 4 * first + second
                        parts.append((sum_ref[residue, rows_at, :LANES], sum_ref[residue, rows_at, LANES:]))
                    for first, value in enumerate(dft_8(parts, 1)):
                        if first * second:
                            angle = TWO_PI * first * second / SUB
                            value = times(value, (math.cos(angle), math.sin(angle)))
                        stage_ref[second, first, 0] = value[0]
                        stage_ref[second, first, 1] = value[1]
                to_rows = pl.ds(pl.multiple_of(tile * 8, 8), 8)
                for first in range(8):
                    parts = [(stage_ref[second, first, 0], stage_ref[second, first, 1]) for second in range(4)]
                    for second, value in enumerate(dft_4(parts, 1)):
                        lanes = pl.ds((first + 8 * second) * LANES, LANES)
                        out_ref[step, 0, to_rows, lanes] = value[0]
                        out_ref[step, 1, to_rows, lanes] = value[1]
                return innermost

            lax.fori_loop(0, out_rows // 8, one_tile, 0)
            copy_out(block, step).start()
            return inner

        lax.fori_loop(0, out_steps, one_step, 0)
        return carry

    lax.fori_loop(0, x_blocks, one_block, 0)
    for step in range(out_steps):
        copy_out(x_blocks - 1, step).wait()


def mix_kernel(scale, base_ref, sub_ref, turn_ref, mix_ref, twist_ref):
    x_block = mix_ref.shape[2] // 4
    highest = lax.Precision.HIGHEST
    cell = lax.broadcasted_iota(jnp.int32, (x_block, LANES), 1)

    def one_block(block, carry):
        x_index = lax.broadcasted_iota(jnp.int32, (x_block, LANES), 0) + (base_ref[0] + block * x_block)
        line_re, line_im = cos_sin_turns(jnp.bitwise_and(x_index * cell, G - 1).astype(jnp.float32) * (1.0 / G))
        by_re = jnp.dot(line_re, sub_ref[...], precision=highest, preferred_element_type=jnp.float32)
        by_im = jnp.dot(line_im, sub_ref[...], precision=highest, preferred_element_type=jnp.float32)
        core = (by_re[:, :LANES] - by_im[:, LANES:], by_re[:, LANES:] + by_im[:, :LANES])
        for rho in range(4):
            re, im = times(core, (turn_ref[rho : rho + 1], turn_ref[4 + rho : 5 + rho]))
            rows_at = pl.ds(rho * x_block, x_block)
            mix_ref[block, 0, rows_at, :LANES] = re.astype(jnp.bfloat16)
            mix_ref[block, 0, rows_at, LANES:] = (-im).astype(jnp.bfloat16)
            mix_ref[block, 1, rows_at, :LANES] = im.astype(jnp.bfloat16)
            mix_ref[block, 1, rows_at, LANES:] = re.astype(jnp.bfloat16)
        return carry

    lax.fori_loop(0, mix_ref.shape[0], one_block, 0)
    residue = lax.broadcasted_iota(jnp.int32, (SUB, LANES), 0)
    angle = residue * lax.broadcasted_iota(jnp.int32, (SUB, LANES), 1) + jnp.bitwise_and(residue, 1) * (G // 2)
    re, im = cos_sin_turns(angle.astype(jnp.float32) * (1.0 / G))
    twist_ref[:SUB] = re * scale
    twist_ref[SUB:] = im * scale


def mix_table(x_base, x_count, x_block, scale):
    cells, pixels = np.arange(LANES)[:, None], np.arange(LANES)[None, :] % SUB
    angle = -2.0 * np.pi * ((cells - SUB // 2) * (pixels - SUB // 2) % SUB) / SUB
    used = cells < SUB
    sub = np.concatenate([np.where(used, np.cos(angle), 0.0), np.where(used, np.sin(angle), 0.0)], axis=1)
    turn = (np.arange(4)[:, None] * (np.arange(LANES)[None, :] // SUB)) % 4
    turns = np.concatenate([np.array([1.0, 0.0, -1.0, 0.0])[turn], np.array([0.0, -1.0, 0.0, 1.0])[turn]])
    smem = pl.BlockSpec(memory_space=pltpu.SMEM)
    vmem = pl.BlockSpec(memory_space=pltpu.VMEM)
    return pl.pallas_call(
        functools.partial(mix_kernel, scale),
        out_shape=[
            jax.ShapeDtypeStruct((x_count // x_block, 2, 4 * x_block, 2 * LANES), jnp.bfloat16),
            jax.ShapeDtypeStruct((2 * SUB, LANES), jnp.float32),
        ],
        in_specs=[smem, vmem, vmem],
        out_specs=[vmem, vmem],
        cost_estimate=pl.CostEstimate(flops=1 << 30, bytes_accessed=1 << 22, transcendentals=0),
        compiler_params=pltpu.CompilerParams(vmem_limit_bytes=16 * 1024 * 1024),
        name="mix",
    )(x_base, jnp.asarray(sub, jnp.float32), jnp.asarray(turns, jnp.float32))


def image_of(groups, x_base, first, more, rows, cols, mix, x_count, x_block, pol_step):
    out_rows = min(x_block, 64)
    parts = 4 // pol_step
    slabs = len(first)
    smem = pl.BlockSpec(memory_space=pltpu.SMEM)
    vmem = pl.BlockSpec(memory_space=pltpu.VMEM)
    hbm = pl.BlockSpec(memory_space=pl.ANY)
    return pl.pallas_call(
        functools.partial(image_kernel, pol_step, x_block, slabs, bool(more)),
        out_shape=jax.ShapeDtypeStruct((2, x_count, G), jnp.float32),
        in_specs=[smem, smem] + [vmem] * (4 + slabs) + [hbm] * len(more),
        out_specs=hbm,
        scratch_shapes=[
            pltpu.VMEM((parts, LANES, 2 * SUB * SUB), jnp.bfloat16),
            pltpu.VMEM((SUB, parts * 2 * LANES, 2 * LANES), jnp.bfloat16),
            pltpu.VMEM((2, x_block, LANES), jnp.float32),
            pltpu.VMEM((2, 4 * x_block, 2 * LANES), jnp.float32),
            pltpu.VMEM((2, 4 * x_block, 2 * LANES), jnp.float32),
            pltpu.VMEM((SUB, x_block, parts * 2 * LANES), jnp.bfloat16),
            pltpu.VMEM((SUB, x_block, 2 * LANES), jnp.float32),
            pltpu.VMEM((4, 8, 2, 8, LANES), jnp.float32),
            pltpu.VMEM((x_block // out_rows, 2, out_rows, G), jnp.float32),
            pltpu.VMEM((slabs if more else 1,) + first[0].shape, first[0].dtype),
            pltpu.SemaphoreType.DMA((x_block // out_rows,)),
            pltpu.SemaphoreType.DMA,
        ],
        compiler_params=pltpu.CompilerParams(vmem_limit_bytes=46 * 1024 * 1024),
        name="image",
    )(groups, x_base, rows, cols, *mix, *first, *more)


def exchanged(value, axis, distance):
    peers = lax.axis_size(axis)
    return lax.ppermute(value, axis, [(i, i ^ distance) for i in range(peers)])


def gathered(pieces, beside=None):
    slabs = lax.axis_size("slab")
    value = jnp.stack([pieces[0]] + [exchanged(piece, "pol", k) for k, piece in enumerate(pieces) if k])
    planes = [value] + [exchanged(value, "slab", k) for k in range(2, slabs, 2)]
    made = None
    if beside is not None:
        made = beside(value)
        planes[-1], made = lax.optimization_barrier((planes[-1], made))
    values = []
    for plane in planes:
        values += [plane, exchanged(plane, "slab", 1)]
    return values, made


def in_image_domain(correlations, tracks, vis_counts, offsets, held_counts, pixel_weight):
    pols, slabs = lax.axis_size("pol"), lax.axis_size("slab")
    pol, slab = lax.axis_index("pol"), lax.axis_index("slab")
    devices = pols * slabs
    capacity = SLOTS * slabs // devices
    x_count = G // slabs
    held = held_counts.astype(jnp.int32)
    holders = jnp.arange(slabs, dtype=jnp.int32)
    where_at = jnp.stack([slab, pol]).astype(jnp.int32)
    sent = packed(held, where_at, vis_counts.reshape(1, SLOTS), correlations[:, 0], tracks, devices)
    slots = lax.all_to_all(sent, ("pol", "slab"), 0, 0, tiled=True)
    held, _ = lax.optimization_barrier((held, sent))
    before = jnp.sum(jnp.where(holders[None, :] < holders[:, None], held[None, :], 0), axis=1)
    total = jnp.sum(held)

    slot = jnp.arange(SLOTS, dtype=jnp.int32)
    order = jnp.where(slot[None, :] < held[:, None], before[:, None] + slot[None, :], -1).reshape(-1)
    device_at, seat_at = order % devices, order // devices
    pol_step = LANES // (GROUP * slabs)
    lane_order = (device_at % slabs) ^ slab
    pol_order = (device_at // slabs) ^ pol
    place = (seat_at // GROUP) * (pols // pol_step) + pol_order // pol_step
    place = place * LANES + lane_order * (pol_step * GROUP) + pol_order % pol_step * GROUP + seat_at % GROUP
    place = jnp.where(order >= 0, place, -1)
    chunk_count = capacity // GROUP * (pols // pol_step)
    spots = jnp.arange(chunk_count * LANES, dtype=jnp.int32)
    chosen = spots[:, None] == place[None, :]
    rows = jnp.sum(jnp.where(chosen, offsets[0][None, :], 0), axis=1).reshape(chunk_count, LANES)
    cols = jnp.sum(jnp.where(chosen, offsets[1][None, :], 0), axis=1).reshape(chunk_count, LANES)
    slots, rows, cols = lax.optimization_barrier((slots, rows, cols))
    weight_row = pixel_weight.reshape(1, SUB * SUB)
    *pieces, extra = subgrids_of(held, where_at, offsets.astype(jnp.int32), slots, weight_row, capacity)
    norm_scale = 1.0 / (SUB * SUB * math.sqrt(VIS * SLOTS * slabs / 8.0))
    x_base = (slab * x_count).reshape(1)
    x_block = min(x_count, 256)

    def mixed(after):
        base, _ = lax.optimization_barrier((x_base, after))
        return mix_table(base, x_count, x_block, norm_scale)

    first, mix = gathered(pieces, mixed)
    many = total > devices * GROUP

    def image(groups, more):
        groups = jnp.full((1,), groups, jnp.int32)
        return image_of(groups, x_base, first, more, rows, cols, mix, x_count, x_block, pol_step)

    def image_of_all():
        more = jnp.stack(gathered([extra[k] for k in range(pols)])[0])
        return image(capacity // GROUP, [more])

    sky = lax.cond(many, image_of_all, lambda: image(1, []))
    return sky[:, None]


def fits_image_domain(mesh):
    pols, slabs = mesh.shape["pol"], mesh.shape["slab"]
    devices = pols * slabs
    whole = slabs & (slabs - 1) == 0 and slabs * GROUP <= LANES and SLOTS * slabs == 2 * GROUP * devices
    return whole and pols == 4 and SLOTS == WAVES * devices and pols % (LANES // (GROUP * slabs)) == 0


def solution(mesh):
    in_specs = (P(None, "pol", "slab", None), P(None, "slab", None), P("slab"), P(), P(), P())
    out_specs = P(None, "pol", "slab", None)
    body = in_image_domain if fits_image_domain(mesh) else on_device
    return jax.shard_map(body, mesh=mesh, in_specs=in_specs, out_specs=out_specs, check_vma=False)
```

```python
import functools
import math

import jax
import jax.numpy as jnp
import numpy as np
from jax import lax
from jax.experimental import pallas as pl
from jax.experimental.pallas import tpu as pltpu
from jax.sharding import PartitionSpec as P

G = 4096
SUB = 32
VIS = 256
SLOTS = 64


TWO_PI = 2.0 * math.pi
FIELD_VIEW = 0.6
DEPTH_SCALE = 40.0
TRACK_SCALE = 0.375
COEF_REAL = np.array(
    [[0.5, 0.0, 0.0, 0.5], [0.5, 0.0, 0.0, -0.5], [0.0, 0.5, 0.5, 0.0], [0.0, 0.0, 0.0, 0.0]],
    np.float32,
)
COEF_IMAG = np.array(
    [[0.0, 0.0, 0.0, 0.0], [0.0, 0.0, 0.0, 0.0], [0.0, 0.0, 0.0, 0.0], [0.0, -0.5, 0.5, 0.0]],
    np.float32,
)


def partner_2(value, axis, distance):
    return lax.ppermute(value, axis, [(i, i ^ 1 << distance) for i in range(lax.axis_size(axis))])


def passed_along(value, axis, by):
    peers = lax.axis_size(axis)
    pairs = [(i, i + by) for i in range(peers) if 0 <= i + by < peers]
    return lax.ppermute(value, axis, pairs)


def pixel_tables():
    cells = jnp.arange(SUB * SUB, dtype=jnp.int32)
    row_pos = (cells // SUB - SUB // 2).astype(jnp.float32) / SUB
    col_pos = (cells % SUB - SUB // 2).astype(jnp.float32) / SUB
    depth = jnp.sqrt(1.0 - (FIELD_VIEW * col_pos) ** 2 - (FIELD_VIEW * row_pos) ** 2) - 1.0
    return (col_pos, row_pos, depth)


def phasor_table(track_set, tables):
    col_pos, row_pos, depth = tables
    u_cells = track_set[0] * (TRACK_SCALE * SUB)
    v_cells = track_set[1] * (TRACK_SCALE * SUB)
    w_cells = track_set[2] * DEPTH_SCALE
    phase = TWO_PI * (
        u_cells[:, None] * col_pos[None, :]
        + v_cells[:, None] * row_pos[None, :]
        + w_cells[:, None] * depth[None, :]
    )
    return jnp.concatenate([jnp.cos(phase), jnp.sin(phase)], axis=1).astype(jnp.bfloat16)


def subgrid_tables():
    positions = jnp.arange(SUB, dtype=jnp.int32) - SUB // 2
    turn_count = positions[:, None] * positions[None, :] % SUB
    angles = -TWO_PI * turn_count.astype(jnp.float32) / SUB
    return (jnp.cos(angles), jnp.sin(angles))


def dft_table(length):
    positions = jnp.arange(length, dtype=jnp.int32)
    turn_count = positions[:, None] * positions[None, :] % length
    angles = TWO_PI * turn_count.astype(jnp.float32) / length
    return (jnp.cos(angles), jnp.sin(angles))


def twiddle_table(first_len, second_len, length):
    first_pos = jnp.arange(first_len, dtype=jnp.int32)
    second_pos = jnp.arange(second_len, dtype=jnp.int32)
    turn_count = first_pos[:, None] * second_pos[None, :] % length
    angles = TWO_PI * turn_count.astype(jnp.float32) / length
    return (jnp.cos(angles), jnp.sin(angles))


def complex_einsum(pattern, left_pair, right_pair):
    highest = lax.Precision.HIGHEST
    left_re, left_im = left_pair
    right_re, right_im = right_pair
    real_part = jnp.einsum(pattern, left_re, right_re, precision=highest) - jnp.einsum(
        pattern, left_im, right_im, precision=highest
    )
    imag_part = jnp.einsum(pattern, left_re, right_im, precision=highest) + jnp.einsum(
        pattern, left_im, right_re, precision=highest
    )
    return (real_part, imag_part)


def complex_multiply(data_pair, table_pair):
    data_re, data_im = data_pair
    table_re, table_im = table_pair
    return (data_re * table_re - data_im * table_im, data_re * table_im + data_im * table_re)


def subgrid_transform(sub_re, sub_im, dft_pair):
    half_re, half_im = complex_einsum("...ij,cj->...ic", (sub_re, sub_im), dft_pair)
    return complex_einsum("ai,...ic->...ac", dft_pair, (half_re, half_im))


def place_blocks(window, blocks, row_starts, col_starts):
    block_count = blocks.shape[1]
    zero_index = jnp.zeros((), jnp.int32)

    def add_one(slot_index, current_window):
        block = lax.dynamic_index_in_dim(blocks, slot_index, 1, keepdims=False)
        corner = (zero_index, row_starts[slot_index], col_starts[slot_index])
        current = lax.dynamic_slice(current_window, corner, (2, SUB, SUB))
        return lax.dynamic_update_slice(current_window, current + block, corner)

    return lax.fori_loop(0, block_count, add_one, window)


def on_device(correlations, tracks, vis_counts, offsets, held_counts, pixel_weight):
    highest = lax.Precision.HIGHEST
    slab_count = lax.axis_size("slab")
    slab_index = lax.axis_index("slab")
    stokes_index = lax.axis_index("pol")
    pixel_area = SUB * SUB
    rows_local = G // slab_count
    tables = pixel_tables()
    dft_pair = subgrid_tables()
    gathered = lax.all_gather(correlations, "pol", axis=1, tiled=True)
    corr_float = gathered.astype(jnp.float32)
    select = (jnp.arange(4, dtype=jnp.int32) == stokes_index).astype(jnp.float32)
    coef_re = jnp.sum(select[:, None] * jnp.asarray(COEF_REAL), axis=0)
    coef_im = jnp.sum(select[:, None] * jnp.asarray(COEF_IMAG), axis=0)
    stokes_re = jnp.einsum("p,pnv->nv", coef_re, corr_float[0], precision=highest) - jnp.einsum(
        "p,pnv->nv", coef_im, corr_float[1], precision=highest
    )
    stokes_im = jnp.einsum("p,pnv->nv", coef_re, corr_float[1], precision=highest) + jnp.einsum(
        "p,pnv->nv", coef_im, corr_float[0], precision=highest
    )
    visible = (jnp.arange(VIS, dtype=jnp.int32)[None, :] < vis_counts[:, None]).astype(jnp.bfloat16)
    stokes_vis = jnp.stack([stokes_re, stokes_im]).astype(jnp.bfloat16) * visible[None]
    holder_ids = jnp.arange(slab_count, dtype=jnp.int32)
    own_held = jnp.sum(jnp.where(holder_ids == slab_index, held_counts, 0))

    def grid_range(vis_set, track_set, first_slot, stop_slot, capacity):

        def one_slot(slot_index, subgrid_set):
            phasor = phasor_table(
                lax.dynamic_index_in_dim(track_set, slot_index, 1, keepdims=False), tables
            )
            vis_slot = lax.dynamic_index_in_dim(vis_set, slot_index, 1, keepdims=False)
            product = jnp.dot(vis_slot, phasor, preferred_element_type=jnp.float32)
            sub_re = product[0, :pixel_area] - product[1, pixel_area:]
            sub_im = product[0, pixel_area:] + product[1, :pixel_area]
            update = jnp.stack([sub_re, sub_im])[:, None, :]
            return lax.dynamic_update_slice_in_dim(subgrid_set, update, slot_index, 1)

        zero_set = jnp.zeros((2, capacity, pixel_area), jnp.float32)
        return lax.fori_loop(first_slot, stop_slot, one_slot, zero_set)

    half_slots = SLOTS // 2
    swap_bit = slab_count.bit_length() - 2
    partner = jnp.bitwise_xor(slab_index, slab_count // 2)
    partner_held = jnp.sum(jnp.where(holder_ids == partner, held_counts, 0))
    pair_total = own_held + partner_held
    own_give = jnp.maximum(own_held - (pair_total + 1) // 2, 0)
    partner_give = jnp.maximum(partner_held - (pair_total + 1) // 2, 0)
    own_start = jnp.minimum(own_held - own_give, SLOTS - half_slots)
    partner_start = jnp.minimum(partner_held - partner_give, SLOTS - half_slots)
    send_vis = lax.dynamic_slice_in_dim(stokes_vis, own_start, half_slots, 1).astype(jnp.float32)
    send_track = lax.dynamic_slice_in_dim(tracks, own_start, half_slots, 1)
    got_vis, got_track = partner_2((send_vis, send_track), "slab", swap_bit)
    first_slot = partner_held - partner_give - partner_start
    helped = grid_range(
        got_vis.astype(jnp.bfloat16), got_track, first_slot, first_slot + partner_give, half_slots
    )
    returned_set = partner_2(helped, "slab", swap_bit)
    own_part = grid_range(stokes_vis, tracks, 0, own_held - own_give, SLOTS)
    subgrids = own_part + lax.dynamic_update_slice_in_dim(
        jnp.zeros_like(own_part), returned_set, own_start, 1
    )
    weight_flat = pixel_weight.reshape(pixel_area)
    sub_re = (subgrids[0] * weight_flat).reshape(SLOTS, SUB, SUB)
    sub_im = (subgrids[1] * weight_flat).reshape(SLOTS, SUB, SUB)
    uv_re, uv_im = subgrid_transform(sub_re, sub_im, dft_pair)
    uv_blocks = jnp.stack([uv_re, uv_im])
    own_offsets = lax.dynamic_slice_in_dim(offsets, slab_index * SLOTS, SLOTS, 1)
    own_rows = own_offsets[0] - slab_index * rows_local
    own_cols = own_offsets[1]
    window = jnp.zeros((2, rows_local + SUB, G), jnp.float32)
    window = place_blocks(window, uv_blocks, own_rows, own_cols)
    lower_rows = passed_along(window[:, rows_local:], "slab", 1)
    slab_grid = window[:, :rows_local].at[:, :SUB].add(lower_rows)
    small_side = G // 128
    large_side = 128
    table_small = dft_table(small_side)
    table_large = dft_table(large_side)
    twiddle = twiddle_table(small_side, large_side, G)
    plane_re = slab_grid[0].reshape(rows_local, small_side, large_side)
    plane_im = slab_grid[1].reshape(rows_local, small_side, large_side)
    step_re, step_im = complex_einsum("rkc,kx->rxc", (plane_re, plane_im), table_small)
    step_re, step_im = complex_multiply((step_re, step_im), twiddle)
    step_re, step_im = complex_einsum("rxc,cb->bxr", (step_re, step_im), table_large)
    moved_block = lax.all_to_all(
        jnp.stack([step_re, step_im]), "slab", split_axis=1, concat_axis=3, tiled=True
    )
    line_re = moved_block[0].reshape(rows_local, large_side, small_side)
    line_im = moved_block[1].reshape(rows_local, large_side, small_side)
    line_re, line_im = complex_einsum("xab,ay->xby", (line_re, line_im), table_large)
    line_re, line_im = complex_multiply((line_re, line_im), twiddle)
    line_re, line_im = complex_einsum("xby,bz->xzy", (line_re, line_im), table_small)
    norm_scale = 1.0 / (SUB * SUB * math.sqrt(VIS * SLOTS * slab_count / 8.0))
    sky_re = line_re.reshape(rows_local, G) * norm_scale
    sky_im = line_im.reshape(rows_local, G) * norm_scale
    return jnp.stack([sky_re, sky_im])[:, None]


LANES = 128
GROUP = 8


def turn_polynomials():
    z = np.cos(np.linspace(0.0, np.pi, 4001)) * 0.125 + 0.125
    r = np.sqrt(z)
    sine = np.where(r > 0, np.sin(np.pi * r) / np.where(r > 0, r, 1.0), np.pi)
    fits = []
    for values in (sine, np.cos(np.pi * r)):
        fit = np.polynomial.chebyshev.Chebyshev.fit(z, values, 4, domain=[0.0, 0.25])
        fits.append([float(v) for v in fit.convert(kind=np.polynomial.Polynomial).coef])
    return fits


SINE_COEF, COSINE_COEF = turn_polynomials()


def cos_sin_turns(turns):
    rest = turns - jnp.floor(turns + 0.5)
    square = rest * rest
    sine = SINE_COEF[-1]
    cosine = COSINE_COEF[-1]
    for coef in SINE_COEF[-2::-1]:
        sine = sine * square + coef
    for coef in COSINE_COEF[-2::-1]:
        cosine = cosine * square + coef
    sine = sine * rest
    double = sine + sine
    return 1.0 - double * sine, double * cosine


def times(left, right):
    return (left[0] * right[0] - left[1] * right[1], left[0] * right[1] + left[1] * right[0])


def plus(left, right):
    return (left[0] + right[0], left[1] + right[1])


def minus(left, right):
    return (left[0] - right[0], left[1] - right[1])


def quarter(value, sign):
    if sign > 0:
        return (-value[1], value[0])
    return (value[1], -value[0])


def dft_4(values, sign):
    a, b, c, d = values
    even_sum, even_diff = plus(a, c), minus(a, c)
    odd_sum, odd_diff = plus(b, d), quarter(minus(b, d), sign)
    return [plus(even_sum, odd_sum), plus(even_diff, odd_diff), minus(even_sum, odd_sum), minus(even_diff, odd_diff)]


ROOT_HALF = math.sqrt(0.5)


def dft_8(values, sign):
    even = dft_4(values[0::2], sign)
    odd = dft_4(values[1::2], sign)
    a, b = odd[1]
    odd[1] = ((a - b) * ROOT_HALF, (a + b) * ROOT_HALF) if sign > 0 else ((a + b) * ROOT_HALF, (b - a) * ROOT_HALF)
    odd[2] = quarter(odd[2], sign)
    a, b = odd[3]
    odd[3] = ((-a - b) * ROOT_HALF, (a - b) * ROOT_HALF) if sign > 0 else ((b - a) * ROOT_HALF, (-a - b) * ROOT_HALF)
    return [plus(e, o) for e, o in zip(even, odd)] + [minus(e, o) for e, o in zip(even, odd)]


def pixel_rows():
    row, col = np.divmod(np.arange(SUB * SUB), SUB)
    l = ((col - SUB // 2) / SUB).astype(np.float32)
    m = ((row - SUB // 2) / SUB).astype(np.float32)
    view = np.float32(FIELD_VIEW)
    n = (np.sqrt(np.float32(1.0) - (view * l) ** 2 - (view * m) ** 2) - np.float32(1.0)).astype(np.float32)
    return np.stack([l, m, n, row.astype(np.float32)] + [np.zeros_like(l)] * 4).astype(np.float32)


HALVES = VIS // LANES
WAVES = 2
TRACK_ROWS = WAVES * 3 * HALVES


def pack_kernel(held_ref, place_ref, counts_ref, corr_ref, track_ref, out_ref):
    devices = out_ref.shape[0]
    slab, pol = place_ref[0], place_ref[1]

    def count_before(holder, total):
        return total + jnp.where(holder < slab, held_ref[holder], 0)

    shift = jnp.bitwise_and(lax.fori_loop(0, held_ref.shape[0], count_before, 0), devices - 1)
    counts = jnp.transpose(jnp.broadcast_to(counts_ref[...].astype(jnp.float32), (LANES, counts_ref.shape[1])))
    lane = lax.broadcasted_iota(jnp.int32, (devices, LANES), 1).astype(jnp.float32)
    rows = []
    for wave in range(WAVES):
        at = pl.ds(wave * devices, devices)
        for c in range(2):
            for half in range(HALVES):
                value = corr_ref[c, at, pl.ds(half * LANES, LANES)].astype(jnp.float32)
                limit = counts[wave * devices : (wave + 1) * devices] - float(half * LANES)
                rows.append(jnp.where(lane < limit, value, 0.0))
    piece = TRACK_ROWS // 4
    for row in range(piece):
        value = None
        for sender in range(4):
            wave, axis, half = np.unravel_index(sender * piece + row, (WAVES, 3, HALVES))
            part = track_ref[int(axis), pl.ds(int(wave) * devices, devices), pl.ds(int(half) * LANES, LANES)]
            value = part if value is None else jnp.where(pol == sender, part, value)
        rows.append(value)
    for row, value in enumerate(rows):
        out_ref[:, row, :] = pltpu.roll(value, shift, 0)
    for row in range(len(rows), out_ref.shape[1]):
        out_ref[:, row, :] = jnp.zeros((devices, LANES), jnp.float32)


def packed(held, place, counts, corr, tracks, devices):
    smem = pl.BlockSpec(memory_space=pltpu.SMEM)
    vmem = pl.BlockSpec(memory_space=pltpu.VMEM)
    return pl.pallas_call(
        pack_kernel,
        out_shape=jax.ShapeDtypeStruct((devices, 16, LANES), jnp.float32),
        in_specs=[smem, smem, vmem, vmem, vmem],
        out_specs=vmem,
        name="packed",
    )(held, place, counts, corr, tracks)


def row_twiddles():
    angle = -2.0 * np.pi * np.arange(8)[:, None] * (np.arange(LANES)[None, :] // SUB) / SUB
    return np.concatenate([np.cos(angle), np.sin(angle)], axis=0).astype(np.float32)


def subgrid_kernel(held_counts_ref, place_ref, offsets_ref, slots_ref, table_ref, twiddle_ref, weight_ref, *refs):
    piece_refs, more_ref, held_ref = refs[:4], refs[4], refs[5]
    held_ref[...] = jnp.zeros_like(held_ref)
    slab, pol = place_ref[0], place_ref[1]
    slabs = slots_ref.shape[0] // 4
    devices = slots_ref.shape[0]
    own = pol * slabs + slab
    total = lax.fori_loop(0, slabs, lambda holder, value: value + held_counts_ref[holder], 0)
    count = lax.shift_right_logical(total - own + (devices - 1), devices.bit_length() - 1)

    def locate(index):
        wanted = index * devices + own

        def look(holder, found):
            before, at_holder, at_slot = found
            after = before + held_counts_ref[holder]
            inside = (wanted >= before) & (wanted < after)
            return after, jnp.where(inside, holder, at_holder), jnp.where(inside, wanted - before, at_slot)

        _, at_holder, at_slot = lax.fori_loop(0, slabs, look, (0, 0, 0))
        return at_holder, at_slot

    def one_slot(index, carry):
        holder, slot = locate(index)
        early = slot < devices
        row_start = jnp.bitwise_and(offsets_ref[0, holder * SLOTS + slot], SUB - 1).astype(jnp.float32)
        tiles = [slots_ref[p * slabs + holder] for p in range(4)]
        xx, xy, yx, yy = [0.5 * jnp.where(early, tile[0:4], tile[4:8]) for tile in tiles]
        turned = xy - yx
        parameters = [xx + yy, xx - yy, xy + yx, jnp.concatenate([turned[2:4], -turned[0:2]], axis=0)]
        chosen = []
        for k in range(4):
            value = parameters[k]
            for other in range(1, 4):
                value = jnp.where(pol == other, parameters[k ^ other], value)
            chosen.append(value)
        halves = [
            jnp.concatenate([chosen[k][2 * c + half : 2 * c + half + 1] for c in range(2) for k in range(4)], axis=0)
            for half in range(2)
        ]
        vis = jnp.concatenate(halves, axis=1).astype(jnp.bfloat16)

        def track_half(axis, half):
            found = []
            for wave in range(WAVES):
                sender, row = divmod((wave * 3 + axis) * HALVES + half, TRACK_ROWS // 4)
                found.append(tiles[sender][8 + row : 9 + row])
            return jnp.where(early, found[0], found[1])

        track = jnp.concatenate(
            [jnp.concatenate([track_half(axis, half) for half in range(2)], axis=1) for axis in (0, 1, 2, 2, 2, 2, 2, 2)], axis=0
        )
        track = jnp.transpose(track)
        shape = (VIS, LANES)
        u = jnp.broadcast_to(track[:, 0:1] * (TRACK_SCALE * SUB), shape)
        v = jnp.broadcast_to(track[:, 1:2] * (TRACK_SCALE * SUB), shape)
        w = jnp.broadcast_to(track[:, 2:3] * DEPTH_SCALE, shape)
        placed = []
        for tile in range(SUB * SUB // LANES):
            lanes = pl.ds(tile * LANES, LANES)
            turns = u * table_ref[0:1, lanes] + v * table_ref[1:2, lanes] + w * table_ref[2:3, lanes]
            cosine, sine = cos_sin_turns(turns)
            phasor = jnp.concatenate([cosine.astype(jnp.bfloat16), sine.astype(jnp.bfloat16)], axis=1)
            product = jnp.dot(vis, phasor, preferred_element_type=jnp.float32)
            real = product[:4, :LANES] - product[4:, LANES:]
            imag = product[:4, LANES:] + product[4:, :LANES]
            weight = weight_ref[0:1, lanes]
            pixel_row = table_ref[3:4, lanes]
            turn = (row_start * (pixel_row - SUB // 2) + pixel_row * (SUB // 2)) * (1.0 / SUB)
            turn_re, turn_im = cos_sin_turns(turn)
            turn_re, turn_im = turn_re * weight, turn_im * weight
            placed.append(times((real, imag), (turn_re, turn_im)))
        for rho, value in enumerate(dft_8(placed, -1)):
            if rho:
                value = times(value, (twiddle_ref[rho : rho + 1], twiddle_ref[8 + rho : 9 + rho]))
            held_ref[index, :, pl.ds(2 * rho * LANES, LANES)] = value[0]
            held_ref[index, :, pl.ds((2 * rho + 1) * LANES, LANES)] = value[1]
        return carry

    lax.fori_loop(0, count, one_slot, 0)
    for k in range(4):
        piece_refs[k][...] = held_ref[:GROUP, k, :].astype(jnp.bfloat16)
        more_ref[k] = held_ref[GROUP:, k, :].astype(jnp.bfloat16)


def subgrids_of(held, place, offsets, slots, weight_row, capacity):
    smem = pl.BlockSpec(memory_space=pltpu.SMEM)
    vmem = pl.BlockSpec(memory_space=pltpu.VMEM)
    return pl.pallas_call(
        subgrid_kernel,
        out_shape=[jax.ShapeDtypeStruct((GROUP, 2 * SUB * SUB), jnp.bfloat16)] * 4
        + [jax.ShapeDtypeStruct((4, capacity - GROUP, 2 * SUB * SUB), jnp.bfloat16)],
        in_specs=[smem] * 3 + [vmem] * 4,
        out_specs=[vmem] * 5,
        scratch_shapes=[pltpu.VMEM((capacity, 4, 2 * SUB * SUB), jnp.float32)],
        name="subgrids",
    )(held, place, offsets, slots, jnp.asarray(pixel_rows()), jnp.asarray(row_twiddles()), weight_row)


def image_kernel(pol_step, x_block, slabs, twice, groups_ref, base_ref, row_ref, col_ref, mix_ref, twist_ref, *refs):
    first_refs, more_ref = refs[:slabs], refs[slabs]
    refs = refs[slabs + twice :]
    sky_ref = refs[0]
    bundle_ref, phase_ref, col_phase_ref, *half_refs, moved_ref, sum_ref, stage_ref, out_ref = refs[1:-3]
    later_ref, sem_ref, later_sem_ref = refs[-3:]
    x_blocks = sky_ref.shape[1] // x_block
    groups = groups_ref[0] if twice else 1
    lane_index = lax.broadcasted_iota(jnp.int32, (LANES, LANES), 1)
    eighth = SUB // 4
    out_rows = out_ref.shape[2]
    out_steps = x_block // out_rows
    group_chunks = 4 // pol_step
    depth = 2 * LANES

    def load_phases(group, part):
        chunk = group * group_chunks + part
        rows = jnp.transpose(jnp.broadcast_to(row_ref[pl.ds(chunk, 1), :].astype(jnp.float32), (LANES, LANES)))
        rows = rows.astype(jnp.int32)
        high = lax.shift_right_logical(rows, 5)
        low = jnp.bitwise_and(rows, SUB - 1)
        here = cos_sin_turns(jnp.bitwise_and(high * lane_index, LANES - 1).astype(jnp.float32) * (1.0 / LANES))
        later = cos_sin_turns(jnp.bitwise_and((high + 1) * lane_index, LANES - 1).astype(jnp.float32) * (1.0 / LANES))
        re_rows = pl.ds(part * depth, LANES)
        im_rows = pl.ds(part * depth + LANES, LANES)

        def one_phase(residue, inner):
            carried = low > residue
            twist = (twist_ref[pl.ds(residue, 1)], twist_ref[pl.ds(SUB + residue, 1)])
            re, im = times((jnp.where(carried, later[0], here[0]), jnp.where(carried, later[1], here[1])), twist)
            re = re.astype(jnp.bfloat16)
            phase_ref[residue, re_rows, :LANES] = re
            phase_ref[residue, re_rows, LANES:] = im.astype(jnp.bfloat16)
            phase_ref[residue, im_rows, :LANES] = (-im).astype(jnp.bfloat16)
            phase_ref[residue, im_rows, LANES:] = re
            return inner

        lax.fori_loop(0, SUB, one_phase, 0)

    def move_rows(group, part, block):
        chunk = group * group_chunks + part
        cols = col_ref[pl.ds(chunk, 1), :]
        x_index = lax.broadcasted_iota(jnp.int32, (x_block, LANES), 0) + (base_ref[0] + block * x_block)
        turns = jnp.bitwise_and(x_index * cols, G - 1).astype(jnp.float32) * (1.0 / G)
        turn_re, turn_im = cos_sin_turns(turns)
        col_phase_ref[0] = turn_re
        col_phase_ref[1] = turn_im
        re_lanes = pl.ds(pl.multiple_of(part * depth, LANES), LANES)
        im_lanes = pl.ds(pl.multiple_of(part * depth + LANES, LANES), LANES)

        def mix_pair(pair, half_ref):
            wide = jnp.concatenate(
                [
                    bundle_ref[part, :, pl.ds(4 * pair * LANES, depth)],
                    bundle_ref[part, :, pl.ds((4 * pair + 2) * LANES, depth)],
                ],
                axis=0,
            )
            for side in range(2):
                half_ref[side] = lax.dot_general(
                    mix_ref[block, side], wide, (((1,), (1,)), ((), ())), preferred_element_type=jnp.float32
                )

        def turn_pair(pair, half_ref):
            for tile in range(x_block // 16):
                rows_at = pl.ds(tile * 16, 16)
                turn = (col_phase_ref[0, rows_at], col_phase_ref[1, rows_at])
                for low in range(2):
                    at = pl.ds(low * LANES, LANES)
                    for high in range(4):
                        tile_rows = pl.ds(high * x_block + tile * 16, 16)
                        re, im = times((half_ref[0, tile_rows, at], half_ref[1, tile_rows, at]), turn)
                        residue = 2 * pair + low + 8 * high
                        moved_ref[residue, rows_at, re_lanes] = re.astype(jnp.bfloat16)
                        moved_ref[residue, rows_at, im_lanes] = im.astype(jnp.bfloat16)

        halves = half_refs
        mix_pair(0, halves[0])
        for pair in range(1, eighth // 2):
            mix_pair(pair, halves[pair % 2])
            turn_pair(pair - 1, halves[(pair - 1) % 2])
        turn_pair(eighth // 2 - 1, halves[(eighth // 2 - 1) % 2])

    def load_group(group):
        if twice:

            @pl.when(group > 0)
            def _():
                copy = pltpu.make_async_copy(more_ref, later_ref, later_sem_ref)
                copy.start()
                copy.wait()

        for part in range(group_chunks):
            polarized = pl.ds(part * pol_step, pol_step)
            span = pol_step * GROUP
            for peer in range(slabs):
                rows_at = pl.ds(peer * span, span)

                @pl.when(group == 0)
                def _(part=part, polarized=polarized, peer=peer, rows_at=rows_at):
                    bundle_ref[part, rows_at] = first_refs[peer][polarized].reshape(span, -1)

                if twice:

                    @pl.when(group > 0)
                    def _(part=part, polarized=polarized, peer=peer, rows_at=rows_at):
                        bundle_ref[part, rows_at] = later_ref[peer, polarized].reshape(span, -1)

            load_phases(group, part)

    def copy_out(block, step):
        x_at = pl.ds(pl.multiple_of(block * x_block + step * out_rows, 8), out_rows)
        return pltpu.make_async_copy(out_ref.at[step], sky_ref.at[:, x_at], sem_ref.at[step])

    def one_block(block, carry):
        def one_group(group, inner):
            @pl.when((block == 0) | (groups > 1))
            def _():
                load_group(group)

            def one_part(part, innermost):
                move_rows(group, part, block)
                return innermost

            lax.fori_loop(0, group_chunks, one_part, 0)

            @pl.when(group == 0)
            def _():
                def one_residue(residue, innermost):
                    sum_ref[residue] = jnp.dot(
                        moved_ref[residue], phase_ref[residue], preferred_element_type=jnp.float32
                    )
                    return innermost

                lax.fori_loop(0, SUB, one_residue, 0, unroll=16)

            @pl.when(group > 0)
            def _():
                def one_residue(residue, innermost):
                    sum_ref[residue] += jnp.dot(
                        moved_ref[residue], phase_ref[residue], preferred_element_type=jnp.float32
                    )
                    return innermost

                lax.fori_loop(0, SUB, one_residue, 0)

            return inner

        lax.fori_loop(0, groups, one_group, 0)

        def one_step(step, inner):
            @pl.when(block > 0)
            def _():
                copy_out(block - 1, step).wait()

            def one_tile(tile, innermost):
                rows_at = pl.ds(pl.multiple_of(step * out_rows + tile * 8, 8), 8)
                for second in range(4):
                    parts = []
                    for first in range(8):
                        residue = 4 * first + second
                        parts.append((sum_ref[residue, rows_at, :LANES], sum_ref[residue, rows_at, LANES:]))
                    for first, value in enumerate(dft_8(parts, 1)):
                        if first * second:
                            angle = TWO_PI * first * second / SUB
                            value = times(value, (math.cos(angle), math.sin(angle)))
                        stage_ref[second, first, 0] = value[0]
                        stage_ref[second, first, 1] = value[1]
                to_rows = pl.ds(pl.multiple_of(tile * 8, 8), 8)
                for first in range(8):
                    parts = [(stage_ref[second, first, 0], stage_ref[second, first, 1]) for second in range(4)]
                    for second, value in enumerate(dft_4(parts, 1)):
                        lanes = pl.ds((first + 8 * second) * LANES, LANES)
                        out_ref[step, 0, to_rows, lanes] = value[0]
                        out_ref[step, 1, to_rows, lanes] = value[1]
                return innermost

            lax.fori_loop(0, out_rows // 8, one_tile, 0)
            copy_out(block, step).start()
            return inner

        lax.fori_loop(0, out_steps, one_step, 0)
        return carry

    lax.fori_loop(0, x_blocks, one_block, 0)
    for step in range(out_steps):
        copy_out(x_blocks - 1, step).wait()


def mix_kernel(scale, base_ref, sub_ref, turn_ref, mix_ref, twist_ref):
    x_block = mix_ref.shape[2] // 4
    highest = lax.Precision.HIGHEST
    cell = lax.broadcasted_iota(jnp.int32, (x_block, LANES), 1)

    def one_block(block, carry):
        x_index = lax.broadcasted_iota(jnp.int32, (x_block, LANES), 0) + (base_ref[0] + block * x_block)
        line_re, line_im = cos_sin_turns(jnp.bitwise_and(x_index * cell, G - 1).astype(jnp.float32) * (1.0 / G))
        by_re = jnp.dot(line_re, sub_ref[...], precision=highest, preferred_element_type=jnp.float32)
        by_im = jnp.dot(line_im, sub_ref[...], precision=highest, preferred_element_type=jnp.float32)
        core = (by_re[:, :LANES] - by_im[:, LANES:], by_re[:, LANES:] + by_im[:, :LANES])
        for rho in range(4):
            re, im = times(core, (turn_ref[rho : rho + 1], turn_ref[4 + rho : 5 + rho]))
            rows_at = pl.ds(rho * x_block, x_block)
            mix_ref[block, 0, rows_at, :LANES] = re.astype(jnp.bfloat16)
            mix_ref[block, 0, rows_at, LANES:] = (-im).astype(jnp.bfloat16)
            mix_ref[block, 1, rows_at, :LANES] = im.astype(jnp.bfloat16)
            mix_ref[block, 1, rows_at, LANES:] = re.astype(jnp.bfloat16)
        return carry

    lax.fori_loop(0, mix_ref.shape[0], one_block, 0)
    residue = lax.broadcasted_iota(jnp.int32, (SUB, LANES), 0)
    angle = residue * lax.broadcasted_iota(jnp.int32, (SUB, LANES), 1) + jnp.bitwise_and(residue, 1) * (G // 2)
    re, im = cos_sin_turns(angle.astype(jnp.float32) * (1.0 / G))
    twist_ref[:SUB] = re * scale
    twist_ref[SUB:] = im * scale


def mix_table(x_base, x_count, x_block, scale):
    cells, pixels = np.arange(LANES)[:, None], np.arange(LANES)[None, :] % SUB
    angle = -2.0 * np.pi * ((cells - SUB // 2) * (pixels - SUB // 2) % SUB) / SUB
    used = cells < SUB
    sub = np.concatenate([np.where(used, np.cos(angle), 0.0), np.where(used, np.sin(angle), 0.0)], axis=1)
    turn = (np.arange(4)[:, None] * (np.arange(LANES)[None, :] // SUB)) % 4
    turns = np.concatenate([np.array([1.0, 0.0, -1.0, 0.0])[turn], np.array([0.0, -1.0, 0.0, 1.0])[turn]])
    smem = pl.BlockSpec(memory_space=pltpu.SMEM)
    vmem = pl.BlockSpec(memory_space=pltpu.VMEM)
    return pl.pallas_call(
        functools.partial(mix_kernel, scale),
        out_shape=[
            jax.ShapeDtypeStruct((x_count // x_block, 2, 4 * x_block, 2 * LANES), jnp.bfloat16),
            jax.ShapeDtypeStruct((2 * SUB, LANES), jnp.float32),
        ],
        in_specs=[smem, vmem, vmem],
        out_specs=[vmem, vmem],
        cost_estimate=pl.CostEstimate(flops=1 << 30, bytes_accessed=1 << 22, transcendentals=0),
        compiler_params=pltpu.CompilerParams(vmem_limit_bytes=16 * 1024 * 1024),
        name="mix",
    )(x_base, jnp.asarray(sub, jnp.float32), jnp.asarray(turns, jnp.float32))


def image_of(groups, x_base, first, more, rows, cols, mix, x_count, x_block, pol_step):
    out_rows = min(x_block, 64)
    parts = 4 // pol_step
    slabs = len(first)
    smem = pl.BlockSpec(memory_space=pltpu.SMEM)
    vmem = pl.BlockSpec(memory_space=pltpu.VMEM)
    hbm = pl.BlockSpec(memory_space=pl.ANY)
    return pl.pallas_call(
        functools.partial(image_kernel, pol_step, x_block, slabs, bool(more)),
        out_shape=jax.ShapeDtypeStruct((2, x_count, G), jnp.float32),
        in_specs=[smem, smem] + [vmem] * (4 + slabs) + [hbm] * len(more),
        out_specs=hbm,
        scratch_shapes=[
            pltpu.VMEM((parts, LANES, 2 * SUB * SUB), jnp.bfloat16),
            pltpu.VMEM((SUB, parts * 2 * LANES, 2 * LANES), jnp.bfloat16),
            pltpu.VMEM((2, x_block, LANES), jnp.float32),
            pltpu.VMEM((2, 4 * x_block, 2 * LANES), jnp.float32),
            pltpu.VMEM((2, 4 * x_block, 2 * LANES), jnp.float32),
            pltpu.VMEM((SUB, x_block, parts * 2 * LANES), jnp.bfloat16),
            pltpu.VMEM((SUB, x_block, 2 * LANES), jnp.float32),
            pltpu.VMEM((4, 8, 2, 8, LANES), jnp.float32),
            pltpu.VMEM((x_block // out_rows, 2, out_rows, G), jnp.float32),
            pltpu.VMEM((slabs if more else 1,) + first[0].shape, first[0].dtype),
            pltpu.SemaphoreType.DMA((x_block // out_rows,)),
            pltpu.SemaphoreType.DMA,
        ],
        compiler_params=pltpu.CompilerParams(vmem_limit_bytes=46 * 1024 * 1024),
        name="image",
    )(groups, x_base, rows, cols, *mix, *first, *more)


def exchanged(value, axis, distance):
    peers = lax.axis_size(axis)
    return lax.ppermute(value, axis, [(i, i ^ distance) for i in range(peers)])


def gathered(pieces, beside=None):
    slabs = lax.axis_size("slab")
    value = jnp.stack([pieces[0]] + [exchanged(piece, "pol", k) for k, piece in enumerate(pieces) if k])
    planes = [value] + [exchanged(value, "slab", k) for k in range(2, slabs, 2)]
    made = None
    if beside is not None:
        made = beside(value)
        planes[-1], made = lax.optimization_barrier((planes[-1], made))
    values = []
    for plane in planes:
        values += [plane, exchanged(plane, "slab", 1)]
    return values, made


def in_image_domain(correlations, tracks, vis_counts, offsets, held_counts, pixel_weight):
    pols, slabs = lax.axis_size("pol"), lax.axis_size("slab")
    pol, slab = lax.axis_index("pol"), lax.axis_index("slab")
    devices = pols * slabs
    capacity = SLOTS * slabs // devices
    x_count = G // slabs
    held = held_counts.astype(jnp.int32)
    holders = jnp.arange(slabs, dtype=jnp.int32)
    where_at = jnp.stack([slab, pol]).astype(jnp.int32)
    sent = packed(held, where_at, vis_counts.reshape(1, SLOTS), correlations[:, 0], tracks, devices)
    slots = lax.all_to_all(sent, ("pol", "slab"), 0, 0, tiled=True)
    held, _ = lax.optimization_barrier((held, sent))
    before = jnp.sum(jnp.where(holders[None, :] < holders[:, None], held[None, :], 0), axis=1)
    total = jnp.sum(held)

    slot = jnp.arange(SLOTS, dtype=jnp.int32)
    order = jnp.where(slot[None, :] < held[:, None], before[:, None] + slot[None, :], -1).reshape(-1)
    device_at, seat_at = order % devices, order // devices
    pol_step = LANES // (GROUP * slabs)
    lane_order = (device_at % slabs) ^ slab
    pol_order = (device_at // slabs) ^ pol
    place = (seat_at // GROUP) * (pols // pol_step) + pol_order // pol_step
    place = place * LANES + lane_order * (pol_step * GROUP) + pol_order % pol_step * GROUP + seat_at % GROUP
    place = jnp.where(order >= 0, place, -1)
    chunk_count = capacity // GROUP * (pols // pol_step)
    spots = jnp.arange(chunk_count * LANES, dtype=jnp.int32)
    chosen = spots[:, None] == place[None, :]
    rows = jnp.sum(jnp.where(chosen, offsets[0][None, :], 0), axis=1).reshape(chunk_count, LANES)
    cols = jnp.sum(jnp.where(chosen, offsets[1][None, :], 0), axis=1).reshape(chunk_count, LANES)
    many = total > devices * GROUP
    slots, rows, cols, many = lax.optimization_barrier((slots, rows, cols, many))
    weight_row = pixel_weight.reshape(1, SUB * SUB)
    *pieces, extra = subgrids_of(held, where_at, offsets.astype(jnp.int32), slots, weight_row, capacity)
    norm_scale = 1.0 / (SUB * SUB * math.sqrt(VIS * SLOTS * slabs / 8.0))
    x_base = (slab * x_count).reshape(1)
    x_block = min(x_count, 256)

    def mixed(after):
        base, _ = lax.optimization_barrier((x_base, after))
        return mix_table(base, x_count, x_block, norm_scale)

    first, mix = gathered(pieces, mixed)

    def image(groups, more):
        groups = jnp.full((1,), groups, jnp.int32)
        return image_of(groups, x_base, first, more, rows, cols, mix, x_count, x_block, pol_step)

    def image_of_all():
        more = jnp.stack(gathered([extra[k] for k in range(pols)])[0])
        return image(capacity // GROUP, [more])

    sky = lax.cond(many, image_of_all, lambda: image(1, []))
    return sky[:, None]


def fits_image_domain(mesh):
    pols, slabs = mesh.shape["pol"], mesh.shape["slab"]
    devices = pols * slabs
    whole = slabs & (slabs - 1) == 0 and slabs * GROUP <= LANES and SLOTS * slabs == 2 * GROUP * devices
    return whole and pols == 4 and SLOTS == WAVES * devices and pols % (LANES // (GROUP * slabs)) == 0


def solution(mesh):
    in_specs = (P(None, "pol", "slab", None), P(None, "slab", None), P("slab"), P(), P(), P())
    out_specs = P(None, "pol", "slab", None)
    body = in_image_domain if fits_image_domain(mesh) else on_device
    return jax.shard_map(body, mesh=mesh, in_specs=in_specs, out_specs=out_specs, check_vma=False)
```
